128 devices in a mesh: lat: 8 (over x, core), lon: 16 (over z, y).
Axes of the slice: x: 4, y: 4, z: 4, core: 2. Of those that a mesh axis runs over, the one named last changes fastest.
Arguments:
- prognostic_samples: float32 [40, 25, 64, 2048], P(None, None, 'lat', 'lon'), may hold values from -6 to 6
- wind: float32 [2, 64, 2048], P(None, 'lat', 'lon'), may hold values from -0.4 to 0.4
- obs_lat: int32 [2, 512], replicated, may hold values from 0 to 63
- obs_lon: int32 [2, 512], replicated, may hold values from 0 to 2047
- obs_var: int32 [2, 512], replicated, may hold values from 0 to 24
- obs_value: float32 [2, 512], replicated, may hold values from -6 to 6
- obs_error: float32 [2, 512], replicated, may hold values from 0.5 to 4
Outputs:
- analysis: float32 [40, 25, 64, 2048], P(None, None, 'lat', 'lon')
The draws below stay inside these ranges and needn't reach their ends.
All inputs are finite; a program needn't handle non-finite values.
Results may differ from the reference program's by a relative error of at most 0.0001.
Values sent between devices are 32-bit elements; how exact they have to be, the bound alone decides.
A program may use at most 128 MiB of HBM per device.

```python
import math
import jax
import jax.numpy as jnp
from jax import lax

MEMBERS = 40
VARS = 25
NLAT = 64
NLON = 2048
LOC = 32
STEPS = 2
MEASURED_GROUPS = 2
OBS = 512
BLOCK = 128


def touch_ends(array, stream_key, low, top_value):
    shape = array.shape
    place = [jax.random.randint(jax.random.fold_in(stream_key, axis), (), 0, shape[axis]) for axis in range(len(shape))]
    array = array.at[tuple(place)].set(low)
    longest = shape.index(max(shape))
    place[longest] = (place[longest] + 1) % shape[longest]
    return array.at[tuple(place)].set(top_value)


def level_of(key, shape, cuts, low, high):
    factor_of = 1.0
    for axis_at, shards_of in cuts:
        steps = jax.random.uniform(jax.random.fold_in(jax.random.fold_in(key, 6), axis_at), (shards_of,), jnp.float32, low / len(cuts), high / len(cuts))
        factor_of = factor_of * jnp.repeat(jnp.exp(steps), shape[axis_at] // shards_of).reshape((-1,) + (1,) * (len(shape) - 1 - axis_at))
    return factor_of


def noise(rng, extent, spread, most, pieces=(), held_as=jnp.bfloat16):
    entries = spread * jax.random.normal(rng, extent, jnp.float32)
    if pieces:
        entries = entries * level_of(rng, extent, pieces, -0.22, 0.18)
    return jnp.clip(entries, -most, most).astype(held_as)


def setup_inputs(seed: int = 0) -> dict:
    key_list = jax.random.split(jax.random.key(seed), 8)
    prognostic_samples = noise(key_list[0], (MEMBERS, VARS, NLAT, NLON), 1.0, 6.0, ((2, 8), (3, 16)), jnp.float32)
    wind = jnp.clip(jax.random.uniform(key_list[1], (2, NLAT, NLON), jnp.float32, -0.4, 0.4) * level_of(key_list[1], (2, NLAT, NLON), ((1, 8), (2, 16)), -0.4, 0.0), -0.4, 0.4)
    obs_lat = touch_ends(jax.random.randint(key_list[2], (MEASURED_GROUPS, OBS), 0, NLAT), jax.random.fold_in(key_list[2], 1), 0, NLAT - 1).astype(jnp.int32)
    obs_lon = touch_ends(jax.random.randint(key_list[3], (MEASURED_GROUPS, OBS), 0, NLON), jax.random.fold_in(key_list[3], 1), 0, NLON - 1).astype(jnp.int32)
    obs_var = touch_ends(jax.random.randint(key_list[4], (MEASURED_GROUPS, OBS), 0, VARS), jax.random.fold_in(key_list[4], 1), 0, VARS - 1).astype(jnp.int32)
    obs_value = noise(key_list[5], (MEASURED_GROUPS, OBS), 1.5, 6.0, (), jnp.float32)
    obs_error = jnp.clip(jnp.exp(jax.random.uniform(key_list[6], (MEASURED_GROUPS, OBS), jnp.float32, math.log(0.5), math.log(4.0))), 0.5, 4.0)
    return {"prognostic_samples": prognostic_samples, "wind": wind, "obs_lat": obs_lat, "obs_lon": obs_lon, "obs_var": obs_var, "obs_value": obs_value, "obs_error": obs_error}


HIGHEST = lax.Precision.HIGHEST
DIFFUSE = 0.1

def taper(scaled):
    inner_part = (((-0.25 * scaled + 0.5) * scaled + 0.625) * scaled - 5.0 / 3.0) * scaled * scaled + 1.0
    scaled_safe = jnp.maximum(scaled, 1.0)
    outer_part = ((((scaled / 12.0 - 0.5) * scaled + 0.625) * scaled + 5.0 / 3.0) * scaled - 5.0) * scaled + 4.0 - 2.0 / (3.0 * scaled_safe)
    return jnp.where(scaled <= 1.0, inner_part, jnp.where(scaled < 2.0, outer_part, 0.0))

def taper_to(lat_a, lon_a, lat_b, lon_b, cycle_length, reach):
    meridional_spacing = (lat_a - lat_b).astype(jnp.float32)
    lon_gap = jnp.abs(lon_a - lon_b)
    lon_gap = jnp.minimum(lon_gap, cycle_length - lon_gap).astype(jnp.float32)
    return taper(jnp.sqrt(meridional_spacing * meridional_spacing + lon_gap * lon_gap) / reach)

def advance(padded, east_wind, north_wind):
    centre = padded[..., 1:-1, 1:-1]
    above_v = padded[..., 2:, 1:-1]
    below_v = padded[..., :-2, 1:-1]
    right_v = padded[..., 1:-1, 2:]
    left_v = padded[..., 1:-1, :-2]
    return centre - 0.5 * east_wind * (right_v - left_v) - 0.5 * north_wind * (above_v - below_v) + DIFFUSE * (right_v + left_v + above_v + below_v - 4.0 * centre)

def gains(prior, values, errors):
    members = prior.shape[0]
    average = lax.optimization_barrier(jnp.mean(prior, axis=0))
    anomaly = prior - average
    ensemble_spread = lax.optimization_barrier(jnp.sum(anomaly * anomaly, axis=0)) / (members - 1)
    total = ensemble_spread + errors
    weights = anomaly / ((members - 1) * total)
    shifts = values - average - anomaly / (1.0 + jnp.sqrt(errors / total))
    return (weights, shifts)

def reference(prognostic_samples, wind, obs_lat, obs_lon, obs_var, obs_value, obs_error):

    def predicted_model_vector(realization_grids):
        for section in range(STEPS):
            padded = jnp.pad(realization_grids, ((0, 0), (1, 1), (0, 0)))
            padded = jnp.concatenate([padded[:, :, -1:], padded, padded[:, :, :1]], axis=2)
            realization_grids = advance(padded, wind[0], wind[1])
        return realization_grids
    sample_realizations = lax.map(predicted_model_vector, jnp.moveaxis(prognostic_samples, 1, 0))
    sample_realizations = sample_realizations.reshape(VARS, MEMBERS, NLAT * NLON)
    cell_ids = jnp.arange(NLAT * NLON, dtype=jnp.int32)
    cell_lat = (cell_ids // NLON)[:, None]
    cell_lon = (cell_ids % NLON)[:, None]
    for batch_no in range(MEASURED_GROUPS):
        for block_no in range(OBS // BLOCK):
            first_obs = block_no * BLOCK
            blk_lat = obs_lat[batch_no, first_obs:first_obs + BLOCK]
            block_longitude = obs_lon[batch_no, first_obs:first_obs + BLOCK]
            blk_var = obs_var[batch_no, first_obs:first_obs + BLOCK]
            position = blk_lat * NLON + block_longitude
            prior = sample_realizations[blk_var, :, position].T
            weights, shifts = gains(prior, obs_value[batch_no, first_obs:first_obs + BLOCK], obs_error[batch_no, first_obs:first_obs + BLOCK])
            damping_factors = taper_to(cell_lat, cell_lon, blk_lat[None, :], block_longitude[None, :], NLON, float(LOC))

            def update_one(members_now):
                projected = jnp.einsum('mc,mk->ck', members_now, weights, precision=HIGHEST)
                return members_now + jnp.einsum('ck,mk->mc', projected * damping_factors, shifts, precision=HIGHEST)
            sample_realizations = lax.map(update_one, sample_realizations)
    return jnp.moveaxis(sample_realizations.reshape(VARS, MEMBERS, NLAT, NLON), 0, 1)
```

```python
import jax
import jax.numpy as jnp
from jax import lax
from jax.experimental import pallas as pl
from jax.experimental.pallas import tpu as pltpu
from jax.sharding import PartitionSpec as P

MEMBERS, NVAR, ROWS, COLS = 40, 25, 8, 128
NLON = 2048
NB, BLOCK = 8, 128
LOC = 32.0
KC = 32
NCH = BLOCK // KC
VG = 5
F32, BF = jnp.float32, jnp.bfloat16
STEPS = 2
DIFFUSE = 0.1


def taper_sq(d2):
    z = jnp.sqrt(d2) * (1.0 / LOC)
    inner = (((-0.25 * z + 0.5) * z + 0.625) * z - 5.0 / 3.0) * z * z + 1.0
    outer = (
        ((((z * (1.0 / 12.0) - 0.5) * z + 0.625) * z + 5.0 / 3.0) * z - 5.0) * z
        + 4.0
        - (2.0 / 3.0) / jnp.maximum(z, 1.0)
    )
    return jnp.where(z <= 1.0, inner, jnp.where(z < 2.0, outer, 0.0))


def hi(x):
    return x.astype(BF).astype(F32)


def dot(a, b, dims=((1,), (0,))):
    return lax.dot_general(a, b, (dims, ((), ())), preferred_element_type=F32)


def analysis_kernel(
    orig_ref, x_ref, y_ref, lat_ref, lon_ref, val_ref, err_ref,
    out_ref,
    ys, a_all, s_all, a_pk, b_pk, t_pk, xv, rhs, q3, nch,
):
    lat0 = orig_ref[0]
    lon0 = orig_ref[1]
    lat = lat_ref[...].astype(F32)
    lon = lon_ref[...].astype(F32)
    lat_t = lat.T
    lon_t = lon.T
    lat0f = lat0.astype(F32)
    lon0f = lon0.astype(F32)
    dy = jnp.maximum(jnp.maximum(lat0f - lat, lat - (lat0f + (ROWS - 1))), 0.0)
    off = lon - lon0f
    off = jnp.where(off < 0, off + NLON, off)
    dx = jnp.maximum(jnp.minimum(off - (COLS - 1), NLON - off), 0.0)
    reach = dx * dx + dy * dy < 4.0 * LOC * LOC
    reach_b = reach.astype(F32)
    before = (
        lax.broadcasted_iota(jnp.int32, (BLOCK, BLOCK), 0)
        < lax.broadcasted_iota(jnp.int32, (BLOCK, BLOCK), 1)
    ).astype(F32)
    rank = dot(reach_b.astype(BF), before.astype(BF))
    rank = jnp.where(reach, rank, -1.0)
    for b in range(NB):
        n = jnp.sum(reach_b[b : b + 1, :])
        nch[b] = ((n + (KC - 1)) * (1.0 / KC)).astype(jnp.int32)

    for b in range(NB):
        ys[:, b * BLOCK : (b + 1) * BLOCK] = y_ref[b]
    zero8 = jnp.zeros((8, BLOCK), F32)
    for b in range(NB):
        prior = ys[:, b * BLOCK : (b + 1) * BLOCK]
        average = jnp.sum(prior, axis=0, keepdims=True) * (1.0 / MEMBERS)
        anomaly = prior - average
        spread = jnp.sum(anomaly * anomaly, axis=0, keepdims=True) / (MEMBERS - 1)
        errors = err_ref[b : b + 1, :]
        total = spread + errors
        weights = anomaly * (1.0 / ((MEMBERS - 1) * total))
        shifts = (val_ref[b : b + 1, :] - average) - anomaly * (
            1.0 / (1.0 + jnp.sqrt(errors / total))
        )
        wh = hi(weights)
        a = jnp.concatenate([wh, weights - wh, wh, zero8], axis=0).T.astype(BF)
        sh = shifts.astype(BF)
        sl = (shifts - sh.astype(F32)).astype(BF)
        s2 = jnp.concatenate([sh, sl], axis=1)
        a_all[b] = a
        s_all[b] = s2
        if b + 1 < NB:
            first = (b + 1) * BLOCK
            s3 = jnp.concatenate([sh, sl, sh], axis=1)
            latk = lat_t[:, b : b + 1]
            lonk = lon_t[:, b : b + 1]
            for j in range(b + 1, NB):
                yl = ys[:, j * BLOCK : (j + 1) * BLOCK]
                yh = hi(yl)
                y3 = jnp.concatenate([yh, yh, yl - yh, zero8], axis=0).astype(BF)
                p = dot(a, y3)
                dlat = latk - lat[j : j + 1, :]
                dlon = jnp.abs(lonk - lon[j : j + 1, :])
                dlon = jnp.minimum(dlon, NLON - dlon)
                q = p * taper_sq(dlat * dlat + dlon * dlon)
                qh = q.astype(BF)
                ql = (q - qh.astype(F32)).astype(BF)
                ys[:, j * BLOCK : (j + 1) * BLOCK] = yl + dot(
                    s3, jnp.concatenate([qh, qh, ql], axis=0)
                )

    row_id = lax.broadcasted_iota(jnp.int32, (KC, BLOCK), 0)
    col_f = lax.broadcasted_iota(jnp.int32, (KC, COLS), 1).astype(F32) + lon0f
    for b in range(NB):

        @pl.loop(0, nch[b])
        def _(c):
            slot = b * NCH + c
            pick = ((row_id + c * KC).astype(F32) == rank[b : b + 1, :]).astype(F32)
            pick_b = pick.astype(BF)
            a_pk[slot] = dot(pick_b, a_all[b]).astype(BF)
            zero = jnp.zeros_like(pick_b)
            pick3 = jnp.concatenate(
                [
                    jnp.concatenate([pick_b, zero], axis=1),
                    jnp.concatenate([zero, pick_b], axis=1),
                    jnp.concatenate([pick_b, zero], axis=1),
                ],
                axis=0,
            )
            b_pk[slot] = dot(s_all[b], pick3, ((1,), (1,))).astype(BF)
            latc = jnp.sum(pick * lat[b : b + 1, :], axis=1, keepdims=True)
            lonc = jnp.sum(pick * lon[b : b + 1, :], axis=1, keepdims=True)
            dlon = jnp.abs(lonc - col_f)
            dlon = jnp.minimum(dlon, NLON - dlon)
            dlon = dlon * dlon
            for r in range(ROWS):
                dlat = latc - (lat0f + float(r))
                t_pk[slot, :, r * COLS : (r + 1) * COLS] = taper_sq(dlon + dlat * dlat)

    zero256 = jnp.zeros((8, 256), F32)

    @pl.loop(0, NVAR // VG)
    def _(g):
        for i in range(VG):
            for r in range(ROWS):
                xv[i, :, r * COLS : (r + 1) * COLS] = x_ref[
                    pl.ds((g * VG + i) * ROWS + r, MEMBERS, stride=NVAR * ROWS), :
                ]

        @pl.loop(0, NB)
        def _(b):
            for i in range(VG):
                for h in range(4):
                    x = xv[i, :, h * 256 : (h + 1) * 256]
                    xh = hi(x)
                    rhs[i, :, h * 256 : (h + 1) * 256] = jnp.concatenate(
                        [xh, xh, x - xh, zero256], axis=0
                    ).astype(BF)

            @pl.loop(0, nch[b])
            def _(c):
                slot = b * NCH + c
                a = a_pk[slot]
                s3 = b_pk[slot]
                for i in range(VG):
                    q = dot(a, rhs[i]) * t_pk[slot]
                    qh = q.astype(BF)
                    q3[i] = jnp.concatenate([qh, qh, (q - qh.astype(F32)).astype(BF)], axis=0)
                for i in range(VG):
                    xv[i] += dot(s3, q3[i])

        for i in range(VG):
            for r in range(ROWS):
                out_ref[
                    pl.ds((g * VG + i) * ROWS + r, MEMBERS, stride=NVAR * ROWS), :
                ] = xv[i, :, r * COLS : (r + 1) * COLS]


def analysis(origin, x, y, lat, lon, val, err):
    vm = pl.BlockSpec(memory_space=pltpu.VMEM)
    return pl.pallas_call(
        analysis_kernel,
        out_shape=jax.ShapeDtypeStruct((MEMBERS * NVAR * ROWS, COLS), F32),
        in_specs=[pl.BlockSpec(memory_space=pltpu.SMEM)] + [vm] * 6,
        out_specs=vm,
        scratch_shapes=[
            pltpu.VMEM((MEMBERS, NB * BLOCK), F32),
            pltpu.VMEM((NB, BLOCK, 128), BF),
            pltpu.VMEM((NB, MEMBERS, 256), BF),
            pltpu.VMEM((NB * NCH, KC, 128), BF),
            pltpu.VMEM((NB * NCH, MEMBERS, 3 * KC), BF),
            pltpu.VMEM((NB * NCH, KC, ROWS * COLS), F32),
            pltpu.VMEM((VG, MEMBERS, ROWS * COLS), F32),
            pltpu.VMEM((VG, 128, ROWS * COLS), BF),
            pltpu.VMEM((VG, 3 * KC, ROWS * COLS), BF),
            pltpu.SMEM((NB,), jnp.int32),
        ],
        compiler_params=pltpu.CompilerParams(vmem_limit_bytes=40 << 20),
        name="analysis",
    )(origin, x, y, lat, lon, val, err)


def with_halo(block, sides, width):
    for axis, dim in sides:
        count = lax.axis_size(axis)
        forward = [(i, i + 1) for i in range(count - 1)]
        forward.append((count - 1, 0))
        backward = [(target, source) for source, target in forward]
        low = lax.ppermute(
            lax.slice_in_dim(block, block.shape[dim] - width, None, axis=dim), axis, forward
        )
        high = lax.ppermute(lax.slice_in_dim(block, 0, width, axis=dim), axis, backward)
        block = jnp.concatenate([low, block, high], axis=dim)
    return block


def advance(padded, east_wind, north_wind):
    centre = padded[..., 1:-1, 1:-1]
    above_v = padded[..., 2:, 1:-1]
    below_v = padded[..., :-2, 1:-1]
    right_v = padded[..., 1:-1, 2:]
    left_v = padded[..., 1:-1, :-2]
    return (
        centre
        - 0.5 * east_wind * (right_v - left_v)
        - 0.5 * north_wind * (above_v - below_v)
        + DIFFUSE * (right_v + left_v + above_v + below_v - 4.0 * centre)
    )


def zero_outside_block(padded, margin):
    overall_line_count = padded.shape[-2]
    band_rows = overall_line_count - 2 * margin
    global_row = (
        lax.axis_index("lat") * band_rows - margin + lax.iota(jnp.int32, overall_line_count)
    )
    inside = (global_row >= 0) & (global_row < band_rows * lax.axis_size("lat"))
    return jnp.where(inside[:, None], padded, 0.0)


def read_priors(sample_realizations, sel_lat, sel_lon, sel_var, band_rows, band_cols):
    members, variables, cells = sample_realizations.shape
    local_lat = sel_lat - lax.axis_index("lat") * band_rows
    local_lon = sel_lon - lax.axis_index("lon") * band_cols
    owned = (local_lat >= 0) & (local_lat < band_rows) & (local_lon >= 0) & (local_lon < band_cols)
    position = (
        sel_var * cells
        + jnp.clip(local_lat, 0, band_rows - 1) * band_cols
        + jnp.clip(local_lon, 0, band_cols - 1)
    )
    picked = jnp.take(sample_realizations.reshape(members, variables * cells), position, axis=1)
    return jnp.where(owned[None, :], picked, 0.0)


def body(prognostic_samples, wind, obs_lat, obs_lon, obs_var, obs_value, obs_error):
    members, variables, band_rows, band_cols = prognostic_samples.shape
    state_now = prognostic_samples
    for section in range(STEPS):
        padded = with_halo(state_now, (("lat", 2), ("lon", 3)), 1)
        state_now = advance(zero_outside_block(padded, 1), wind[0], wind[1])
    sample_realizations = state_now.reshape(members, variables, band_rows * band_cols)
    own_part = read_priors(
        sample_realizations,
        obs_lat.reshape(-1),
        obs_lon.reshape(-1),
        obs_var.reshape(-1),
        band_rows,
        band_cols,
    )
    prior = lax.psum(own_part, ("lat", "lon"))
    y = jnp.moveaxis(prior.reshape(members, NB, BLOCK), 1, 0)
    origin = jnp.stack([lax.axis_index("lat") * band_rows, lax.axis_index("lon") * band_cols])
    out = analysis(
        origin.astype(jnp.int32),
        state_now.reshape(members * variables * band_rows, band_cols),
        y,
        obs_lat.reshape(NB, BLOCK),
        obs_lon.reshape(NB, BLOCK),
        obs_value.reshape(NB, BLOCK),
        obs_error.reshape(NB, BLOCK),
    )
    return out.reshape(members, variables, band_rows, band_cols)


def solution(mesh):
    in_specs = (P(None, None, "lat", "lon"), P(None, "lat", "lon"), P(), P(), P(), P(), P())
    out_specs = P(None, None, "lat", "lon")
    return jax.shard_map(body, mesh=mesh, in_specs=in_specs, out_specs=out_specs, check_vma=False)
```

```python
import jax
import jax.numpy as jnp
from jax import lax
from jax.experimental import pallas as pl
from jax.experimental.pallas import tpu as pltpu
from jax.sharding import PartitionSpec as P

MEMBERS, NVAR, ROWS, COLS = 40, 25, 8, 128
NLON = 2048
NB, BLOCK = 8, 128
LOC = 32.0
KC = 32
NCH = BLOCK // KC
VG = 5
F32, BF = jnp.float32, jnp.bfloat16
VS = 5
MG = MEMBERS // 8
MESH = pl.DeviceIdType.MESH
DIFFUSE = 0.1


def front_kernel(
    nlat, nlon,
    x_ref, wind_ref, lat_ref, lon_ref, var_ref,
    xf, out,
    xt, from_lo, from_hi, edge, edge_w, edge_e, corner, wind_n, halo, halo1, coef,
    part, line, block_sum, got_a, got_b,
    s_row, r_row, s_edge, r_edge, s_corner, r_corner, s_wind, r_wind,
    send, recv_a, recv_b, recv_c,
):
    me_lat = lax.axis_index("lat")
    me_lon = lax.axis_index("lon")

    def lat_peer(o):
        return lax.rem(me_lat + (o + nlat), nlat)

    def lon_peer(o):
        return lax.rem(me_lon + (o + nlon), nlon)

    def remote(src, dst, ssem, rsem, dlat, dlon):
        return pltpu.make_async_remote_copy(
            src_ref=src,
            dst_ref=dst,
            send_sem=ssem,
            recv_sem=rsem,
            device_id=(lat_peer(dlat) if dlat else me_lat, lon_peer(dlon) if dlon else me_lon),
            device_id_type=MESH,
        )

    barrier = pltpu.get_barrier_semaphore()
    greet = [(o, 0) for o in range(1, nlat)] + [(0, o) for o in range(1, nlon)]
    greet += [(-1, -1), (-1, 1), (1, -1), (1, 1)]
    for dlat, dlon in greet:
        pl.semaphore_signal(
            barrier,
            inc=1,
            device_id=(lat_peer(dlat) if dlat else me_lat, lon_peer(dlon) if dlon else me_lon),
            device_id_type=MESH,
        )

    lane = lax.broadcasted_iota(jnp.int32, (8, COLS), 1)
    lane4 = lax.rem(lane, 4)
    edge[...] = jnp.zeros_like(edge)

    def pack(vg):
        @pl.loop(0, VS)
        def _(vi):
            v = vg * VS + vi
            for r in range(ROWS):
                e = edge[r, vg]
                for mg in range(MG):
                    t = x_ref[pl.ds(mg * (8 * NVAR * ROWS) + v * ROWS + r, 8, stride=NVAR * ROWS), :]
                    xt[v, r, mg * 8 : (mg + 1) * 8, :] = t
                    g4 = 4 * (vi * MG + mg)
                    e = jnp.where(((lane - g4 + 2) & (COLS - 1)) < 4, pltpu.roll(t, g4, 1), e)
                edge[r, vg] = e

    def rows(vg, up):
        vs = pl.ds(vg * VS, VS)
        if up:
            return remote(xt.at[vs, 0:2], from_hi.at[vs], s_row.at[vg, 0], r_row.at[vg, 0], -1, 0)
        return remote(
            xt.at[vs, ROWS - 2 : ROWS], from_lo.at[vs], s_row.at[vg, 1], r_row.at[vg, 1], 1, 0
        )

    winds = [
        remote(wind_ref, wind_n.at[i], s_wind.at[i], r_wind.at[i], dlat, dlon)
        for i, (dlat, dlon) in enumerate([(1, 0), (-1, 0), (0, 1), (0, -1)])
    ]
    edges = [
        remote(edge, edge_w, s_edge.at[0], r_edge.at[0], 0, 1),
        remote(edge, edge_e, s_edge.at[1], r_edge.at[1], 0, -1),
    ]
    corners = [
        remote(edge.at[ROWS - 1], corner.at[0], s_corner.at[0], r_corner.at[0], 1, 1),
        remote(edge.at[ROWS - 1], corner.at[1], s_corner.at[1], r_corner.at[1], 1, -1),
        remote(edge.at[0], corner.at[2], s_corner.at[2], r_corner.at[2], -1, 1),
        remote(edge.at[0], corner.at[3], s_corner.at[3], r_corner.at[3], -1, -1),
    ]

    pack(0)
    pl.semaphore_wait(barrier, len(greet))
    for w in winds:
        w.start()
    rows(0, True).start()
    rows(0, False).start()
    for vg in range(1, NVAR // VS):
        pack(vg)
        rows(vg, True).start()
        rows(vg, False).start()
    for e in edges + corners:
        e.start()

    for w in winds:
        w.wait_recv()
    has_lo = (me_lat > 0).astype(F32)
    has_hi = (me_lat < nlat - 1).astype(F32)

    def row_wind(r):
        if r < 0:
            return wind_n[0, 0, ROWS - 1 : ROWS, :], wind_n[0, 1, ROWS - 1 : ROWS, :]
        if r == ROWS:
            return wind_n[1, 0, 0:1, :], wind_n[1, 1, 0:1, :]
        return wind_ref[0, r : r + 1, :], wind_ref[1, r : r + 1, :]

    def four(u, v, r):
        nxt, prv = DIFFUSE - 0.5 * v, DIFFUSE + 0.5 * v
        if r == 0:
            prv = prv * has_lo
        if r == ROWS - 1:
            nxt = nxt * has_hi
        return DIFFUSE - 0.5 * u, DIFFUSE + 0.5 * u, nxt, prv

    for r in range(-1, ROWS + 1):
        u, v = row_wind(r)
        for i, c in enumerate(four(u, v, r)):
            coef[r + 1, i] = jnp.broadcast_to(c, (8, COLS))

    for e in edges + corners:
        e.wait_recv()
    nvg = NVAR // VS
    for vg in range(nvg):
        halo[0, vg] = jnp.where(lane4 >= 2, corner[0, vg], corner[1, vg])
        halo[ROWS + 1, vg] = jnp.where(lane4 >= 2, corner[2, vg], corner[3, vg])
        for r in range(ROWS):
            halo[r + 1, vg] = jnp.where(lane4 >= 2, edge_w[r, vg], edge_e[r, vg])
    for r in range(ROWS):
        u, v = [
            jnp.where(
                lane4 >= 2,
                jnp.broadcast_to(wind_n[2, i, r : r + 1, COLS - 1 : COLS], (8, COLS)),
                jnp.broadcast_to(wind_n[3, i, r : r + 1, 0:1], (8, COLS)),
            )
            for i in range(2)
        ]
        ce, cw, cn, cs = four(u, v, r)
        for vg in range(nvg):
            own, got = edge[r, vg], halo[r + 1, vg]
            east = pltpu.roll(jnp.where(lane4 == 0, own, got), COLS - 1, 1)
            west = pltpu.roll(jnp.where(lane4 == 3, own, got), 1, 1)
            halo1[r, vg] = (
                (1.0 - 4.0 * DIFFUSE) * got
                + ce * east
                + cw * west
                + cn * halo[r + 2, vg]
                + cs * halo[r, vg]
            )

    def step(q, nxt, prv, side, r):
        east = pltpu.roll(jnp.where(lane == 0, side, q), COLS - 1, 1)
        west = pltpu.roll(jnp.where(lane == COLS - 1, side, q), 1, 1)
        return (
            (1.0 - 4.0 * DIFFUSE) * q
            + coef[r + 1, 0] * east
            + coef[r + 1, 1] * west
            + coef[r + 1, 2] * nxt
            + coef[r + 1, 3] * prv
        )

    @pl.loop(0, nvg)
    def _(vg):
        rows(vg, True).wait_recv()
        rows(vg, False).wait_recv()

        @pl.loop(0, VS)
        def _(vi):
            v = vg * VS + vi
            for mg in range(MG):
                ms = slice(mg * 8, (mg + 1) * 8)
                back = lax.rem(COLS - 4 * (vi * MG + mg), COLS)
                q = [from_lo[v, 0, ms, :], from_lo[v, 1, ms, :]]
                q += [xt[v, r, ms, :] for r in range(ROWS)]
                q += [from_hi[v, 0, ms, :], from_hi[v, 1, ms, :]]
                q1 = [
                    step(q[i], q[i + 1], q[i - 1], pltpu.roll(halo[i - 1, vg], back, 1), i - 2)
                    for i in range(1, ROWS + 3)
                ]
                for r in range(ROWS):
                    xf[v, r, ms, :] = step(
                        q1[r + 1], q1[r + 2], q1[r], pltpu.roll(halo1[r, vg], back, 1), r
                    )

    lane_m = lax.broadcasted_iota(jnp.int32, (MEMBERS, COLS), 1)
    lat0 = me_lat * ROWS
    lon0 = me_lon * COLS
    for b in range(NB):

        def pick(k, acc):
            row = lat_ref[b * BLOCK + k] - lat0
            col = lon_ref[b * BLOCK + k] - lon0
            owned = (row >= 0) & (row < ROWS) & (col >= 0) & (col < COLS)
            row = jnp.clip(row, 0, ROWS - 1)
            t = xf[var_ref[b * BLOCK + k], row]
            return jnp.where(
                lane_m == jnp.where(owned, k, -1), pltpu.roll(t, (k - col) & (COLS - 1), 1), acc
            )

        part[b] = lax.fori_loop(
            0, BLOCK, pick, jnp.zeros((MEMBERS, COLS), F32), unroll=8
        )

    first = [
        remote(part.at[lat_peer(o)], got_a.at[o - 1], send.at[o - 1], recv_a.at[o - 1], o, 0)
        for o in range(1, nlat)
    ]
    for c in first:
        c.start()
    total = part[me_lat]
    for i, c in enumerate(first):
        c.wait_recv()
        total = total + got_a[i]
    line[...] = total
    second = [
        remote(line, got_b.at[o - 1], send.at[nlat + o - 2], recv_b.at[o - 1], 0, o)
        for o in range(1, nlon)
    ]
    for c in second:
        c.start()
    for i, c in enumerate(second):
        c.wait_recv()
        total = total + got_b[i]
    block_sum[...] = total
    third = [
        remote(block_sum, out.at[me_lat], send.at[nlat + nlon + o - 3], recv_c.at[o - 1], o, 0)
        for o in range(1, nlat)
    ]
    for c in third:
        c.start()
    out[me_lat] = total
    for c in third:
        c.wait_recv()
    for c in winds + edges + corners + first + second + third:
        c.wait_send()

    @pl.loop(0, nvg)
    def _(vg):
        rows(vg, True).wait_send()
        rows(vg, False).wait_send()


def front(x, wind, lat, lon, var, nlat, nlon):
    vm = pl.BlockSpec(memory_space=pltpu.VMEM)
    sm = pl.BlockSpec(memory_space=pltpu.SMEM)
    nvg = NVAR // VS
    dma = pltpu.SemaphoreType.DMA
    return pl.pallas_call(
        lambda *refs: front_kernel(nlat, nlon, *refs),
        out_shape=(
            jax.ShapeDtypeStruct((NVAR, ROWS, MEMBERS, COLS), F32),
            jax.ShapeDtypeStruct((NB, MEMBERS, BLOCK), F32),
        ),
        in_specs=[vm, vm, sm, sm, sm],
        out_specs=(vm, vm),
        scratch_shapes=[
            pltpu.VMEM((NVAR, ROWS, MEMBERS, COLS), F32),
            pltpu.VMEM((NVAR, 2, MEMBERS, COLS), F32),
            pltpu.VMEM((NVAR, 2, MEMBERS, COLS), F32),
            pltpu.VMEM((ROWS, nvg, 8, COLS), F32),
            pltpu.VMEM((ROWS, nvg, 8, COLS), F32),
            pltpu.VMEM((ROWS, nvg, 8, COLS), F32),
            pltpu.VMEM((4, nvg, 8, COLS), F32),
            pltpu.VMEM((4, 2, ROWS, COLS), F32),
            pltpu.VMEM((ROWS + 2, nvg, 8, COLS), F32),
            pltpu.VMEM((ROWS, nvg, 8, COLS), F32),
            pltpu.VMEM((ROWS + 2, 4, 8, COLS), F32),
            pltpu.VMEM((NB, MEMBERS, BLOCK), F32),
            pltpu.VMEM((MEMBERS, BLOCK), F32),
            pltpu.VMEM((MEMBERS, BLOCK), F32),
            pltpu.VMEM((nlat - 1, MEMBERS, BLOCK), F32),
            pltpu.VMEM((nlon - 1, MEMBERS, BLOCK), F32),
            dma((nvg, 2)), dma((nvg, 2)), dma((2,)), dma((2,)), dma((4,)), dma((4,)),
            dma((4,)), dma((4,)),
            dma((2 * nlat + nlon - 3,)), dma((nlat - 1,)), dma((nlon - 1,)), dma((nlat - 1,)),
        ],
        compiler_params=pltpu.CompilerParams(
            collective_id=0, has_side_effects=True, vmem_limit_bytes=40 << 20
        ),
        name="front",
    )(x, wind, lat, lon, var)


def taper_sq(d2):
    z = jnp.sqrt(d2) * (1.0 / LOC)
    inner = (((-0.25 * z + 0.5) * z + 0.625) * z - 5.0 / 3.0) * z * z + 1.0
    outer = (
        ((((z * (1.0 / 12.0) - 0.5) * z + 0.625) * z + 5.0 / 3.0) * z - 5.0) * z
        + 4.0
        - (2.0 / 3.0) / jnp.maximum(z, 1.0)
    )
    return jnp.where(z <= 1.0, inner, jnp.where(z < 2.0, outer, 0.0))


def hi(x):
    return x.astype(BF).astype(F32)


def dot(a, b, dims=((1,), (0,))):
    return lax.dot_general(a, b, (dims, ((), ())), preferred_element_type=F32)


def analysis_kernel(
    orig_ref, x_ref, y_ref, lat_ref, lon_ref, val_ref, err_ref,
    out_ref,
    ys, a_all, s_all, a_pk, b_pk, t_pk, xv, rhs, q3, nch,
):
    lat0 = orig_ref[0]
    lon0 = orig_ref[1]
    lat = lat_ref[...].astype(F32)
    lon = lon_ref[...].astype(F32)
    lat_t = lat.T
    lon_t = lon.T
    lat0f = lat0.astype(F32)
    lon0f = lon0.astype(F32)
    dy = jnp.maximum(jnp.maximum(lat0f - lat, lat - (lat0f + (ROWS - 1))), 0.0)
    off = lon - lon0f
    off = jnp.where(off < 0, off + NLON, off)
    dx = jnp.maximum(jnp.minimum(off - (COLS - 1), NLON - off), 0.0)
    reach = dx * dx + dy * dy < 4.0 * LOC * LOC
    reach_b = reach.astype(F32)
    before = (
        lax.broadcasted_iota(jnp.int32, (BLOCK, BLOCK), 0)
        < lax.broadcasted_iota(jnp.int32, (BLOCK, BLOCK), 1)
    ).astype(F32)
    rank = dot(reach_b.astype(BF), before.astype(BF))
    rank = jnp.where(reach, rank, -1.0)
    for b in range(NB):
        n = jnp.sum(reach_b[b : b + 1, :])
        nch[b] = ((n + (KC - 1)) * (1.0 / KC)).astype(jnp.int32)

    for b in range(NB):
        ys[:, b * BLOCK : (b + 1) * BLOCK] = y_ref[b]
    zero8 = jnp.zeros((8, BLOCK), F32)
    for b in range(NB):
        prior = ys[:, b * BLOCK : (b + 1) * BLOCK]
        average = jnp.sum(prior, axis=0, keepdims=True) * (1.0 / MEMBERS)
        anomaly = prior - average
        spread = jnp.sum(anomaly * anomaly, axis=0, keepdims=True) / (MEMBERS - 1)
        errors = err_ref[b : b + 1, :]
        total = spread + errors
        weights = anomaly * (1.0 / ((MEMBERS - 1) * total))
        shifts = (val_ref[b : b + 1, :] - average) - anomaly * (
            1.0 / (1.0 + jnp.sqrt(errors / total))
        )
        wh = hi(weights)
        a = jnp.concatenate([wh, weights - wh, wh, zero8], axis=0).T.astype(BF)
        sh = shifts.astype(BF)
        sl = (shifts - sh.astype(F32)).astype(BF)
        s2 = jnp.concatenate([sh, sl], axis=1)
        a_all[b] = a
        s_all[b] = s2
        if b + 1 < NB:
            first = (b + 1) * BLOCK
            s3 = jnp.concatenate([sh, sl, sh], axis=1)
            latk = lat_t[:, b : b + 1]
            lonk = lon_t[:, b : b + 1]
            for j in range(b + 1, NB):
                yl = ys[:, j * BLOCK : (j + 1) * BLOCK]
                yh = hi(yl)
                y3 = jnp.concatenate([yh, yh, yl - yh, zero8], axis=0).astype(BF)
                p = dot(a, y3)
                dlat = latk - lat[j : j + 1, :]
                dlon = jnp.abs(lonk - lon[j : j + 1, :])
                dlon = jnp.minimum(dlon, NLON - dlon)
                q = p * taper_sq(dlat * dlat + dlon * dlon)
                qh = q.astype(BF)
                ql = (q - qh.astype(F32)).astype(BF)
                ys[:, j * BLOCK : (j + 1) * BLOCK] = yl + dot(
                    s3, jnp.concatenate([qh, qh, ql], axis=0)
                )

    row_id = lax.broadcasted_iota(jnp.int32, (KC, BLOCK), 0)
    col_f = lax.broadcasted_iota(jnp.int32, (KC, COLS), 1).astype(F32) + lon0f
    for b in range(NB):

        @pl.loop(0, nch[b])
        def _(c):
            slot = b * NCH + c
            pick = ((row_id + c * KC).astype(F32) == rank[b : b + 1, :]).astype(F32)
            pick_b = pick.astype(BF)
            a_pk[slot] = dot(pick_b, a_all[b]).astype(BF)
            zero = jnp.zeros_like(pick_b)
            pick3 = jnp.concatenate(
                [
                    jnp.concatenate([pick_b, zero], axis=1),
                    jnp.concatenate([zero, pick_b], axis=1),
                    jnp.concatenate([pick_b, zero], axis=1),
                ],
                axis=0,
            )
            b_pk[slot] = dot(s_all[b], pick3, ((1,), (1,))).astype(BF)
            latc = jnp.sum(pick * lat[b : b + 1, :], axis=1, keepdims=True)
            lonc = jnp.sum(pick * lon[b : b + 1, :], axis=1, keepdims=True)
            dlon = jnp.abs(lonc - col_f)
            dlon = jnp.minimum(dlon, NLON - dlon)
            dlon = dlon * dlon
            for r in range(ROWS):
                dlat = latc - (lat0f + float(r))
                t_pk[slot, :, r * COLS : (r + 1) * COLS] = taper_sq(dlon + dlat * dlat)

    zero256 = jnp.zeros((8, 256), F32)

    @pl.loop(0, NVAR // VG)
    def _(g):
        for i in range(VG):
            for r in range(ROWS):
                xv[i, :, r * COLS : (r + 1) * COLS] = x_ref[g * VG + i, r]

        @pl.loop(0, NB)
        def _(b):
            for i in range(VG):
                for h in range(4):
                    x = xv[i, :, h * 256 : (h + 1) * 256]
                    xh = hi(x)
                    rhs[i, :, h * 256 : (h + 1) * 256] = jnp.concatenate(
                        [xh, xh, x - xh, zero256], axis=0
                    ).astype(BF)

            @pl.loop(0, nch[b])
            def _(c):
                slot = b * NCH + c
                a = a_pk[slot]
                s3 = b_pk[slot]
                for i in range(VG):
                    q = dot(a, rhs[i]) * t_pk[slot]
                    qh = q.astype(BF)
                    q3[i] = jnp.concatenate([qh, qh, (q - qh.astype(F32)).astype(BF)], axis=0)
                for i in range(VG):
                    xv[i] += dot(s3, q3[i])

        for i in range(VG):
            for r in range(ROWS):
                out_ref[
                    pl.ds((g * VG + i) * ROWS + r, MEMBERS, stride=NVAR * ROWS), :
                ] = xv[i, :, r * COLS : (r + 1) * COLS]


def analysis(origin, x, y, lat, lon, val, err):
    vm = pl.BlockSpec(memory_space=pltpu.VMEM)
    return pl.pallas_call(
        analysis_kernel,
        out_shape=jax.ShapeDtypeStruct((MEMBERS * NVAR * ROWS, COLS), F32),
        in_specs=[pl.BlockSpec(memory_space=pltpu.SMEM)] + [vm] * 6,
        out_specs=vm,
        scratch_shapes=[
            pltpu.VMEM((MEMBERS, NB * BLOCK), F32),
            pltpu.VMEM((NB, BLOCK, 128), BF),
            pltpu.VMEM((NB, MEMBERS, 256), BF),
            pltpu.VMEM((NB * NCH, KC, 128), BF),
            pltpu.VMEM((NB * NCH, MEMBERS, 3 * KC), BF),
            pltpu.VMEM((NB * NCH, KC, ROWS * COLS), F32),
            pltpu.VMEM((VG, MEMBERS, ROWS * COLS), F32),
            pltpu.VMEM((VG, 128, ROWS * COLS), BF),
            pltpu.VMEM((VG, 3 * KC, ROWS * COLS), BF),
            pltpu.SMEM((NB,), jnp.int32),
        ],
        compiler_params=pltpu.CompilerParams(vmem_limit_bytes=40 << 20),
        name="analysis",
    )(origin, x, y, lat, lon, val, err)


def solution(mesh):
    nlat, nlon = mesh.shape["lat"], mesh.shape["lon"]

    def body(prognostic_samples, wind, obs_lat, obs_lon, obs_var, obs_value, obs_error):
        xf, y = front(
            prognostic_samples.reshape(MEMBERS * NVAR * ROWS, COLS),
            wind,
            obs_lat.reshape(-1),
            obs_lon.reshape(-1),
            obs_var.reshape(-1),
            nlat,
            nlon,
        )
        origin = jnp.stack([lax.axis_index("lat") * ROWS, lax.axis_index("lon") * COLS])
        out = analysis(
            origin.astype(jnp.int32),
            xf,
            y,
            obs_lat.reshape(NB, BLOCK),
            obs_lon.reshape(NB, BLOCK),
            obs_value.reshape(NB, BLOCK),
            obs_error.reshape(NB, BLOCK),
        )
        return out.reshape(prognostic_samples.shape)

    in_specs = (P(None, None, "lat", "lon"), P(None, "lat", "lon"), P(), P(), P(), P(), P())
    out_specs = P(None, None, "lat", "lon")
    return jax.shard_map(body, mesh=mesh, in_specs=in_specs, out_specs=out_specs, check_vma=False)
```

```python
import jax
import jax.numpy as jnp
from jax import lax
from jax.experimental import pallas as pl
from jax.experimental.pallas import tpu as pltpu
from jax.sharding import PartitionSpec as P

MEMBERS, NVAR, ROWS, COLS = 40, 25, 8, 128
NLON = 2048
GROUPS, OBS = 2, 512
NB, BLOCK = 8, 128
PER = OBS // BLOCK
LOC = 32.0
DIFFUSE = 0.1
VS = 5
NVG = NVAR // VS
MG = MEMBERS // 8
KC = 32
NCH = BLOCK // KC
VG = 5
F32, BF = jnp.float32, jnp.bfloat16
MESH = pl.DeviceIdType.MESH


def hi(x):
    return x.astype(BF).astype(F32)


def split(x):
    high = x.astype(BF)
    return high, (x - high.astype(F32)).astype(BF)


def dot(a, b, dims=((1,), (0,))):
    return lax.dot_general(a, b, (dims, ((), ())), preferred_element_type=F32)


def peers(nlat, nlon):
    me_lat = lax.axis_index("lat")
    me_lon = lax.axis_index("lon")

    def place(dlat, dlon):
        lat = lax.rem(me_lat + (dlat + nlat), nlat) if dlat else me_lat
        lon = lax.rem(me_lon + (dlon + nlon), nlon) if dlon else me_lon
        return lat, lon

    def remote(src, dst, ssem, rsem, dlat, dlon):
        return pltpu.make_async_remote_copy(
            src_ref=src,
            dst_ref=dst,
            send_sem=ssem,
            recv_sem=rsem,
            device_id=place(dlat, dlon),
            device_id_type=MESH,
        )

    def signal(barrier, offsets):
        for o in offsets:
            pl.semaphore_signal(barrier, inc=1, device_id=place(*o), device_id_type=MESH)

    return me_lat, me_lon, place, remote, signal


def forecast_kernel(
    nlat, nlon,
    x_ref, wind_ref, lat_ref, lon_ref, var_ref,
    xf, desc,
    xt, edge, edge_w, edge_e, corner, wind_n, halo, halo_s, halo1_s, coef, shift, q1_s,
    s_row, r_row, s_edge, r_edge, s_corner, r_corner, s_wind, r_wind,
):
    me_lat, me_lon, place, remote, signal = peers(nlat, nlon)
    barrier = pltpu.get_barrier_semaphore()
    near = [(a, b) for a in (-1, 0, 1) for b in (-1, 0, 1) if a or b]
    signal(barrier, near)

    def column(r, mg, v):
        return x_ref[pl.ds(mg * (8 * NVAR * ROWS) + v * ROWS + r, 8, stride=NVAR * ROWS), :]

    @pl.loop(0, NVAR)
    def _(v):
        for r in (0, 1, ROWS - 2, ROWS - 1):
            for mg in range(MG):
                xt[v, r + 2, mg * 8 : (mg + 1) * 8, :] = column(r, mg, v)

    def rows(vg, up):
        vs = pl.ds(vg * VS, VS)
        if up:
            return remote(
                xt.at[vs, 2:4],
                xt.at[vs, ROWS + 2 : ROWS + 4],
                s_row.at[vg, 0], r_row.at[vg, 0], -1, 0,
            )
        return remote(
            xt.at[vs, ROWS : ROWS + 2], xt.at[vs, 0:2], s_row.at[vg, 1], r_row.at[vg, 1], 1, 0
        )

    winds = [
        remote(wind_ref, wind_n.at[i], s_wind.at[i], r_wind.at[i], dlat, dlon)
        for i, (dlat, dlon) in enumerate([(1, 0), (-1, 0), (0, 1), (0, -1)])
    ]
    edges = [
        remote(edge, edge_w, s_edge.at[0], r_edge.at[0], 0, 1),
        remote(edge, edge_e, s_edge.at[1], r_edge.at[1], 0, -1),
    ]
    corners = [
        remote(edge.at[ROWS - 1], corner.at[0], s_corner.at[0], r_corner.at[0], 1, 1),
        remote(edge.at[ROWS - 1], corner.at[1], s_corner.at[1], r_corner.at[1], 1, -1),
        remote(edge.at[0], corner.at[2], s_corner.at[2], r_corner.at[2], -1, 1),
        remote(edge.at[0], corner.at[3], s_corner.at[3], r_corner.at[3], -1, -1),
    ]
    pl.semaphore_wait(barrier, len(near))
    for w in winds:
        w.start()
    for vg in range(NVG):
        rows(vg, True).start()
        rows(vg, False).start()

    lane = lax.broadcasted_iota(jnp.int32, (8, COLS), 1)
    edge[...] = jnp.zeros_like(edge)

    @pl.loop(0, NVAR)
    def _(v):
        mine = ((lane - 4 * v + 2) & (COLS - 1)) < 4
        for r in range(ROWS):
            for mg in range(MG):
                ms = slice(mg * 8, (mg + 1) * 8)
                if 2 <= r < ROWS - 2:
                    t = column(r, mg, v)
                    xt[v, r + 2, ms, :] = t
                else:
                    t = xt[v, r + 2, ms, :]
                edge[r, ms, :] = jnp.where(mine, pltpu.roll(t, 4 * v, 1), edge[r, ms, :])

    for e in edges + corners:
        e.start()

    row = lat_ref[...] - me_lat * ROWS
    col = lon_ref[...] - me_lon * COLS
    owned = (row >= 0) & (row < ROWS) & (col >= 0) & (col < COLS)
    desc[...] = jnp.where(owned, (var_ref[...] * ROWS + row) * COLS + col, -1)

    src = lax.rem(lax.broadcasted_iota(jnp.int32, (2 * COLS, 2 * COLS), 0), COLS)
    dst = lax.broadcasted_iota(jnp.int32, (2 * COLS, 2 * COLS), 1)
    east_of = (dst < COLS) & (src == dst + 1)
    west_of = (dst >= COLS) & (src == dst - COLS - 1)
    shift[...] = jnp.where(east_of | west_of, 1.0, 0.0).astype(BF)

    for w in winds:
        w.wait_recv()
    has_lo = (me_lat > 0).astype(F32)
    has_hi = (me_lat < nlat - 1).astype(F32)

    def row_wind(r):
        if r < 0:
            return wind_n[0, 0, ROWS - 1 : ROWS, :], wind_n[0, 1, ROWS - 1 : ROWS, :]
        if r == ROWS:
            return wind_n[1, 0, 0:1, :], wind_n[1, 1, 0:1, :]
        return wind_ref[0, r : r + 1, :], wind_ref[1, r : r + 1, :]

    def four(u, v, r):
        nxt, prv = DIFFUSE - 0.5 * v, DIFFUSE + 0.5 * v
        if r == 0:
            prv = prv * has_lo
        if r == ROWS - 1:
            nxt = nxt * has_hi
        return DIFFUSE - 0.5 * u, DIFFUSE + 0.5 * u, nxt, prv

    for r in range(-1, ROWS + 1):
        u, v = row_wind(r)
        for i, c in enumerate(four(u, v, r)):
            coef[i, r + 1] = jnp.broadcast_to(c, (8, COLS))

    for e in edges + corners:
        e.wait_recv()
    lane4 = lax.rem(lax.broadcasted_iota(jnp.int32, (MEMBERS, COLS), 1), 4)
    from_west = lane4 >= 2
    halo[0] = jnp.where(from_west, corner[0], corner[1])
    halo[ROWS + 1] = jnp.where(from_west, corner[2], corner[3])
    for r in range(ROWS):
        halo[r + 1] = jnp.where(from_west, edge_w[r], edge_e[r])
    for r in range(ROWS + 2):
        high, low = split(halo[r])
        halo_s[r] = jnp.concatenate([high, low], axis=1)
    for r in range(ROWS):
        u, v = [
            jnp.where(
                from_west,
                jnp.broadcast_to(wind_n[2, i, r : r + 1, COLS - 1 : COLS], (MEMBERS, COLS)),
                jnp.broadcast_to(wind_n[3, i, r : r + 1, 0:1], (MEMBERS, COLS)),
            )
            for i in range(2)
        ]
        ce, cw, cn, cs = four(u, v, r)
        own, got = edge[r], halo[r + 1]
        east = pltpu.roll(jnp.where(lane4 == 0, own, got), COLS - 1, 1)
        west = pltpu.roll(jnp.where(lane4 == 3, own, got), 1, 1)
        after = (
            (1.0 - 4.0 * DIFFUSE) * got
            + ce * east
            + cw * west
            + cn * halo[r + 2]
            + cs * halo[r]
        )
        high, low = split(after)
        halo1_s[r] = jnp.concatenate([high, low], axis=1)

    def step(q, nxt, prv, side, place_side, first, count):
        shape = (count, MG, 8, COLS)
        high, low = split(q)
        both = dot(jnp.concatenate([high, low], axis=1), shift[...]) + dot(
            side.reshape(count * MEMBERS, 2 * COLS), place_side
        )
        c = [coef[i, first : first + count].reshape(count, 1, 8, COLS) for i in range(4)]
        new = (
            (1.0 - 4.0 * DIFFUSE) * q.reshape(shape)
            + c[0] * both[:, :COLS].reshape(shape)
            + c[1] * both[:, COLS:].reshape(shape)
            + c[2] * nxt.reshape(shape)
            + c[3] * prv.reshape(shape)
        )
        return new.reshape(count * MEMBERS, COLS)

    def place_side(v):
        at_end = (dst == COLS - 1) & (src == 4 * v)
        at_start = (dst == COLS) & (src == ((4 * v - 1) & (COLS - 1)))
        return jnp.where(at_end | at_start, 1.0, 0.0).astype(BF)

    def block(ref, v, first, count):
        return ref[v, first : first + count].reshape(count * MEMBERS, COLS)

    @pl.loop(0, NVG)
    def _(vg):
        rows(vg, True).wait_recv()
        rows(vg, False).wait_recv()
        n1, n2 = ROWS + 2, ROWS
        for vi in range(VS):
            v = vg * VS + vi
            q1_s[vi] = step(
                block(xt, v, 1, n1), block(xt, v, 2, n1), block(xt, v, 0, n1),
                halo_s[...], place_side(v), 0, n1,
            ).reshape(n1, MEMBERS, COLS)
        for vi in range(VS):
            v = vg * VS + vi
            xf[v] = step(
                block(q1_s, vi, 1, n2), block(q1_s, vi, 2, n2), block(q1_s, vi, 0, n2),
                halo1_s[...], place_side(v), 1, n2,
            ).reshape(n2, MEMBERS, COLS)

    for c in winds + edges + corners:
        c.wait_send()

    @pl.loop(0, NVG)
    def _(vg):
        rows(vg, True).wait_send()
        rows(vg, False).wait_send()


def forecast(x, wind, lat, lon, var, nlat, nlon):
    vm = pl.BlockSpec(memory_space=pltpu.VMEM)
    dma = pltpu.SemaphoreType.DMA
    return pl.pallas_call(
        lambda *refs: forecast_kernel(nlat, nlon, *refs),
        out_shape=(
            jax.ShapeDtypeStruct((NVAR, ROWS, MEMBERS, COLS), F32),
            jax.ShapeDtypeStruct((GROUPS, OBS), jnp.int32),
        ),
        in_specs=[vm] * 5,
        out_specs=(vm, vm),
        scratch_shapes=[
            pltpu.VMEM((NVAR, ROWS + 4, MEMBERS, COLS), F32),
            pltpu.VMEM((ROWS, MEMBERS, COLS), F32),
            pltpu.VMEM((ROWS, MEMBERS, COLS), F32),
            pltpu.VMEM((ROWS, MEMBERS, COLS), F32),
            pltpu.VMEM((4, MEMBERS, COLS), F32),
            pltpu.VMEM((4, 2, ROWS, COLS), F32),
            pltpu.VMEM((ROWS + 2, MEMBERS, COLS), F32),
            pltpu.VMEM((ROWS + 2, MEMBERS, 2 * COLS), BF),
            pltpu.VMEM((ROWS, MEMBERS, 2 * COLS), BF),
            pltpu.VMEM((4, ROWS + 2, 8, COLS), F32),
            pltpu.VMEM((2 * COLS, 2 * COLS), BF),
            pltpu.VMEM((VS, ROWS + 2, MEMBERS, COLS), F32),
            dma((NVG, 2)), dma((NVG, 2)), dma((2,)), dma((2,)),
            dma((4,)), dma((4,)), dma((4,)), dma((4,)),
        ],
        compiler_params=pltpu.CompilerParams(
            collective_id=0, has_side_effects=True, vmem_limit_bytes=40 << 20
        ),
        name="forecast",
    )(x, wind, lat, lon, var)


def pick_kernel(desc, xf, part):
    part[...] = jnp.zeros_like(part)
    lane = lax.broadcasted_iota(jnp.int32, (MEMBERS, COLS), 1)
    width = 8

    @pl.loop(0, GROUPS * OBS // width)
    def _(g):
        batch, first = g // (OBS // width), lax.rem(g, OBS // width) * width
        d = [desc[batch, first + j] for j in range(width)]
        top = d[0]
        for j in range(1, width):
            top = jnp.maximum(top, d[j])

        @pl.when(top >= 0)
        def _():
            for j in range(width):

                @pl.when(d[j] >= 0)
                def _(j=j):
                    k = lax.rem(g, BLOCK // width) * width + j
                    b = g // (BLOCK // width)
                    col = d[j] & (COLS - 1)
                    t = xf[lax.shift_right_logical(d[j], 7)]
                    part[b] = jnp.where(
                        lane == k, pltpu.roll(t, (k - col) & (COLS - 1), 1), part[b]
                    )


def pick(desc, xf):
    vm = pl.BlockSpec(memory_space=pltpu.VMEM)
    return pl.pallas_call(
        pick_kernel,
        out_shape=jax.ShapeDtypeStruct((NB, MEMBERS, BLOCK), F32),
        in_specs=[pl.BlockSpec(memory_space=pltpu.SMEM), vm],
        out_specs=vm,
        compiler_params=pltpu.CompilerParams(vmem_limit_bytes=16 << 20),
        name="pick",
    )(desc, xf)


def total_kernel(nlat, nlon, part, out, part_b, line, got_a, got_b, send, recv_a, recv_b, recv_c):
    me_lat = lax.axis_index("lat")
    me_lon = lax.axis_index("lon")

    def lat_peer(o):
        return lax.rem(me_lat + o, nlat)

    def lon_peer(o):
        return lax.rem(me_lon + o, nlon)

    barrier = pltpu.get_barrier_semaphore()
    for o in range(1, nlat):
        pl.semaphore_signal(barrier, inc=1, device_id=(lat_peer(o), me_lon), device_id_type=MESH)
    for o in range(1, nlon):
        pl.semaphore_signal(barrier, inc=1, device_id=(me_lat, lon_peer(o)), device_id_type=MESH)
    pl.semaphore_wait(barrier, nlat + nlon - 2)

    first = []
    for o in range(1, nlat):
        copy = pltpu.make_async_remote_copy(
            src_ref=part.at[lat_peer(o)],
            dst_ref=got_a.at[o - 1],
            send_sem=send.at[o - 1],
            recv_sem=recv_a.at[o - 1],
            device_id=(lat_peer(o), me_lon),
            device_id_type=MESH,
        )
        copy.start()
        first.append(copy)
    total = part[me_lat]
    for copy, o in zip(first, range(1, nlat)):
        copy.wait_recv()
        total = total + got_a[o - 1]
    line[...] = total
    second = []
    for o in range(1, nlon):
        copy = pltpu.make_async_remote_copy(
            src_ref=line,
            dst_ref=got_b.at[o - 1],
            send_sem=send.at[nlat + o - 2],
            recv_sem=recv_b.at[o - 1],
            device_id=(me_lat, lon_peer(o)),
            device_id_type=MESH,
        )
        copy.start()
        second.append(copy)
    for copy, o in zip(second, range(1, nlon)):
        copy.wait_recv()
        total = total + got_b[o - 1]
    part_b[...] = total
    third = []
    for o in range(1, nlat):
        copy = pltpu.make_async_remote_copy(
            src_ref=part_b,
            dst_ref=out.at[me_lat],
            send_sem=send.at[nlat + nlon + o - 3],
            recv_sem=recv_c.at[o - 1],
            device_id=(lat_peer(o), me_lon),
            device_id_type=MESH,
        )
        copy.start()
        third.append(copy)
    out[me_lat] = total
    for copy in third:
        copy.wait_recv()
    for copy in first + second + third:
        copy.wait_send()


def total_over_devices(part, nlat, nlon):
    vm = pl.BlockSpec(memory_space=pltpu.VMEM)
    return pl.pallas_call(
        lambda *refs: total_kernel(nlat, nlon, *refs),
        out_shape=jax.ShapeDtypeStruct(part.shape, F32),
        in_specs=[vm],
        out_specs=vm,
        scratch_shapes=[
            pltpu.VMEM((MEMBERS, BLOCK), F32),
            pltpu.VMEM((MEMBERS, BLOCK), F32),
            pltpu.VMEM((nlat - 1, MEMBERS, BLOCK), F32),
            pltpu.VMEM((nlon - 1, MEMBERS, BLOCK), F32),
            pltpu.SemaphoreType.DMA((2 * nlat + nlon - 3,)),
            pltpu.SemaphoreType.DMA((nlat - 1,)),
            pltpu.SemaphoreType.DMA((nlon - 1,)),
            pltpu.SemaphoreType.DMA((nlat - 1,)),
        ],
        compiler_params=pltpu.CompilerParams(collective_id=1, has_side_effects=True),
        name="total_over_devices",
    )(part)


def taper_sq(d2):
    z = jnp.sqrt(d2) * (1.0 / LOC)
    inner = (((-0.25 * z + 0.5) * z + 0.625) * z - 5.0 / 3.0) * z * z + 1.0
    outer = (
        ((((z * (1.0 / 12.0) - 0.5) * z + 0.625) * z + 5.0 / 3.0) * z - 5.0) * z
        + 4.0
        - (2.0 / 3.0) / jnp.maximum(z, 1.0)
    )
    return jnp.where(z <= 1.0, inner, jnp.where(z < 2.0, outer, 0.0))


def analysis_kernel(
    x_ref, y_ref, lat_ref, lon_ref, val_ref, err_ref,
    out_ref,
    ys, a_all, s_all, a_pk, b_pk, t_pk, xv, rhs, q3, nch,
):
    lat0 = lax.axis_index("lat") * ROWS
    lon0 = lax.axis_index("lon") * COLS

    def by_block(ref):
        rows = [ref[b // PER : b // PER + 1, (b % PER) * BLOCK : (b % PER + 1) * BLOCK] for b in range(NB)]
        return jnp.concatenate(rows, axis=0)

    lat = by_block(lat_ref).astype(F32)
    lon = by_block(lon_ref).astype(F32)
    values = by_block(val_ref)
    variances = by_block(err_ref)
    lat_t = lat.T
    lon_t = lon.T
    lat0f = lat0.astype(F32)
    lon0f = lon0.astype(F32)
    dy = jnp.maximum(jnp.maximum(lat0f - lat, lat - (lat0f + (ROWS - 1))), 0.0)
    off = lon - lon0f
    off = jnp.where(off < 0, off + NLON, off)
    dx = jnp.maximum(jnp.minimum(off - (COLS - 1), NLON - off), 0.0)
    reach = dx * dx + dy * dy < 4.0 * LOC * LOC
    reach_b = reach.astype(F32)
    before = (
        lax.broadcasted_iota(jnp.int32, (BLOCK, BLOCK), 0)
        < lax.broadcasted_iota(jnp.int32, (BLOCK, BLOCK), 1)
    ).astype(F32)
    rank = dot(reach_b.astype(BF), before.astype(BF))
    rank = jnp.where(reach, rank, -1.0)
    for b in range(NB):
        n = jnp.sum(reach_b[b : b + 1, :])
        nch[b] = ((n + (KC - 1)) * (1.0 / KC)).astype(jnp.int32)

    for b in range(NB):
        ys[:, b * BLOCK : (b + 1) * BLOCK] = y_ref[b]
    zero8 = jnp.zeros((8, BLOCK), F32)
    for b in range(NB):
        prior = ys[:, b * BLOCK : (b + 1) * BLOCK]
        average = jnp.sum(prior, axis=0, keepdims=True) * (1.0 / MEMBERS)
        anomaly = prior - average
        spread = jnp.sum(anomaly * anomaly, axis=0, keepdims=True) / (MEMBERS - 1)
        errors = variances[b : b + 1, :]
        total = spread + errors
        weights = anomaly * (1.0 / ((MEMBERS - 1) * total))
        shifts = (values[b : b + 1, :] - average) - anomaly * (
            1.0 / (1.0 + jnp.sqrt(errors / total))
        )
        wh = hi(weights)
        a = jnp.concatenate([wh, weights - wh, wh, zero8], axis=0).T.astype(BF)
        sh = shifts.astype(BF)
        sl = (shifts - sh.astype(F32)).astype(BF)
        s2 = jnp.concatenate([sh, sl], axis=1)
        a_all[b] = a
        s_all[b] = s2
        if b + 1 < NB:
            first = (b + 1) * BLOCK
            s3 = jnp.concatenate([sh, sl, sh], axis=1)
            latk = lat_t[:, b : b + 1]
            lonk = lon_t[:, b : b + 1]
            for j in range(b + 1, NB):
                yl = ys[:, j * BLOCK : (j + 1) * BLOCK]
                yh = hi(yl)
                y3 = jnp.concatenate([yh, yh, yl - yh, zero8], axis=0).astype(BF)
                p = dot(a, y3)
                dlat = latk - lat[j : j + 1, :]
                dlon = jnp.abs(lonk - lon[j : j + 1, :])
                dlon = jnp.minimum(dlon, NLON - dlon)
                q = p * taper_sq(dlat * dlat + dlon * dlon)
                qh = q.astype(BF)
                ql = (q - qh.astype(F32)).astype(BF)
                ys[:, j * BLOCK : (j + 1) * BLOCK] = yl + dot(
                    s3, jnp.concatenate([qh, qh, ql], axis=0)
                )

    row_id = lax.broadcasted_iota(jnp.int32, (KC, BLOCK), 0)
    col_f = lax.broadcasted_iota(jnp.int32, (KC, COLS), 1).astype(F32) + lon0f
    for b in range(NB):

        @pl.loop(0, nch[b])
        def _(c):
            slot = b * NCH + c
            pick = ((row_id + c * KC).astype(F32) == rank[b : b + 1, :]).astype(F32)
            pick_b = pick.astype(BF)
            a_pk[slot] = dot(pick_b, a_all[b]).astype(BF)
            zero = jnp.zeros_like(pick_b)
            pick3 = jnp.concatenate(
                [
                    jnp.concatenate([pick_b, zero], axis=1),
                    jnp.concatenate([zero, pick_b], axis=1),
                    jnp.concatenate([pick_b, zero], axis=1),
                ],
                axis=0,
            )
            b_pk[slot] = dot(s_all[b], pick3, ((1,), (1,))).astype(BF)
            latc = jnp.sum(pick * lat[b : b + 1, :], axis=1, keepdims=True)
            lonc = jnp.sum(pick * lon[b : b + 1, :], axis=1, keepdims=True)
            dlon = jnp.abs(lonc - col_f)
            dlon = jnp.minimum(dlon, NLON - dlon)
            dlon = dlon * dlon
            for r in range(ROWS):
                dlat = latc - (lat0f + float(r))
                t_pk[slot, :, r * COLS : (r + 1) * COLS] = taper_sq(dlon + dlat * dlat)

    zero256 = jnp.zeros((8, 256), F32)

    @pl.loop(0, NVAR // VG)
    def _(g):
        for i in range(VG):
            for r in range(ROWS):
                xv[i, :, r * COLS : (r + 1) * COLS] = x_ref[g * VG + i, r]

        @pl.loop(0, NB)
        def _(b):
            for i in range(VG):
                for h in range(4):
                    x = xv[i, :, h * 256 : (h + 1) * 256]
                    xh = hi(x)
                    rhs[i, :, h * 256 : (h + 1) * 256] = jnp.concatenate(
                        [xh, xh, x - xh, zero256], axis=0
                    ).astype(BF)

            @pl.loop(0, nch[b])
            def _(c):
                slot = b * NCH + c
                a = a_pk[slot]
                s3 = b_pk[slot]
                for i in range(VG):
                    q = dot(a, rhs[i]) * t_pk[slot]
                    qh = q.astype(BF)
                    q3[i] = jnp.concatenate([qh, qh, (q - qh.astype(F32)).astype(BF)], axis=0)
                for i in range(VG):
                    xv[i] += dot(s3, q3[i])

        for i in range(VG):
            for r in range(ROWS):
                out_ref[
                    pl.ds((g * VG + i) * ROWS + r, MEMBERS, stride=NVAR * ROWS), :
                ] = xv[i, :, r * COLS : (r + 1) * COLS]


def analysis(x, y, lat, lon, val, err):
    vm = pl.BlockSpec(memory_space=pltpu.VMEM)
    return pl.pallas_call(
        analysis_kernel,
        out_shape=jax.ShapeDtypeStruct((MEMBERS * NVAR * ROWS, COLS), F32),
        in_specs=[vm] * 6,
        out_specs=vm,
        scratch_shapes=[
            pltpu.VMEM((MEMBERS, NB * BLOCK), F32),
            pltpu.VMEM((NB, BLOCK, 128), BF),
            pltpu.VMEM((NB, MEMBERS, 256), BF),
            pltpu.VMEM((NB * NCH, KC, 128), BF),
            pltpu.VMEM((NB * NCH, MEMBERS, 3 * KC), BF),
            pltpu.VMEM((NB * NCH, KC, ROWS * COLS), F32),
            pltpu.VMEM((VG, MEMBERS, ROWS * COLS), F32),
            pltpu.VMEM((VG, 128, ROWS * COLS), BF),
            pltpu.VMEM((VG, 3 * KC, ROWS * COLS), BF),
            pltpu.SMEM((NB,), jnp.int32),
        ],
        compiler_params=pltpu.CompilerParams(vmem_limit_bytes=40 << 20),
        name="analysis",
    )(x, y, lat, lon, val, err)


def solution(mesh):
    nlat, nlon = mesh.shape["lat"], mesh.shape["lon"]

    def body(prognostic_samples, wind, obs_lat, obs_lon, obs_var, obs_value, obs_error):
        xf, desc = forecast(
            prognostic_samples.reshape(MEMBERS * NVAR * ROWS, COLS),
            wind, obs_lat, obs_lon, obs_var, nlat, nlon,
        )
        part = pick(desc, xf.reshape(NVAR * ROWS, MEMBERS, COLS))
        y = total_over_devices(part, nlat, nlon)
        out = analysis(xf, y, obs_lat, obs_lon, obs_value, obs_error)
        return out.reshape(prognostic_samples.shape)

    in_specs = (P(None, None, "lat", "lon"), P(None, "lat", "lon"), P(), P(), P(), P(), P())
    out_specs = P(None, None, "lat", "lon")
    return jax.shard_map(body, mesh=mesh, in_specs=in_specs, out_specs=out_specs, check_vma=False)
```

```python
import jax
import jax.numpy as jnp
from jax import lax
from jax.experimental import pallas as pl
from jax.experimental.pallas import tpu as pltpu
from jax.sharding import PartitionSpec as P

MEMBERS, NVAR, ROWS, COLS = 40, 25, 8, 128
NLON = 2048
GROUPS, OBS = 2, 512
NB, BLOCK = 8, 128
PER = OBS // BLOCK
LOC = 32.0
DIFFUSE = 0.1
VS = 5
NVG = NVAR // VS
MG = MEMBERS // 8
KC = 32
NCH = BLOCK // KC
VG = 5
F32, BF = jnp.float32, jnp.bfloat16
MESH = pl.DeviceIdType.MESH


def hi(x):
    return x.astype(BF).astype(F32)


def split(x):
    high = x.astype(BF)
    return high, (x - high.astype(F32)).astype(BF)


def dot(a, b, dims=((1,), (0,))):
    return lax.dot_general(a, b, (dims, ((), ())), preferred_element_type=F32)


def peers(nlat, nlon):
    me_lat = lax.axis_index("lat")
    me_lon = lax.axis_index("lon")

    def place(dlat, dlon):
        lat = lax.rem(me_lat + (dlat + nlat), nlat) if dlat else me_lat
        lon = lax.rem(me_lon + (dlon + nlon), nlon) if dlon else me_lon
        return lat, lon

    def remote(src, dst, ssem, rsem, dlat, dlon):
        return pltpu.make_async_remote_copy(
            src_ref=src,
            dst_ref=dst,
            send_sem=ssem,
            recv_sem=rsem,
            device_id=place(dlat, dlon),
            device_id_type=MESH,
        )

    def signal(barrier, offsets):
        for o in offsets:
            pl.semaphore_signal(barrier, inc=1, device_id=place(*o), device_id_type=MESH)

    return me_lat, me_lon, place, remote, signal


def forecast_kernel(
    nlat, nlon,
    x_hbm, wind_hbm, lat_hbm, lon_hbm, var_hbm,
    xf, out,
    xb, wind_ref, lat_ref, lon_ref, var_ref, desc, desc_s, xft, yo, part, line, block_sum, got_a, got_b,
    xt, edge, edge_w, edge_e, corner, wind_n, halo, halo_s, halo1_s, coef, shift, unit, q1_s,
    s_row, r_row, s_edge, r_edge, s_corner, r_corner, s_wind, r_wind,
    send, recv_a, recv_b, recv_c, l_x, l_small,
):
    def fetch(vg):
        vs = pl.ds(vg * VS, VS)
        return pltpu.make_async_copy(x_hbm.at[:, vs], xb.at[:, vs], l_x.at[vg])

    small = [
        pltpu.make_async_copy(a, b, l_small.at[i])
        for i, (a, b) in enumerate(
            [(wind_hbm, wind_ref), (lat_hbm, lat_ref), (lon_hbm, lon_ref), (var_hbm, var_ref)]
        )
    ]
    for vg in range(NVG):
        fetch(vg).start()
    for c in small:
        c.start()
    x_ref = xb.reshape(MEMBERS * NVAR * ROWS, COLS)
    me_lat, me_lon, place, remote, signal = peers(nlat, nlon)
    barrier = pltpu.get_barrier_semaphore()
    near = [(o, 0) for o in range(1, nlat)] + [(0, o) for o in range(1, nlon)]
    near += [(-1, -1), (-1, 1), (1, -1), (1, 1)]
    signal(barrier, near)

    def column(r, mg, v):
        return x_ref[pl.ds(mg * (8 * NVAR * ROWS) + v * ROWS + r, 8, stride=NVAR * ROWS), :]

    def rows(vg, up):
        vs = pl.ds(vg * VS, VS)
        if up:
            return remote(
                xt.at[vs, 2:4],
                xt.at[vs, ROWS + 2 : ROWS + 4],
                s_row.at[vg, 0], r_row.at[vg, 0], -1, 0,
            )
        return remote(
            xt.at[vs, ROWS : ROWS + 2], xt.at[vs, 0:2], s_row.at[vg, 1], r_row.at[vg, 1], 1, 0
        )

    winds = [
        remote(wind_ref, wind_n.at[i], s_wind.at[i], r_wind.at[i], dlat, dlon)
        for i, (dlat, dlon) in enumerate([(1, 0), (-1, 0), (0, 1), (0, -1)])
    ]
    edges = [
        remote(edge, edge_w, s_edge.at[0], r_edge.at[0], 0, 1),
        remote(edge, edge_e, s_edge.at[1], r_edge.at[1], 0, -1),
    ]
    corners = [
        remote(edge.at[ROWS - 1], corner.at[0], s_corner.at[0], r_corner.at[0], 1, 1),
        remote(edge.at[ROWS - 1], corner.at[1], s_corner.at[1], r_corner.at[1], 1, -1),
        remote(edge.at[0], corner.at[2], s_corner.at[2], r_corner.at[2], -1, 1),
        remote(edge.at[0], corner.at[3], s_corner.at[3], r_corner.at[3], -1, -1),
    ]
    for vg in range(NVG):
        fetch(vg).wait()

        @pl.loop(vg * VS, (vg + 1) * VS)
        def _(v):
            for r in (0, 1, ROWS - 2, ROWS - 1):
                for mg in range(MG):
                    xt[v, r + 2, mg * 8 : (mg + 1) * 8, :] = column(r, mg, v)

        if vg == 0:
            for c in small:
                c.wait()
            pl.semaphore_wait(barrier, len(near))
            for w in winds:
                w.start()
        rows(vg, True).start()
        rows(vg, False).start()

    lane = lax.broadcasted_iota(jnp.int32, (8, COLS), 1)
    edge[...] = jnp.zeros_like(edge)

    @pl.loop(0, NVAR)
    def _(v):
        mine = ((lane - 4 * v + 2) & (COLS - 1)) < 4
        for r in range(ROWS):
            for mg in range(MG):
                ms = slice(mg * 8, (mg + 1) * 8)
                if 2 <= r < ROWS - 2:
                    t = column(r, mg, v)
                    xt[v, r + 2, ms, :] = t
                else:
                    t = xt[v, r + 2, ms, :]
                edge[r, ms, :] = jnp.where(mine, pltpu.roll(t, 4 * v, 1), edge[r, ms, :])

    for e in edges + corners:
        e.start()

    lat_all, lon_all = lat_ref[...], lon_ref[...]
    owned = (lat_all // ROWS == me_lat) & (lon_all // COLS == me_lon)
    desc[...] = (var_ref[...] * ROWS + (lat_all & (ROWS - 1))) * COLS + (lon_all & (COLS - 1))
    to_scalar = pltpu.make_async_copy(desc, desc_s, l_small.at[4])
    to_scalar.start()

    src = lax.rem(lax.broadcasted_iota(jnp.int32, (2 * COLS, 2 * COLS), 0), COLS)
    dst = lax.broadcasted_iota(jnp.int32, (2 * COLS, 2 * COLS), 1)
    east_of = (dst < COLS) & (src == dst + 1)
    west_of = (dst >= COLS) & (src == dst - COLS - 1)
    shift[...] = jnp.where(east_of | west_of, 1.0, 0.0).astype(BF)
    col_of = lax.rem(lax.broadcasted_iota(jnp.int32, (COLS, 2 * COLS), 1), COLS)
    row_of = lax.broadcasted_iota(jnp.int32, (COLS, 2 * COLS), 0)
    unit[...] = jnp.where(col_of == row_of, 1.0, 0.0).astype(BF)

    for w in winds:
        w.wait_recv()
    has_lo = (me_lat > 0).astype(F32)
    has_hi = (me_lat < nlat - 1).astype(F32)

    def row_wind(r):
        if r < 0:
            return wind_n[0, 0, ROWS - 1 : ROWS, :], wind_n[0, 1, ROWS - 1 : ROWS, :]
        if r == ROWS:
            return wind_n[1, 0, 0:1, :], wind_n[1, 1, 0:1, :]
        return wind_ref[0, r : r + 1, :], wind_ref[1, r : r + 1, :]

    def four(u, v, r):
        nxt, prv = DIFFUSE - 0.5 * v, DIFFUSE + 0.5 * v
        if r == 0:
            prv = prv * has_lo
        if r == ROWS - 1:
            nxt = nxt * has_hi
        return DIFFUSE - 0.5 * u, DIFFUSE + 0.5 * u, nxt, prv

    for r in range(-1, ROWS + 1):
        u, v = row_wind(r)
        for i, c in enumerate(four(u, v, r)):
            coef[i, r + 1] = jnp.broadcast_to(c, (8, COLS))

    for e in edges + corners:
        e.wait_recv()
    lane4 = lax.rem(lax.broadcasted_iota(jnp.int32, (MEMBERS, COLS), 1), 4)
    from_west = lane4 >= 2
    halo[0] = jnp.where(from_west, corner[0], corner[1])
    halo[ROWS + 1] = jnp.where(from_west, corner[2], corner[3])
    for r in range(ROWS):
        halo[r + 1] = jnp.where(from_west, edge_w[r], edge_e[r])
    for r in range(ROWS + 2):
        high, low = split(halo[r])
        halo_s[r] = jnp.concatenate([high, low], axis=1)
    for r in range(ROWS):
        u, v = [
            jnp.where(
                from_west,
                jnp.broadcast_to(wind_n[2, i, r : r + 1, COLS - 1 : COLS], (MEMBERS, COLS)),
                jnp.broadcast_to(wind_n[3, i, r : r + 1, 0:1], (MEMBERS, COLS)),
            )
            for i in range(2)
        ]
        ce, cw, cn, cs = four(u, v, r)
        own, got = edge[r], halo[r + 1]
        east = pltpu.roll(jnp.where(lane4 == 0, own, got), COLS - 1, 1)
        west = pltpu.roll(jnp.where(lane4 == 3, own, got), 1, 1)
        after = (
            (1.0 - 4.0 * DIFFUSE) * got
            + ce * east
            + cw * west
            + cn * halo[r + 2]
            + cs * halo[r]
        )
        high, low = split(after)
        halo1_s[r] = jnp.concatenate([high, low], axis=1)

    def step(q, nxt, prv, side, place_side, first, count):
        shape = (count, MG, 8, COLS)
        high, low = split(q)
        both = dot(jnp.concatenate([high, low], axis=1), shift[...]) + dot(
            side.reshape(count * MEMBERS, 2 * COLS), place_side
        )
        c = [coef[i, first : first + count].reshape(count, 1, 8, COLS) for i in range(4)]
        new = (
            (1.0 - 4.0 * DIFFUSE) * q.reshape(shape)
            + c[0] * both[:, :COLS].reshape(shape)
            + c[1] * both[:, COLS:].reshape(shape)
            + c[2] * nxt.reshape(shape)
            + c[3] * prv.reshape(shape)
        )
        return new.reshape(count * MEMBERS, COLS)

    def place_side(v):
        at_end = (dst == COLS - 1) & (src == 4 * v)
        at_start = (dst == COLS) & (src == ((4 * v - 1) & (COLS - 1)))
        return jnp.where(at_end | at_start, 1.0, 0.0).astype(BF)

    def block(ref, v, first, count):
        return ref[v, first : first + count].reshape(count * MEMBERS, COLS)

    @pl.loop(0, NVG)
    def _(vg):
        rows(vg, True).wait_recv()
        rows(vg, False).wait_recv()
        n1, n2 = ROWS + 2, ROWS
        for vi in range(VS):
            v = vg * VS + vi
            q1_s[vi] = step(
                block(xt, v, 1, n1), block(xt, v, 2, n1), block(xt, v, 0, n1),
                halo_s[...], place_side(v), 0, n1,
            ).reshape(n1, MEMBERS, COLS)
        for vi in range(VS):
            v = vg * VS + vi
            new = step(
                block(q1_s, vi, 1, n2), block(q1_s, vi, 2, n2), block(q1_s, vi, 0, n2),
                halo1_s[...], place_side(v), 1, n2,
            )
            xf[v] = new.reshape(n2, MEMBERS, COLS)
            high, low = split(new)
            both = jnp.concatenate([high, low], axis=1)
            for r in range(ROWS):
                xft[pl.ds((v * ROWS + r) * COLS, COLS), 0:MEMBERS] = dot(
                    unit[...], both[r * MEMBERS : (r + 1) * MEMBERS, :], ((1,), (1,))
                )

    to_scalar.wait()
    for b in range(NB):

        @pl.loop(0, BLOCK // 8)
        def _(g):
            for j in range(8):
                k = g * 8 + j
                at = desc_s[b // PER, (b % PER) * BLOCK + k]
                yo[b, pl.ds(k, 1), :] = xft[pl.ds(at, 1), :]

    for b in range(NB):
        mine = owned[b // PER : b // PER + 1, (b % PER) * BLOCK : (b % PER + 1) * BLOCK]
        part[b] = jnp.where(mine, yo[b].T[0:MEMBERS, :], 0.0)

    first = [
        remote(part.at[place(o, 0)[0]], got_a.at[o - 1], send.at[o - 1], recv_a.at[o - 1], o, 0)
        for o in range(1, nlat)
    ]
    for c in first:
        c.start()
    total = part[me_lat]
    for i, c in enumerate(first):
        c.wait_recv()
        total = total + got_a[i]
    line[...] = total
    second = [
        remote(line, got_b.at[o - 1], send.at[nlat + o - 2], recv_b.at[o - 1], 0, o)
        for o in range(1, nlon)
    ]
    for c in second:
        c.start()
    for i, c in enumerate(second):
        c.wait_recv()
        total = total + got_b[i]
    block_sum[...] = total
    third = [
        remote(block_sum, out.at[me_lat], send.at[nlat + nlon + o - 3], recv_c.at[o - 1], o, 0)
        for o in range(1, nlat)
    ]
    for c in third:
        c.start()
    out[me_lat] = total
    for c in third:
        c.wait_recv()

    for c in winds + edges + corners + first + second + third:
        c.wait_send()

    @pl.loop(0, NVG)
    def _(vg):
        rows(vg, True).wait_send()
        rows(vg, False).wait_send()


def forecast(x, wind, lat, lon, var, nlat, nlon):
    vm = pl.BlockSpec(memory_space=pltpu.VMEM)
    dma = pltpu.SemaphoreType.DMA
    return pl.pallas_call(
        lambda *refs: forecast_kernel(nlat, nlon, *refs),
        out_shape=(
            jax.ShapeDtypeStruct((NVAR, ROWS, MEMBERS, COLS), F32),
            jax.ShapeDtypeStruct((NB, MEMBERS, BLOCK), F32),
        ),
        in_specs=[pl.BlockSpec(memory_space=pltpu.HBM)] * 5,
        out_specs=(vm, vm),
        scratch_shapes=[
            pltpu.VMEM((MEMBERS, NVAR, ROWS, COLS), F32),
            pltpu.VMEM((2, ROWS, COLS), F32),
            pltpu.VMEM((GROUPS, OBS), jnp.int32),
            pltpu.VMEM((GROUPS, OBS), jnp.int32),
            pltpu.VMEM((GROUPS, OBS), jnp.int32),
            pltpu.VMEM((GROUPS, OBS), jnp.int32),
            pltpu.SMEM((GROUPS, OBS), jnp.int32),
            pltpu.VMEM((NVAR * ROWS * COLS, COLS), F32),
            pltpu.VMEM((NB, BLOCK, COLS), F32),
            pltpu.VMEM((NB, MEMBERS, BLOCK), F32),
            pltpu.VMEM((MEMBERS, BLOCK), F32),
            pltpu.VMEM((MEMBERS, BLOCK), F32),
            pltpu.VMEM((nlat - 1, MEMBERS, BLOCK), F32),
            pltpu.VMEM((nlon - 1, MEMBERS, BLOCK), F32),
            pltpu.VMEM((NVAR, ROWS + 4, MEMBERS, COLS), F32),
            pltpu.VMEM((ROWS, MEMBERS, COLS), F32),
            pltpu.VMEM((ROWS, MEMBERS, COLS), F32),
            pltpu.VMEM((ROWS, MEMBERS, COLS), F32),
            pltpu.VMEM((4, MEMBERS, COLS), F32),
            pltpu.VMEM((4, 2, ROWS, COLS), F32),
            pltpu.VMEM((ROWS + 2, MEMBERS, COLS), F32),
            pltpu.VMEM((ROWS + 2, MEMBERS, 2 * COLS), BF),
            pltpu.VMEM((ROWS, MEMBERS, 2 * COLS), BF),
            pltpu.VMEM((4, ROWS + 2, 8, COLS), F32),
            pltpu.VMEM((2 * COLS, 2 * COLS), BF),
            pltpu.VMEM((COLS, 2 * COLS), BF),
            pltpu.VMEM((VS, ROWS + 2, MEMBERS, COLS), F32),
            dma((NVG, 2)), dma((NVG, 2)), dma((2,)), dma((2,)),
            dma((4,)), dma((4,)), dma((4,)), dma((4,)),
            dma((2 * nlat + nlon - 3,)), dma((nlat - 1,)), dma((nlon - 1,)), dma((nlat - 1,)),
            dma((NVG,)), dma((5,)),
        ],
        compiler_params=pltpu.CompilerParams(
            collective_id=0, has_side_effects=True, vmem_limit_bytes=34 << 20
        ),
        name="forecast",
    )(x, wind, lat, lon, var)


def taper_sq(d2):
    z = jnp.sqrt(d2) * (1.0 / LOC)
    inner = (((-0.25 * z + 0.5) * z + 0.625) * z - 5.0 / 3.0) * z * z + 1.0
    outer = (
        ((((z * (1.0 / 12.0) - 0.5) * z + 0.625) * z + 5.0 / 3.0) * z - 5.0) * z
        + 4.0
        - (2.0 / 3.0) / jnp.maximum(z, 1.0)
    )
    return jnp.where(z <= 1.0, inner, jnp.where(z < 2.0, outer, 0.0))


def analysis_kernel(
    x_ref, y_ref, lat_ref, lon_ref, val_ref, err_ref,
    out_ref,
    ys, a_all, s_all, a_pk, b_pk, t_pk, xv, rhs, q3, nch,
):
    lat0 = lax.axis_index("lat") * ROWS
    lon0 = lax.axis_index("lon") * COLS

    def by_block(ref):
        rows = [ref[b // PER : b // PER + 1, (b % PER) * BLOCK : (b % PER + 1) * BLOCK] for b in range(NB)]
        return jnp.concatenate(rows, axis=0)

    lat = by_block(lat_ref).astype(F32)
    lon = by_block(lon_ref).astype(F32)
    values = by_block(val_ref)
    variances = by_block(err_ref)
    lat_t = lat.T
    lon_t = lon.T
    lat0f = lat0.astype(F32)
    lon0f = lon0.astype(F32)
    dy = jnp.maximum(jnp.maximum(lat0f - lat, lat - (lat0f + (ROWS - 1))), 0.0)
    off = lon - lon0f
    off = jnp.where(off < 0, off + NLON, off)
    dx = jnp.maximum(jnp.minimum(off - (COLS - 1), NLON - off), 0.0)
    reach = dx * dx + dy * dy < 4.0 * LOC * LOC
    reach_b = reach.astype(F32)
    before = (
        lax.broadcasted_iota(jnp.int32, (BLOCK, BLOCK), 0)
        < lax.broadcasted_iota(jnp.int32, (BLOCK, BLOCK), 1)
    ).astype(F32)
    rank = dot(reach_b.astype(BF), before.astype(BF))
    rank = jnp.where(reach, rank, -1.0)
    for b in range(NB):
        n = jnp.sum(reach_b[b : b + 1, :])
        nch[b] = ((n + (KC - 1)) * (1.0 / KC)).astype(jnp.int32)

    for b in range(NB):
        ys[:, b * BLOCK : (b + 1) * BLOCK] = y_ref[b]
    zero8 = jnp.zeros((8, BLOCK), F32)
    for b in range(NB):
        prior = ys[:, b * BLOCK : (b + 1) * BLOCK]
        average = jnp.sum(prior, axis=0, keepdims=True) * (1.0 / MEMBERS)
        anomaly = prior - average
        spread = jnp.sum(anomaly * anomaly, axis=0, keepdims=True) / (MEMBERS - 1)
        errors = variances[b : b + 1, :]
        total = spread + errors
        weights = anomaly * (1.0 / ((MEMBERS - 1) * total))
        shifts = (values[b : b + 1, :] - average) - anomaly * (
            1.0 / (1.0 + jnp.sqrt(errors / total))
        )
        wh = hi(weights)
        a = jnp.concatenate([wh, weights - wh, wh, zero8], axis=0).T.astype(BF)
        sh = shifts.astype(BF)
        sl = (shifts - sh.astype(F32)).astype(BF)
        s2 = jnp.concatenate([sh, sl], axis=1)
        a_all[b] = a
        s_all[b] = s2
        if b + 1 < NB:
            first = (b + 1) * BLOCK
            s3 = jnp.concatenate([sh, sl, sh], axis=1)
            latk = lat_t[:, b : b + 1]
            lonk = lon_t[:, b : b + 1]
            for j in range(b + 1, NB):
                yl = ys[:, j * BLOCK : (j + 1) * BLOCK]
                yh = hi(yl)
                y3 = jnp.concatenate([yh, yh, yl - yh, zero8], axis=0).astype(BF)
                p = dot(a, y3)
                dlat = latk - lat[j : j + 1, :]
                dlon = jnp.abs(lonk - lon[j : j + 1, :])
                dlon = jnp.minimum(dlon, NLON - dlon)
                q = p * taper_sq(dlat * dlat + dlon * dlon)
                qh = q.astype(BF)
                ql = (q - qh.astype(F32)).astype(BF)
                ys[:, j * BLOCK : (j + 1) * BLOCK] = yl + dot(
                    s3, jnp.concatenate([qh, qh, ql], axis=0)
                )

    row_id = lax.broadcasted_iota(jnp.int32, (KC, BLOCK), 0)
    col_f = lax.broadcasted_iota(jnp.int32, (KC, COLS), 1).astype(F32) + lon0f
    for b in range(NB):

        @pl.loop(0, nch[b])
        def _(c):
            slot = b * NCH + c
            pick = ((row_id + c * KC).astype(F32) == rank[b : b + 1, :]).astype(F32)
            pick_b = pick.astype(BF)
            a_pk[slot] = dot(pick_b, a_all[b]).astype(BF)
            zero = jnp.zeros_like(pick_b)
            pick3 = jnp.concatenate(
                [
                    jnp.concatenate([pick_b, zero], axis=1),
                    jnp.concatenate([zero, pick_b], axis=1),
                    jnp.concatenate([pick_b, zero], axis=1),
                ],
                axis=0,
            )
            b_pk[slot] = dot(s_all[b], pick3, ((1,), (1,))).astype(BF)
            latc = jnp.sum(pick * lat[b : b + 1, :], axis=1, keepdims=True)
            lonc = jnp.sum(pick * lon[b : b + 1, :], axis=1, keepdims=True)
            dlon = jnp.abs(lonc - col_f)
            dlon = jnp.minimum(dlon, NLON - dlon)
            dlon = dlon * dlon
            for r in range(ROWS):
                dlat = latc - (lat0f + float(r))
                t_pk[slot, :, r * COLS : (r + 1) * COLS] = taper_sq(dlon + dlat * dlat)

    zero256 = jnp.zeros((8, 256), F32)

    @pl.loop(0, NVAR // VG)
    def _(g):
        for i in range(VG):
            for r in range(ROWS):
                xv[i, :, r * COLS : (r + 1) * COLS] = x_ref[g * VG + i, r]

        @pl.loop(0, NB)
        def _(b):
            for i in range(VG):
                for h in range(4):
                    x = xv[i, :, h * 256 : (h + 1) * 256]
                    xh = hi(x)
                    rhs[i, :, h * 256 : (h + 1) * 256] = jnp.concatenate(
                        [xh, xh, x - xh, zero256], axis=0
                    ).astype(BF)

            @pl.loop(0, nch[b])
            def _(c):
                slot = b * NCH + c
                a = a_pk[slot]
                s3 = b_pk[slot]
                for i in range(VG):
                    q = dot(a, rhs[i]) * t_pk[slot]
                    qh = q.astype(BF)
                    q3[i] = jnp.concatenate([qh, qh, (q - qh.astype(F32)).astype(BF)], axis=0)
                for i in range(VG):
                    xv[i] += dot(s3, q3[i])

        for i in range(VG):
            for r in range(ROWS):
                out_ref[
                    pl.ds((g * VG + i) * ROWS + r, MEMBERS, stride=NVAR * ROWS), :
                ] = xv[i, :, r * COLS : (r + 1) * COLS]


def analysis(x, y, lat, lon, val, err):
    vm = pl.BlockSpec(memory_space=pltpu.VMEM)
    return pl.pallas_call(
        analysis_kernel,
        out_shape=jax.ShapeDtypeStruct((MEMBERS * NVAR * ROWS, COLS), F32),
        in_specs=[vm] * 6,
        out_specs=vm,
        scratch_shapes=[
            pltpu.VMEM((MEMBERS, NB * BLOCK), F32),
            pltpu.VMEM((NB, BLOCK, 128), BF),
            pltpu.VMEM((NB, MEMBERS, 256), BF),
            pltpu.VMEM((NB * NCH, KC, 128), BF),
            pltpu.VMEM((NB * NCH, MEMBERS, 3 * KC), BF),
            pltpu.VMEM((NB * NCH, KC, ROWS * COLS), F32),
            pltpu.VMEM((VG, MEMBERS, ROWS * COLS), F32),
            pltpu.VMEM((VG, 128, ROWS * COLS), BF),
            pltpu.VMEM((VG, 3 * KC, ROWS * COLS), BF),
            pltpu.SMEM((NB,), jnp.int32),
        ],
        compiler_params=pltpu.CompilerParams(vmem_limit_bytes=16 << 20),
        name="analysis",
    )(x, y, lat, lon, val, err)


def solution(mesh):
    nlat, nlon = mesh.shape["lat"], mesh.shape["lon"]

    def body(prognostic_samples, wind, obs_lat, obs_lon, obs_var, obs_value, obs_error):
        xf, y = forecast(
            prognostic_samples, wind, obs_lat, obs_lon, obs_var, nlat, nlon
        )
        out = analysis(xf, y, obs_lat, obs_lon, obs_value, obs_error)
        return out.reshape(prognostic_samples.shape)

    in_specs = (P(None, None, "lat", "lon"), P(None, "lat", "lon"), P(), P(), P(), P(), P())
    out_specs = P(None, None, "lat", "lon")
    return jax.shard_map(body, mesh=mesh, in_specs=in_specs, out_specs=out_specs, check_vma=False)
```

```python
import jax
import jax.numpy as jnp
from jax import lax
from jax.experimental import pallas as pl
from jax.experimental.pallas import tpu as pltpu
from jax.sharding import PartitionSpec as P

MEMBERS, NVAR, ROWS, COLS = 40, 25, 8, 128
NLON = 2048
GROUPS, OBS = 2, 512
NB, BLOCK = 8, 128
PER = OBS // BLOCK
LOC = 32.0
DIFFUSE = 0.1
VS = 5
NVG = NVAR // VS
MG = MEMBERS // 8
SIDE = (ROWS + 2) // 3
KC = 32
NCH = BLOCK // KC
VG = 5
F32, BF = jnp.float32, jnp.bfloat16
MESH = pl.DeviceIdType.MESH


def hi(x):
    return x.astype(BF).astype(F32)


def split(x):
    high = x.astype(BF)
    return high, (x - high.astype(F32)).astype(BF)


def dot(a, b, dims=((1,), (0,))):
    return lax.dot_general(a, b, (dims, ((), ())), preferred_element_type=F32)


def peers(nlat, nlon):
    me_lat = lax.axis_index("lat")
    me_lon = lax.axis_index("lon")

    def place(dlat, dlon):
        lat = lax.rem(me_lat + (dlat + nlat), nlat) if dlat else me_lat
        lon = lax.rem(me_lon + (dlon + nlon), nlon) if dlon else me_lon
        return lat, lon

    def remote(src, dst, ssem, rsem, dlat, dlon):
        return pltpu.make_async_remote_copy(
            src_ref=src,
            dst_ref=dst,
            send_sem=ssem,
            recv_sem=rsem,
            device_id=place(dlat, dlon),
            device_id_type=MESH,
        )

    def signal(barrier, offsets):
        for o in offsets:
            pl.semaphore_signal(barrier, inc=1, device_id=place(*o), device_id_type=MESH)

    return me_lat, me_lon, place, remote, signal


def forecast_kernel(
    nlat, nlon,
    x_hbm, wind_hbm, lat_hbm, lon_hbm, var_hbm,
    xf, out,
    xb, wind_ref, lat_ref, lon_ref, var_ref, desc, desc_s, xft, yo, part, line, block_sum, got_a, got_b,
    xt, edge, edge_w, edge_e, corner, wind_n, halo, halo_s, halo1_s, coef, shift, unit, q1_s,
    s_row, r_row, s_edge, r_edge, s_corner, r_corner, s_wind, r_wind,
    send, recv_a, recv_b, recv_c, l_x, l_small,
):
    def fetch(vg):
        vs = pl.ds(vg * VS, VS)
        return pltpu.make_async_copy(x_hbm.at[:, vs], xb.at[:, vs], l_x.at[vg])

    small = [
        pltpu.make_async_copy(a, b, l_small.at[i])
        for i, (a, b) in enumerate(
            [(wind_hbm, wind_ref), (lat_hbm, lat_ref), (lon_hbm, lon_ref), (var_hbm, var_ref)]
        )
    ]
    for vg in range(NVG):
        fetch(vg).start()
    for c in small:
        c.start()
    x_ref = xb.reshape(MEMBERS * NVAR * ROWS, COLS)
    me_lat, me_lon, place, remote, signal = peers(nlat, nlon)
    barrier = pltpu.get_barrier_semaphore()
    near = [(o, 0) for o in range(1, nlat)] + [(0, o) for o in range(1, nlon)]
    near += [(-1, -1), (-1, 1), (1, -1), (1, 1)]
    signal(barrier, near)

    def column(r, mg, v):
        return x_ref[pl.ds(mg * (8 * NVAR * ROWS) + v * ROWS + r, 8, stride=NVAR * ROWS), :]

    def rows(vg, up):
        vs = pl.ds(vg * VS, VS)
        if up:
            return remote(
                xt.at[vs, 2:4],
                xt.at[vs, ROWS + 2 : ROWS + 4],
                s_row.at[vg, 0], r_row.at[vg, 0], -1, 0,
            )
        return remote(
            xt.at[vs, ROWS : ROWS + 2], xt.at[vs, 0:2], s_row.at[vg, 1], r_row.at[vg, 1], 1, 0
        )

    def send_rows(vg):
        rows(vg, True).start()
        rows(vg, False).start()

    def sent_rows(vg):
        rows(vg, True).wait_send()
        rows(vg, False).wait_send()

    winds = [
        remote(wind_ref, wind_n.at[i], s_wind.at[i], r_wind.at[i], dlat, dlon)
        for i, (dlat, dlon) in enumerate([(1, 0), (-1, 0), (0, 1), (0, -1)])
    ]
    edges = [
        remote(edge, edge_w, s_edge.at[0], r_edge.at[0], 0, 1),
        remote(edge, edge_e, s_edge.at[1], r_edge.at[1], 0, -1),
    ]
    corners = [
        remote(edge.at[ROWS - 1], corner.at[0], s_corner.at[0], r_corner.at[0], 1, 1),
        remote(edge.at[ROWS - 1], corner.at[1], s_corner.at[1], r_corner.at[1], 1, -1),
        remote(edge.at[0], corner.at[2], s_corner.at[2], r_corner.at[2], -1, 1),
        remote(edge.at[0], corner.at[3], s_corner.at[3], r_corner.at[3], -1, -1),
    ]
    for vg in range(NVG):
        fetch(vg).wait()

        @pl.loop(vg * VS, (vg + 1) * VS)
        def _(v):
            for r in (0, 1, ROWS - 2, ROWS - 1):
                for mg in range(MG):
                    xt[v, r + 2, mg * 8 : (mg + 1) * 8, :] = column(r, mg, v)

        if vg == 0:
            for c in small:
                c.wait()
            pl.semaphore_wait(barrier, len(near))
            for w in winds:
                w.start()
        if vg < 2:
            send_rows(vg)

    lane = lax.broadcasted_iota(jnp.int32, (8, COLS), 1)
    edge[...] = jnp.zeros_like(edge)

    @pl.loop(0, NVAR)
    def _(v):
        mine = ((lane - 4 * v + 2) & (COLS - 1)) < 4
        for r in range(ROWS):
            for mg in range(MG):
                ms = slice(mg * 8, (mg + 1) * 8)
                if 2 <= r < ROWS - 2:
                    t = column(r, mg, v)
                    xt[v, r + 2, ms, :] = t
                else:
                    t = xt[v, r + 2, ms, :]
                edge[r, ms, :] = jnp.where(mine, pltpu.roll(t, 4 * v, 1), edge[r, ms, :])

    for e in edges + corners:
        e.start()
    sent_rows(0)
    send_rows(2)

    lat_all, lon_all = lat_ref[...], lon_ref[...]
    owned = (lat_all // ROWS == me_lat) & (lon_all // COLS == me_lon)
    row_all = lat_all & (ROWS - 1)
    group = (row_all >= 3).astype(jnp.int32) + (row_all >= 6).astype(jnp.int32)
    part_of = row_all - 3 * group
    desc[...] = (var_ref[...] * SIDE + group) * COLS + (lon_all & (COLS - 1))
    to_scalar = pltpu.make_async_copy(desc, desc_s, l_small.at[4])
    to_scalar.start()

    src = lax.rem(lax.broadcasted_iota(jnp.int32, (2 * COLS, 2 * COLS), 0), COLS)
    dst = lax.broadcasted_iota(jnp.int32, (2 * COLS, 2 * COLS), 1)
    east_of = (dst < COLS) & (src == dst + 1)
    west_of = (dst >= COLS) & (src == dst - COLS - 1)
    shift[...] = jnp.where(east_of | west_of, 1.0, 0.0).astype(BF)
    col_of = lax.rem(lax.broadcasted_iota(jnp.int32, (COLS, 2 * COLS), 1), COLS)
    row_of = lax.broadcasted_iota(jnp.int32, (COLS, 2 * COLS), 0)
    unit[...] = jnp.where(col_of == row_of, 1.0, 0.0).astype(BF)

    for w in winds:
        w.wait_recv()
    has_lo = (me_lat > 0).astype(F32)
    has_hi = (me_lat < nlat - 1).astype(F32)

    def row_wind(r):
        if r < 0:
            return wind_n[0, 0, ROWS - 1 : ROWS, :], wind_n[0, 1, ROWS - 1 : ROWS, :]
        if r == ROWS:
            return wind_n[1, 0, 0:1, :], wind_n[1, 1, 0:1, :]
        return wind_ref[0, r : r + 1, :], wind_ref[1, r : r + 1, :]

    def four(u, v, r):
        nxt, prv = DIFFUSE - 0.5 * v, DIFFUSE + 0.5 * v
        if r == 0:
            prv = prv * has_lo
        if r == ROWS - 1:
            nxt = nxt * has_hi
        return DIFFUSE - 0.5 * u, DIFFUSE + 0.5 * u, nxt, prv

    for r in range(-1, ROWS + 1):
        u, v = row_wind(r)
        for i, c in enumerate(four(u, v, r)):
            coef[i, r + 1] = jnp.broadcast_to(c, (8, COLS))

    sent_rows(1)
    send_rows(3)

    for e in edges + corners:
        e.wait_recv()
    lane4 = lax.rem(lax.broadcasted_iota(jnp.int32, (MEMBERS, COLS), 1), 4)
    from_west = lane4 >= 2
    halo[0] = jnp.where(from_west, corner[0], corner[1])
    halo[ROWS + 1] = jnp.where(from_west, corner[2], corner[3])
    for r in range(ROWS):
        halo[r + 1] = jnp.where(from_west, edge_w[r], edge_e[r])
    for r in range(ROWS + 2):
        high, low = split(halo[r])
        halo_s[r] = jnp.concatenate([high, low], axis=1)
    for r in range(ROWS):
        u, v = [
            jnp.where(
                from_west,
                jnp.broadcast_to(wind_n[2, i, r : r + 1, COLS - 1 : COLS], (MEMBERS, COLS)),
                jnp.broadcast_to(wind_n[3, i, r : r + 1, 0:1], (MEMBERS, COLS)),
            )
            for i in range(2)
        ]
        ce, cw, cn, cs = four(u, v, r)
        own, got = edge[r], halo[r + 1]
        east = pltpu.roll(jnp.where(lane4 == 0, own, got), COLS - 1, 1)
        west = pltpu.roll(jnp.where(lane4 == 3, own, got), 1, 1)
        after = (
            (1.0 - 4.0 * DIFFUSE) * got
            + ce * east
            + cw * west
            + cn * halo[r + 2]
            + cs * halo[r]
        )
        high, low = split(after)
        halo1_s[r] = jnp.concatenate([high, low], axis=1)

    def step(q, nxt, prv, side, place_side, first, count):
        shape = (count, MG, 8, COLS)
        high, low = split(q)
        both = dot(jnp.concatenate([high, low], axis=1), shift[...]) + dot(
            side.reshape(count * MEMBERS, 2 * COLS), place_side
        )
        c = [coef[i, first : first + count].reshape(count, 1, 8, COLS) for i in range(4)]
        new = (
            (1.0 - 4.0 * DIFFUSE) * q.reshape(shape)
            + c[0] * both[:, :COLS].reshape(shape)
            + c[1] * both[:, COLS:].reshape(shape)
            + c[2] * nxt.reshape(shape)
            + c[3] * prv.reshape(shape)
        )
        return new.reshape(count * MEMBERS, COLS)

    def place_side(v):
        at_end = (dst == COLS - 1) & (src == 4 * v)
        at_start = (dst == COLS) & (src == ((4 * v - 1) & (COLS - 1)))
        return jnp.where(at_end | at_start, 1.0, 0.0).astype(BF)

    def block(ref, v, first, count):
        return ref[v, first : first + count].reshape(count * MEMBERS, COLS)

    @pl.loop(0, NVG)
    def _(vg):
        rows(vg, True).wait_recv()
        rows(vg, False).wait_recv()

        @pl.when(vg == 0)
        def _():
            sent_rows(2)
            send_rows(4)

        n1, n2 = ROWS + 2, ROWS
        for vi in range(VS):
            v = vg * VS + vi
            q1_s[vi] = step(
                block(xt, v, 1, n1), block(xt, v, 2, n1), block(xt, v, 0, n1),
                halo_s[...], place_side(v), 0, n1,
            ).reshape(n1, MEMBERS, COLS)
        for vi in range(VS):
            v = vg * VS + vi
            new = step(
                block(q1_s, vi, 1, n2), block(q1_s, vi, 2, n2), block(q1_s, vi, 0, n2),
                halo1_s[...], place_side(v), 1, n2,
            )
            xf[v] = new.reshape(n2, MEMBERS, COLS)
            high, low = split(new)
            both = jnp.concatenate([high, low], axis=1)
            for i in range(SIDE):
                n = min(3, ROWS - 3 * i) * MEMBERS
                xft[pl.ds((v * SIDE + i) * COLS, COLS), 0:n] = dot(
                    unit[...], both[i * 3 * MEMBERS : i * 3 * MEMBERS + n, :], ((1,), (1,))
                )

    to_scalar.wait()
    for b in range(NB):

        @pl.loop(0, BLOCK // 8)
        def _(g):
            for j in range(8):
                k = g * 8 + j
                at = desc_s[b // PER, (b % PER) * BLOCK + k]
                yo[b, pl.ds(k, 1), :] = xft[pl.ds(at, 1), :]

    for b in range(NB):
        cut = (slice(b // PER, b // PER + 1), slice((b % PER) * BLOCK, (b % PER + 1) * BLOCK))
        turned = yo[b].T
        at = jnp.broadcast_to(jnp.where(owned[cut], part_of[cut], -1), (MEMBERS, BLOCK))
        mine = jnp.zeros((MEMBERS, BLOCK), F32)
        for i in range(3):
            mine = jnp.where(at == i, turned[i * MEMBERS : (i + 1) * MEMBERS, :], mine)
        part[b] = mine

    first = [
        remote(part.at[place(o, 0)[0]], got_a.at[o - 1], send.at[o - 1], recv_a.at[o - 1], o, 0)
        for o in range(1, nlat)
    ]
    for c in first:
        c.start()
    total = part[me_lat]
    for i, c in enumerate(first):
        c.wait_recv()
        total = total + got_a[i]
    line[...] = total
    second = [
        remote(line, got_b.at[o - 1], send.at[nlat + o - 2], recv_b.at[o - 1], 0, o)
        for o in range(1, nlon)
    ]
    for c in second:
        c.start()
    for i, c in enumerate(second):
        c.wait_recv()
        total = total + got_b[i]
    block_sum[...] = total
    third = [
        remote(block_sum, out.at[me_lat], send.at[nlat + nlon + o - 3], recv_c.at[o - 1], o, 0)
        for o in range(1, nlat)
    ]
    for c in third:
        c.start()
    out[me_lat] = total
    for c in third:
        c.wait_recv()

    for c in winds + edges + corners + first + second + third:
        c.wait_send()

    sent_rows(3)
    sent_rows(4)


def forecast(x, wind, lat, lon, var, nlat, nlon):
    vm = pl.BlockSpec(memory_space=pltpu.VMEM)
    dma = pltpu.SemaphoreType.DMA
    return pl.pallas_call(
        lambda *refs: forecast_kernel(nlat, nlon, *refs),
        out_shape=(
            jax.ShapeDtypeStruct((NVAR, ROWS, MEMBERS, COLS), F32),
            jax.ShapeDtypeStruct((NB, MEMBERS, BLOCK), F32),
        ),
        in_specs=[pl.BlockSpec(memory_space=pltpu.HBM)] * 5,
        out_specs=(vm, vm),
        scratch_shapes=[
            pltpu.VMEM((MEMBERS, NVAR, ROWS, COLS), F32),
            pltpu.VMEM((2, ROWS, COLS), F32),
            pltpu.VMEM((GROUPS, OBS), jnp.int32),
            pltpu.VMEM((GROUPS, OBS), jnp.int32),
            pltpu.VMEM((GROUPS, OBS), jnp.int32),
            pltpu.VMEM((GROUPS, OBS), jnp.int32),
            pltpu.SMEM((GROUPS, OBS), jnp.int32),
            pltpu.VMEM((NVAR * SIDE * COLS, COLS), F32),
            pltpu.VMEM((NB, BLOCK, COLS), F32),
            pltpu.VMEM((NB, MEMBERS, BLOCK), F32),
            pltpu.VMEM((MEMBERS, BLOCK), F32),
            pltpu.VMEM((MEMBERS, BLOCK), F32),
            pltpu.VMEM((nlat - 1, MEMBERS, BLOCK), F32),
            pltpu.VMEM((nlon - 1, MEMBERS, BLOCK), F32),
            pltpu.VMEM((NVAR, ROWS + 4, MEMBERS, COLS), F32),
            pltpu.VMEM((ROWS, MEMBERS, COLS), F32),
            pltpu.VMEM((ROWS, MEMBERS, COLS), F32),
            pltpu.VMEM((ROWS, MEMBERS, COLS), F32),
            pltpu.VMEM((4, MEMBERS, COLS), F32),
            pltpu.VMEM((4, 2, ROWS, COLS), F32),
            pltpu.VMEM((ROWS + 2, MEMBERS, COLS), F32),
            pltpu.VMEM((ROWS + 2, MEMBERS, 2 * COLS), BF),
            pltpu.VMEM((ROWS, MEMBERS, 2 * COLS), BF),
            pltpu.VMEM((4, ROWS + 2, 8, COLS), F32),
            pltpu.VMEM((2 * COLS, 2 * COLS), BF),
            pltpu.VMEM((COLS, 2 * COLS), BF),
            pltpu.VMEM((VS, ROWS + 2, MEMBERS, COLS), F32),
            dma((NVG, 2)), dma((NVG, 2)), dma((2,)), dma((2,)),
            dma((4,)), dma((4,)), dma((4,)), dma((4,)),
            dma((2 * nlat + nlon - 3,)), dma((nlat - 1,)), dma((nlon - 1,)), dma((nlat - 1,)),
            dma((NVG,)), dma((5,)),
        ],
        compiler_params=pltpu.CompilerParams(
            collective_id=0, has_side_effects=True, vmem_limit_bytes=34 << 20
        ),
        name="forecast",
    )(x, wind, lat, lon, var)


def taper_sq(d2):
    z = jnp.sqrt(d2) * (1.0 / LOC)
    inner = (((-0.25 * z + 0.5) * z + 0.625) * z - 5.0 / 3.0) * z * z + 1.0
    outer = (
        ((((z * (1.0 / 12.0) - 0.5) * z + 0.625) * z + 5.0 / 3.0) * z - 5.0) * z
        + 4.0
        - (2.0 / 3.0) / jnp.maximum(z, 1.0)
    )
    return jnp.where(z <= 1.0, inner, jnp.where(z < 2.0, outer, 0.0))


def analysis_kernel(
    x_ref, y_ref, lat_ref, lon_ref, val_ref, err_ref,
    out_ref,
    ys, a_all, s_all, a_pk, b_pk, t_pk, xv, rhs, q3, nch,
):
    lat0 = lax.axis_index("lat") * ROWS
    lon0 = lax.axis_index("lon") * COLS

    def by_block(ref):
        rows = [ref[b // PER : b // PER + 1, (b % PER) * BLOCK : (b % PER + 1) * BLOCK] for b in range(NB)]
        return jnp.concatenate(rows, axis=0)

    lat = by_block(lat_ref).astype(F32)
    lon = by_block(lon_ref).astype(F32)
    values = by_block(val_ref)
    variances = by_block(err_ref)
    lat_t = lat.T
    lon_t = lon.T
    lat0f = lat0.astype(F32)
    lon0f = lon0.astype(F32)
    dy = jnp.maximum(jnp.maximum(lat0f - lat, lat - (lat0f + (ROWS - 1))), 0.0)
    off = lon - lon0f
    off = jnp.where(off < 0, off + NLON, off)
    dx = jnp.maximum(jnp.minimum(off - (COLS - 1), NLON - off), 0.0)
    reach = dx * dx + dy * dy < 4.0 * LOC * LOC
    reach_b = reach.astype(F32)
    before = (
        lax.broadcasted_iota(jnp.int32, (BLOCK, BLOCK), 0)
        < lax.broadcasted_iota(jnp.int32, (BLOCK, BLOCK), 1)
    ).astype(F32)
    rank = dot(reach_b.astype(BF), before.astype(BF))
    rank = jnp.where(reach, rank, -1.0)
    for b in range(NB):
        n = jnp.sum(reach_b[b : b + 1, :])
        nch[b] = ((n + (KC - 1)) * (1.0 / KC)).astype(jnp.int32)

    for b in range(NB):
        ys[:, b * BLOCK : (b + 1) * BLOCK] = y_ref[b]
    zero8 = jnp.zeros((8, BLOCK), F32)
    for b in range(NB):
        prior = ys[:, b * BLOCK : (b + 1) * BLOCK]
        average = jnp.sum(prior, axis=0, keepdims=True) * (1.0 / MEMBERS)
        anomaly = prior - average
        spread = jnp.sum(anomaly * anomaly, axis=0, keepdims=True) / (MEMBERS - 1)
        errors = variances[b : b + 1, :]
        total = spread + errors
        weights = anomaly * (1.0 / ((MEMBERS - 1) * total))
        shifts = (values[b : b + 1, :] - average) - anomaly * (
            1.0 / (1.0 + jnp.sqrt(errors / total))
        )
        wh = hi(weights)
        a = jnp.concatenate([wh, weights - wh, wh, zero8], axis=0).T.astype(BF)
        sh = shifts.astype(BF)
        sl = (shifts - sh.astype(F32)).astype(BF)
        s2 = jnp.concatenate([sh, sl], axis=1)
        a_all[b] = a
        s_all[b] = s2
        if b + 1 < NB:
            first = (b + 1) * BLOCK
            s3 = jnp.concatenate([sh, sl, sh], axis=1)
            latk = lat_t[:, b : b + 1]
            lonk = lon_t[:, b : b + 1]
            for j in range(b + 1, NB):
                yl = ys[:, j * BLOCK : (j + 1) * BLOCK]
                yh = hi(yl)
                y3 = jnp.concatenate([yh, yh, yl - yh, zero8], axis=0).astype(BF)
                p = dot(a, y3)
                dlat = latk - lat[j : j + 1, :]
                dlon = jnp.abs(lonk - lon[j : j + 1, :])
                dlon = jnp.minimum(dlon, NLON - dlon)
                q = p * taper_sq(dlat * dlat + dlon * dlon)
                qh = q.astype(BF)
                ql = (q - qh.astype(F32)).astype(BF)
                ys[:, j * BLOCK : (j + 1) * BLOCK] = yl + dot(
                    s3, jnp.concatenate([qh, qh, ql], axis=0)
                )

    row_id = lax.broadcasted_iota(jnp.int32, (KC, BLOCK), 0)
    col_f = lax.broadcasted_iota(jnp.int32, (KC, COLS), 1).astype(F32) + lon0f
    for b in range(NB):

        @pl.loop(0, nch[b])
        def _(c):
            slot = b * NCH + c
            pick = ((row_id + c * KC).astype(F32) == rank[b : b + 1, :]).astype(F32)
            pick_b = pick.astype(BF)
            a_pk[slot] = dot(pick_b, a_all[b]).astype(BF)
            zero = jnp.zeros_like(pick_b)
            pick3 = jnp.concatenate(
                [
                    jnp.concatenate([pick_b, zero], axis=1),
                    jnp.concatenate([zero, pick_b], axis=1),
                    jnp.concatenate([pick_b, zero], axis=1),
                ],
                axis=0,
            )
            b_pk[slot] = dot(s_all[b], pick3, ((1,), (1,))).astype(BF)
            latc = jnp.sum(pick * lat[b : b + 1, :], axis=1, keepdims=True)
            lonc = jnp.sum(pick * lon[b : b + 1, :], axis=1, keepdims=True)
            dlon = jnp.abs(lonc - col_f)
            dlon = jnp.minimum(dlon, NLON - dlon)
            dlon = dlon * dlon
            for r in range(ROWS):
                dlat = latc - (lat0f + float(r))
                t_pk[slot, :, r * COLS : (r + 1) * COLS] = taper_sq(dlon + dlat * dlat)

    zero256 = jnp.zeros((8, 256), F32)

    @pl.loop(0, NVAR // VG)
    def _(g):
        for i in range(VG):
            for r in range(ROWS):
                xv[i, :, r * COLS : (r + 1) * COLS] = x_ref[g * VG + i, r]

        @pl.loop(0, NB)
        def _(b):
            for i in range(VG):
                for h in range(4):
                    x = xv[i, :, h * 256 : (h + 1) * 256]
                    xh = hi(x)
                    rhs[i, :, h * 256 : (h + 1) * 256] = jnp.concatenate(
                        [xh, xh, x - xh, zero256], axis=0
                    ).astype(BF)

            @pl.loop(0, nch[b])
            def _(c):
                slot = b * NCH + c
                a = a_pk[slot]
                s3 = b_pk[slot]
                for i in range(VG):
                    q = dot(a, rhs[i]) * t_pk[slot]
                    qh = q.astype(BF)
                    q3[i] = jnp.concatenate([qh, qh, (q - qh.astype(F32)).astype(BF)], axis=0)
                for i in range(VG):
                    xv[i] += dot(s3, q3[i])

        for i in range(VG):
            for r in range(ROWS):
                out_ref[
                    pl.ds((g * VG + i) * ROWS + r, MEMBERS, stride=NVAR * ROWS), :
                ] = xv[i, :, r * COLS : (r + 1) * COLS]


def analysis(x, y, lat, lon, val, err):
    vm = pl.BlockSpec(memory_space=pltpu.VMEM)
    return pl.pallas_call(
        analysis_kernel,
        out_shape=jax.ShapeDtypeStruct((MEMBERS * NVAR * ROWS, COLS), F32),
        in_specs=[vm] * 6,
        out_specs=vm,
        scratch_shapes=[
            pltpu.VMEM((MEMBERS, NB * BLOCK), F32),
            pltpu.VMEM((NB, BLOCK, 128), BF),
            pltpu.VMEM((NB, MEMBERS, 256), BF),
            pltpu.VMEM((NB * NCH, KC, 128), BF),
            pltpu.VMEM((NB * NCH, MEMBERS, 3 * KC), BF),
            pltpu.VMEM((NB * NCH, KC, ROWS * COLS), F32),
            pltpu.VMEM((VG, MEMBERS, ROWS * COLS), F32),
            pltpu.VMEM((VG, 128, ROWS * COLS), BF),
            pltpu.VMEM((VG, 3 * KC, ROWS * COLS), BF),
            pltpu.SMEM((NB,), jnp.int32),
        ],
        compiler_params=pltpu.CompilerParams(vmem_limit_bytes=16 << 20),
        name="analysis",
    )(x, y, lat, lon, val, err)


def solution(mesh):
    nlat, nlon = mesh.shape["lat"], mesh.shape["lon"]

    def body(prognostic_samples, wind, obs_lat, obs_lon, obs_var, obs_value, obs_error):
        args = [
            pltpu.with_memory_space_constraint(a, pltpu.HBM)
            for a in (prognostic_samples, wind, obs_lat, obs_lon, obs_var)
        ]
        xf, y = forecast(*args, nlat, nlon)
        out = analysis(xf, y, obs_lat, obs_lon, obs_value, obs_error)
        return out.reshape(prognostic_samples.shape)

    in_specs = (P(None, None, "lat", "lon"), P(None, "lat", "lon"), P(), P(), P(), P(), P())
    out_specs = P(None, None, "lat", "lon")
    return jax.shard_map(body, mesh=mesh, in_specs=in_specs, out_specs=out_specs, check_vma=False)
```

```python
import jax
import jax.numpy as jnp
from jax import lax
from jax.experimental import pallas as pl
from jax.experimental.pallas import tpu as pltpu
from jax.sharding import PartitionSpec as P

MEMBERS, NVAR, ROWS, COLS = 40, 25, 8, 128
NLON = 2048
GROUPS, OBS = 2, 512
NB, BLOCK = 8, 128
PER = OBS // BLOCK
LOC = 32.0
DIFFUSE = 0.1
VS = 5
NVG = NVAR // VS
MG = MEMBERS // 8
SIDE = (ROWS + 2) // 3
KC = 32
NCH = BLOCK // KC
VG = 5
F32, BF = jnp.float32, jnp.bfloat16
MESH = pl.DeviceIdType.MESH


def hi(x):
    return x.astype(BF).astype(F32)


def split(x):
    high = x.astype(BF)
    return high, (x - high.astype(F32)).astype(BF)


def dot(a, b, dims=((1,), (0,))):
    return lax.dot_general(a, b, (dims, ((), ())), preferred_element_type=F32)


def peers(nlat, nlon):
    me_lat = lax.axis_index("lat")
    me_lon = lax.axis_index("lon")

    def place(dlat, dlon):
        lat = lax.rem(me_lat + (dlat + nlat), nlat) if dlat else me_lat
        lon = lax.rem(me_lon + (dlon + nlon), nlon) if dlon else me_lon
        return lat, lon

    def remote(src, dst, ssem, rsem, dlat, dlon):
        return pltpu.make_async_remote_copy(
            src_ref=src,
            dst_ref=dst,
            send_sem=ssem,
            recv_sem=rsem,
            device_id=place(dlat, dlon),
            device_id_type=MESH,
        )

    def signal(barrier, offsets):
        for o in offsets:
            pl.semaphore_signal(barrier, inc=1, device_id=place(*o), device_id_type=MESH)

    return me_lat, me_lon, place, remote, signal


def taper_sq(d2):
    z = jnp.sqrt(d2) * (1.0 / LOC)
    inner = (((-0.25 * z + 0.5) * z + 0.625) * z - 5.0 / 3.0) * z * z + 1.0
    outer = (
        ((((z * (1.0 / 12.0) - 0.5) * z + 0.625) * z + 5.0 / 3.0) * z - 5.0) * z
        + 4.0
        - (2.0 / 3.0) / jnp.maximum(z, 1.0)
    )
    return jnp.where(z <= 1.0, inner, jnp.where(z < 2.0, outer, 0.0))


def by_block(ref):
    parts = []
    for b in range(NB):
        first = (b % PER) * BLOCK
        parts.append(ref[b // PER : b // PER + 1, first : first + BLOCK])
    return jnp.concatenate(parts, axis=0)


def pair_at(b, j):
    return b * (2 * NB - b - 1) // 2 + j - b - 1


def cell_tapers(pick, lat_row, lon_row, lat0f, lon0f, out, slot):
    col_f = lax.broadcasted_iota(jnp.int32, (KC, COLS), 1).astype(F32) + lon0f
    latc = jnp.sum(pick * lat_row, axis=1, keepdims=True)
    lonc = jnp.sum(pick * lon_row, axis=1, keepdims=True)
    dlon = jnp.abs(lonc - col_f)
    dlon = jnp.minimum(dlon, NLON - dlon)
    dlon = dlon * dlon
    for r in range(ROWS):
        dlat = latc - (lat0f + float(r))
        out[slot, :, r * COLS : (r + 1) * COLS] = taper_sq(dlon + dlat * dlat)


def reach_tables(lat, lon, lat0f, lon0f, rank_ref, t0_ref):
    dy = jnp.maximum(jnp.maximum(lat0f - lat, lat - (lat0f + (ROWS - 1))), 0.0)
    off = lon - lon0f
    off = jnp.where(off < 0, off + NLON, off)
    dx = jnp.maximum(jnp.minimum(off - (COLS - 1), NLON - off), 0.0)
    reach = dx * dx + dy * dy < 4.0 * LOC * LOC
    before = (
        lax.broadcasted_iota(jnp.int32, (BLOCK, BLOCK), 0)
        < lax.broadcasted_iota(jnp.int32, (BLOCK, BLOCK), 1)
    ).astype(F32)
    rank = jnp.where(reach, dot(reach.astype(F32).astype(BF), before.astype(BF)), -1.0)
    rank_ref[...] = rank
    row_id = lax.broadcasted_iota(jnp.int32, (KC, BLOCK), 0).astype(F32)
    for b in range(NB):
        pick = (row_id == rank[b : b + 1, :]).astype(F32)
        cell_tapers(pick, lat[b : b + 1, :], lon[b : b + 1, :], lat0f, lon0f, t0_ref, b)


def pair_tables(lat, lon, pair_ref):
    lat_t, lon_t = lat.T, lon.T
    for b in range(NB):
        for j in range(b + 1, NB):
            dlat = lat_t[:, b : b + 1] - lat[j : j + 1, :]
            dlon = jnp.abs(lon_t[:, b : b + 1] - lon[j : j + 1, :])
            dlon = jnp.minimum(dlon, NLON - dlon)
            pair_ref[pair_at(b, j)] = taper_sq(dlat * dlat + dlon * dlon)


def forecast_kernel(
    nlat, nlon,
    x_hbm, wind_hbm, lat_hbm, lon_hbm, var_hbm,
    xf, out, rank_ref, t0_ref, pair_ref,
    xb, wind_ref, lat_ref, lon_ref, var_ref, desc, desc_s, xft, yo, part, line, block_sum, got_a, got_b,
    xt, edge, edge_w, edge_e, corner, wind_n, halo, halo_s, halo1_s, coef, shift, unit, q1_s,
    s_row, r_row, s_edge, r_edge, s_corner, r_corner, s_wind, r_wind,
    send, recv_a, recv_b, recv_c, l_x, l_small,
):
    def fetch(vg):
        vs = pl.ds(vg * VS, VS)
        return pltpu.make_async_copy(x_hbm.at[:, vs], xb.at[:, vs], l_x.at[vg])

    small = [
        pltpu.make_async_copy(a, b, l_small.at[i])
        for i, (a, b) in enumerate(
            [(wind_hbm, wind_ref), (lat_hbm, lat_ref), (lon_hbm, lon_ref), (var_hbm, var_ref)]
        )
    ]
    for vg in range(NVG):
        fetch(vg).start()
    for c in small:
        c.start()
    x_ref = xb.reshape(MEMBERS * NVAR * ROWS, COLS)
    me_lat, me_lon, place, remote, signal = peers(nlat, nlon)
    barrier = pltpu.get_barrier_semaphore()
    near = [(o, 0) for o in range(1, nlat)] + [(0, o) for o in range(1, nlon)]
    near += [(-1, -1), (-1, 1), (1, -1), (1, 1)]
    signal(barrier, near)

    def column(r, mg, v):
        return x_ref[pl.ds(mg * (8 * NVAR * ROWS) + v * ROWS + r, 8, stride=NVAR * ROWS), :]

    def rows(vg, up):
        vs = pl.ds(vg * VS, VS)
        if up:
            return remote(
                xt.at[vs, 2:4],
                xt.at[vs, ROWS + 2 : ROWS + 4],
                s_row.at[vg, 0], r_row.at[vg, 0], -1, 0,
            )
        return remote(
            xt.at[vs, ROWS : ROWS + 2], xt.at[vs, 0:2], s_row.at[vg, 1], r_row.at[vg, 1], 1, 0
        )

    def send_rows(vg):
        rows(vg, True).start()
        rows(vg, False).start()

    def sent_rows(vg):
        rows(vg, True).wait_send()
        rows(vg, False).wait_send()

    winds = [
        remote(wind_ref, wind_n.at[i], s_wind.at[i], r_wind.at[i], dlat, dlon)
        for i, (dlat, dlon) in enumerate([(1, 0), (-1, 0), (0, 1), (0, -1)])
    ]
    edges = [
        remote(edge, edge_w, s_edge.at[0], r_edge.at[0], 0, 1),
        remote(edge, edge_e, s_edge.at[1], r_edge.at[1], 0, -1),
    ]
    corners = [
        remote(edge.at[ROWS - 1], corner.at[0], s_corner.at[0], r_corner.at[0], 1, 1),
        remote(edge.at[ROWS - 1], corner.at[1], s_corner.at[1], r_corner.at[1], 1, -1),
        remote(edge.at[0], corner.at[2], s_corner.at[2], r_corner.at[2], -1, 1),
        remote(edge.at[0], corner.at[3], s_corner.at[3], r_corner.at[3], -1, -1),
    ]
    for vg in range(NVG):
        fetch(vg).wait()

        @pl.loop(vg * VS, (vg + 1) * VS)
        def _(v):
            for r in (0, 1, ROWS - 2, ROWS - 1):
                for mg in range(MG):
                    xt[v, r + 2, mg * 8 : (mg + 1) * 8, :] = column(r, mg, v)

        if vg == 0:
            for c in small:
                c.wait()
            pl.semaphore_wait(barrier, len(near))
            for w in winds:
                w.start()
        if vg < 2:
            send_rows(vg)

    lane = lax.broadcasted_iota(jnp.int32, (8, COLS), 1)
    edge[...] = jnp.zeros_like(edge)

    @pl.loop(0, NVAR)
    def _(v):
        mine = ((lane - 4 * v + 2) & (COLS - 1)) < 4
        for r in range(ROWS):
            for mg in range(MG):
                ms = slice(mg * 8, (mg + 1) * 8)
                if 2 <= r < ROWS - 2:
                    t = column(r, mg, v)
                    xt[v, r + 2, ms, :] = t
                else:
                    t = xt[v, r + 2, ms, :]
                edge[r, ms, :] = jnp.where(mine, pltpu.roll(t, 4 * v, 1), edge[r, ms, :])

    for e in edges + corners:
        e.start()
    sent_rows(0)
    send_rows(2)

    lat_all, lon_all = lat_ref[...], lon_ref[...]
    owned = (lat_all // ROWS == me_lat) & (lon_all // COLS == me_lon)
    row_all = lat_all & (ROWS - 1)
    group = (row_all >= 3).astype(jnp.int32) + (row_all >= 6).astype(jnp.int32)
    part_of = row_all - 3 * group
    desc[...] = (var_ref[...] * SIDE + group) * COLS + (lon_all & (COLS - 1))
    to_scalar = pltpu.make_async_copy(desc, desc_s, l_small.at[4])
    to_scalar.start()

    src = lax.rem(lax.broadcasted_iota(jnp.int32, (2 * COLS, 2 * COLS), 0), COLS)
    dst = lax.broadcasted_iota(jnp.int32, (2 * COLS, 2 * COLS), 1)
    east_of = (dst < COLS) & (src == dst + 1)
    west_of = (dst >= COLS) & (src == dst - COLS - 1)
    shift[...] = jnp.where(east_of | west_of, 1.0, 0.0).astype(BF)
    col_of = lax.rem(lax.broadcasted_iota(jnp.int32, (COLS, 2 * COLS), 1), COLS)
    row_of = lax.broadcasted_iota(jnp.int32, (COLS, 2 * COLS), 0)
    unit[...] = jnp.where(col_of == row_of, 1.0, 0.0).astype(BF)

    for w in winds:
        w.wait_recv()
    has_lo = (me_lat > 0).astype(F32)
    has_hi = (me_lat < nlat - 1).astype(F32)

    def row_wind(r):
        if r < 0:
            return wind_n[0, 0, ROWS - 1 : ROWS, :], wind_n[0, 1, ROWS - 1 : ROWS, :]
        if r == ROWS:
            return wind_n[1, 0, 0:1, :], wind_n[1, 1, 0:1, :]
        return wind_ref[0, r : r + 1, :], wind_ref[1, r : r + 1, :]

    def four(u, v, r):
        nxt, prv = DIFFUSE - 0.5 * v, DIFFUSE + 0.5 * v
        if r == 0:
            prv = prv * has_lo
        if r == ROWS - 1:
            nxt = nxt * has_hi
        return DIFFUSE - 0.5 * u, DIFFUSE + 0.5 * u, nxt, prv

    for r in range(-1, ROWS + 1):
        u, v = row_wind(r)
        for i, c in enumerate(four(u, v, r)):
            coef[i, r + 1] = jnp.broadcast_to(c, (8, COLS))

    sent_rows(1)
    send_rows(3)

    for e in edges + corners:
        e.wait_recv()
    lane4 = lax.rem(lax.broadcasted_iota(jnp.int32, (MEMBERS, COLS), 1), 4)
    from_west = lane4 >= 2
    halo[0] = jnp.where(from_west, corner[0], corner[1])
    halo[ROWS + 1] = jnp.where(from_west, corner[2], corner[3])
    for r in range(ROWS):
        halo[r + 1] = jnp.where(from_west, edge_w[r], edge_e[r])
    for r in range(ROWS + 2):
        high, low = split(halo[r])
        halo_s[r] = jnp.concatenate([high, low], axis=1)
    for r in range(ROWS):
        u, v = [
            jnp.where(
                from_west,
                jnp.broadcast_to(wind_n[2, i, r : r + 1, COLS - 1 : COLS], (MEMBERS, COLS)),
                jnp.broadcast_to(wind_n[3, i, r : r + 1, 0:1], (MEMBERS, COLS)),
            )
            for i in range(2)
        ]
        ce, cw, cn, cs = four(u, v, r)
        own, got = edge[r], halo[r + 1]
        east = pltpu.roll(jnp.where(lane4 == 0, own, got), COLS - 1, 1)
        west = pltpu.roll(jnp.where(lane4 == 3, own, got), 1, 1)
        after = (
            (1.0 - 4.0 * DIFFUSE) * got
            + ce * east
            + cw * west
            + cn * halo[r + 2]
            + cs * halo[r]
        )
        high, low = split(after)
        halo1_s[r] = jnp.concatenate([high, low], axis=1)

    def step(q, nxt, prv, side, place_side, first, count):
        shape = (count, MG, 8, COLS)
        high, low = split(q)
        both = dot(jnp.concatenate([high, low], axis=1), shift[...]) + dot(
            side.reshape(count * MEMBERS, 2 * COLS), place_side
        )
        c = [coef[i, first : first + count].reshape(count, 1, 8, COLS) for i in range(4)]
        new = (
            (1.0 - 4.0 * DIFFUSE) * q.reshape(shape)
            + c[0] * both[:, :COLS].reshape(shape)
            + c[1] * both[:, COLS:].reshape(shape)
            + c[2] * nxt.reshape(shape)
            + c[3] * prv.reshape(shape)
        )
        return new.reshape(count * MEMBERS, COLS)

    def place_side(v):
        at_end = (dst == COLS - 1) & (src == 4 * v)
        at_start = (dst == COLS) & (src == ((4 * v - 1) & (COLS - 1)))
        return jnp.where(at_end | at_start, 1.0, 0.0).astype(BF)

    def block(ref, v, first, count):
        return ref[v, first : first + count].reshape(count * MEMBERS, COLS)

    @pl.loop(0, NVG)
    def _(vg):
        rows(vg, True).wait_recv()
        rows(vg, False).wait_recv()

        @pl.when(vg == 0)
        def _():
            sent_rows(2)
            send_rows(4)

        n1, n2 = ROWS + 2, ROWS
        for vi in range(VS):
            v = vg * VS + vi
            q1_s[vi] = step(
                block(xt, v, 1, n1), block(xt, v, 2, n1), block(xt, v, 0, n1),
                halo_s[...], place_side(v), 0, n1,
            ).reshape(n1, MEMBERS, COLS)
        for vi in range(VS):
            v = vg * VS + vi
            new = step(
                block(q1_s, vi, 1, n2), block(q1_s, vi, 2, n2), block(q1_s, vi, 0, n2),
                halo1_s[...], place_side(v), 1, n2,
            )
            xf[v] = new.reshape(n2, MEMBERS, COLS)
            high, low = split(new)
            both = jnp.concatenate([high, low], axis=1)
            for i in range(SIDE):
                n = min(3, ROWS - 3 * i) * MEMBERS
                xft[pl.ds((v * SIDE + i) * COLS, COLS), 0:n] = dot(
                    unit[...], both[i * 3 * MEMBERS : i * 3 * MEMBERS + n, :], ((1,), (1,))
                )

    to_scalar.wait()
    for b in range(NB):

        @pl.loop(0, BLOCK // 8)
        def _(g):
            for j in range(8):
                k = g * 8 + j
                at = desc_s[b // PER, (b % PER) * BLOCK + k]
                yo[b, pl.ds(k, 1), :] = xft[pl.ds(at, 1), :]

    for b in range(NB):
        cut = (slice(b // PER, b // PER + 1), slice((b % PER) * BLOCK, (b % PER + 1) * BLOCK))
        turned = yo[b].T
        at = jnp.broadcast_to(jnp.where(owned[cut], part_of[cut], -1), (MEMBERS, BLOCK))
        mine = jnp.zeros((MEMBERS, BLOCK), F32)
        for i in range(3):
            mine = jnp.where(at == i, turned[i * MEMBERS : (i + 1) * MEMBERS, :], mine)
        part[b] = mine

    first = [
        remote(part.at[place(o, 0)[0]], got_a.at[o - 1], send.at[o - 1], recv_a.at[o - 1], o, 0)
        for o in range(1, nlat)
    ]
    for c in first:
        c.start()
    lat_f, lon_f = by_block(lat_ref).astype(F32), by_block(lon_ref).astype(F32)
    lat0f, lon0f = (me_lat * ROWS).astype(F32), (me_lon * COLS).astype(F32)
    reach_tables(lat_f, lon_f, lat0f, lon0f, rank_ref, t0_ref)
    total = part[me_lat]
    for i, c in enumerate(first):
        c.wait_recv()
        total = total + got_a[i]
    line[...] = total
    second = [
        remote(line, got_b.at[o - 1], send.at[nlat + o - 2], recv_b.at[o - 1], 0, o)
        for o in range(1, nlon)
    ]
    for c in second:
        c.start()
    pair_tables(lat_f, lon_f, pair_ref)
    for i, c in enumerate(second):
        c.wait_recv()
        total = total + got_b[i]
    block_sum[...] = total
    third = [
        remote(block_sum, out.at[me_lat], send.at[nlat + nlon + o - 3], recv_c.at[o - 1], o, 0)
        for o in range(1, nlat)
    ]
    for c in third:
        c.start()
    out[me_lat] = total
    for c in third:
        c.wait_recv()

    for c in winds + edges + corners + first + second + third:
        c.wait_send()

    sent_rows(3)
    sent_rows(4)


def forecast(x, wind, lat, lon, var, nlat, nlon):
    vm = pl.BlockSpec(memory_space=pltpu.VMEM)
    dma = pltpu.SemaphoreType.DMA
    return pl.pallas_call(
        lambda *refs: forecast_kernel(nlat, nlon, *refs),
        out_shape=(
            jax.ShapeDtypeStruct((NVAR, ROWS, MEMBERS, COLS), F32),
            jax.ShapeDtypeStruct((NB, MEMBERS, BLOCK), F32),
            jax.ShapeDtypeStruct((NB, BLOCK), F32),
            jax.ShapeDtypeStruct((NB, KC, ROWS * COLS), F32),
            jax.ShapeDtypeStruct((NB * (NB - 1) // 2, BLOCK, BLOCK), F32),
        ),
        in_specs=[pl.BlockSpec(memory_space=pltpu.HBM)] * 5,
        out_specs=(vm,) * 5,
        scratch_shapes=[
            pltpu.VMEM((MEMBERS, NVAR, ROWS, COLS), F32),
            pltpu.VMEM((2, ROWS, COLS), F32),
            pltpu.VMEM((GROUPS, OBS), jnp.int32),
            pltpu.VMEM((GROUPS, OBS), jnp.int32),
            pltpu.VMEM((GROUPS, OBS), jnp.int32),
            pltpu.VMEM((GROUPS, OBS), jnp.int32),
            pltpu.SMEM((GROUPS, OBS), jnp.int32),
            pltpu.VMEM((NVAR * SIDE * COLS, COLS), F32),
            pltpu.VMEM((NB, BLOCK, COLS), F32),
            pltpu.VMEM((NB, MEMBERS, BLOCK), F32),
            pltpu.VMEM((MEMBERS, BLOCK), F32),
            pltpu.VMEM((MEMBERS, BLOCK), F32),
            pltpu.VMEM((nlat - 1, MEMBERS, BLOCK), F32),
            pltpu.VMEM((nlon - 1, MEMBERS, BLOCK), F32),
            pltpu.VMEM((NVAR, ROWS + 4, MEMBERS, COLS), F32),
            pltpu.VMEM((ROWS, MEMBERS, COLS), F32),
            pltpu.VMEM((ROWS, MEMBERS, COLS), F32),
            pltpu.VMEM((ROWS, MEMBERS, COLS), F32),
            pltpu.VMEM((4, MEMBERS, COLS), F32),
            pltpu.VMEM((4, 2, ROWS, COLS), F32),
            pltpu.VMEM((ROWS + 2, MEMBERS, COLS), F32),
            pltpu.VMEM((ROWS + 2, MEMBERS, 2 * COLS), BF),
            pltpu.VMEM((ROWS, MEMBERS, 2 * COLS), BF),
            pltpu.VMEM((4, ROWS + 2, 8, COLS), F32),
            pltpu.VMEM((2 * COLS, 2 * COLS), BF),
            pltpu.VMEM((COLS, 2 * COLS), BF),
            pltpu.VMEM((VS, ROWS + 2, MEMBERS, COLS), F32),
            dma((NVG, 2)), dma((NVG, 2)), dma((2,)), dma((2,)),
            dma((4,)), dma((4,)), dma((4,)), dma((4,)),
            dma((2 * nlat + nlon - 3,)), dma((nlat - 1,)), dma((nlon - 1,)), dma((nlat - 1,)),
            dma((NVG,)), dma((5,)),
        ],
        compiler_params=pltpu.CompilerParams(
            collective_id=0, has_side_effects=True, vmem_limit_bytes=30 << 20
        ),
        name="forecast",
    )(x, wind, lat, lon, var)


def analysis_kernel(
    x_ref, y_ref, rank_ref, t0_ref, pair_ref, lat_hbm, lon_hbm, val_hbm, err_hbm,
    out_hbm,
    lat_ref, lon_ref, val_ref, err_ref, ob,
    ys, a_all, s_all, a_pk, b_pk, l_pk, a_more, b_more, t_more, xv, rhs, p2, q3, nch,
    l_small, l_out,
):
    small = [
        pltpu.make_async_copy(a, b, l_small.at[i])
        for i, (a, b) in enumerate(
            [(lat_hbm, lat_ref), (lon_hbm, lon_ref), (val_hbm, val_ref), (err_hbm, err_ref)]
        )
    ]
    for c in small:
        c.start()
    out_rows = ob.reshape(MEMBERS * NVAR * ROWS, COLS)

    def store(g):
        vs = pl.ds(g * VG, VG)
        return pltpu.make_async_copy(ob.at[:, vs], out_hbm.at[:, vs], l_out.at[g])

    rank = rank_ref[...]
    for b in range(NB):
        top = jnp.max(rank[b : b + 1, :])
        nch[b] = ((top + KC) * (1.0 / KC)).astype(jnp.int32)
        ys[:, b * BLOCK : (b + 1) * BLOCK] = y_ref[b]
    for c in small:
        c.wait()
    lat, lon = by_block(lat_ref).astype(F32), by_block(lon_ref).astype(F32)
    values, variances = by_block(val_ref), by_block(err_ref)
    row_id = lax.broadcasted_iota(jnp.int32, (KC, BLOCK), 0).astype(F32)
    lane96 = lax.broadcasted_iota(jnp.int32, (KC, 3 * KC), 1)
    zero8 = jnp.zeros((8, BLOCK), F32)

    def packed(pick, b):
        zero = jnp.zeros_like(pick)
        pick3 = jnp.concatenate(
            [
                jnp.concatenate([pick, zero], axis=1),
                jnp.concatenate([zero, pick], axis=1),
                jnp.concatenate([pick, zero], axis=1),
            ],
            axis=0,
        )
        return dot(pick, a_all[b]).astype(BF), dot(s_all[b], pick3, ((1,), (1,))).astype(BF)

    stacked = None
    for b in range(NB):
        prior = ys[:, b * BLOCK : (b + 1) * BLOCK]
        average = jnp.sum(prior, axis=0, keepdims=True) * (1.0 / MEMBERS)
        anomaly = prior - average
        spread = jnp.sum(anomaly * anomaly, axis=0, keepdims=True) / (MEMBERS - 1)
        errors = variances[b : b + 1, :]
        total = spread + errors
        weights = anomaly * (1.0 / ((MEMBERS - 1) * total))
        shifts = (values[b : b + 1, :] - average) - anomaly * (
            1.0 / (1.0 + jnp.sqrt(errors / total))
        )
        wh = hi(weights)
        a = jnp.concatenate([wh, weights - wh, wh, zero8], axis=0).T.astype(BF)
        sh, sl = split(shifts)
        a_all[b] = a
        s_all[b] = jnp.concatenate([sh, sl], axis=1)
        s3 = jnp.concatenate([sh, sl, sh], axis=1)
        for j in range(b + 1, NB):
            yl = ys[:, j * BLOCK : (j + 1) * BLOCK]
            yh = hi(yl)
            y3 = jnp.concatenate([yh, yh, yl - yh, zero8], axis=0).astype(BF)
            qh, ql = split(dot(a, y3) * pair_ref[pair_at(b, j)])
            ys[:, j * BLOCK : (j + 1) * BLOCK] = yl + dot(
                s3, jnp.concatenate([qh, qh, ql], axis=0)
            )
        pick = (row_id == rank[b : b + 1, :]).astype(BF)
        a_pk[b], b_pk[b] = packed(pick, b)
        if b % 2 == 0:
            sh32 = sh.astype(F32)
            s_rows = jnp.concatenate([sh32, sh32, sl.astype(F32), zero8], axis=0).astype(BF)
            stacked = dot(s_rows, jnp.concatenate([pick] * 3, axis=0), ((1,), (1,))).astype(BF)
        else:
            c = dot(a_pk[b], stacked)
            ch = hi(c)
            c3 = jnp.where((lane96 >= KC) & (lane96 < 2 * KC), c - ch, ch)
            l_pk[b // 2] = jnp.concatenate([c3, b_pk[b - 1].astype(F32)], axis=0).astype(BF)

    lat0f = (lax.axis_index("lat") * ROWS).astype(F32)
    lon0f = (lax.axis_index("lon") * COLS).astype(F32)
    for b in range(NB):

        @pl.loop(1, nch[b])
        def _(c):
            slot = b * (NCH - 1) + c - 1
            pick = (row_id + (c * KC).astype(F32) == rank[b : b + 1, :]).astype(F32)
            a_more[slot], b_more[slot] = packed(pick.astype(BF), b)
            cell_tapers(pick, lat[b : b + 1, :], lon[b : b + 1, :], lat0f, lon0f, t_more, slot)

    zero_cols = jnp.zeros((8, ROWS * COLS), F32)

    def stack_x(i):
        x = xv[i]
        xh = hi(x)
        rhs[i] = jnp.concatenate([xh, xh, x - xh, zero_cols], axis=0).astype(BF)

    def put_q(i, q):
        qh, ql = split(q)
        q3[i] = jnp.concatenate([qh, qh, ql], axis=0)

    def add_chunk(a, s3, t):
        for i in range(VG):
            put_q(i, dot(a, rhs[i]) * t[...])
        for i in range(VG):
            xv[i] += dot(s3, q3[i])

    @pl.loop(0, NVAR // VG)
    def _(g):
        for i in range(VG):
            for r in range(ROWS):
                xv[i, :, r * COLS : (r + 1) * COLS] = x_ref[g * VG + i, r]

        @pl.loop(0, NB // 2)
        def _(pair):
            b = 2 * pair
            few = jnp.maximum(nch[b], nch[b + 1]) <= 1

            @pl.when(few)
            def _():
                a2 = a_pk[pl.ds(b, 2)].reshape(2 * KC, 128)
                for i in range(VG):
                    stack_x(i)
                for i in range(VG):
                    p = dot(a2, rhs[i])
                    p2[i] = p[KC:]
                    put_q(i, p[:KC] * t0_ref[b])
                for i in range(VG):
                    r = dot(l_pk[pair], q3[i])
                    xv[i] += r[KC:]
                    put_q(i, (p2[i] + r[:KC]) * t0_ref[b + 1])
                for i in range(VG):
                    xv[i] += dot(b_pk[b + 1], q3[i])

            @pl.when(jnp.logical_not(few))
            def _():
                @pl.loop(b, b + 2)
                def _(bb):
                    for i in range(VG):
                        stack_x(i)
                    add_chunk(a_pk[bb], b_pk[bb], t0_ref.at[bb])

                    @pl.loop(1, nch[bb])
                    def _(c):
                        slot = bb * (NCH - 1) + c - 1
                        add_chunk(a_more[slot], b_more[slot], t_more.at[slot])

        for i in range(VG):
            for r in range(ROWS):
                out_rows[
                    pl.ds((g * VG + i) * ROWS + r, MEMBERS, stride=NVAR * ROWS), :
                ] = xv[i, :, r * COLS : (r + 1) * COLS]
        store(g).start()

    for g in range(NVAR // VG):
        store(g).wait()


def analysis(x, y, rank, t0, pairs, lat, lon, val, err):
    vm = pl.BlockSpec(memory_space=pltpu.VMEM)
    hbm = pl.BlockSpec(memory_space=pltpu.HBM)
    more = NB * (NCH - 1)
    dma = pltpu.SemaphoreType.DMA
    return pl.pallas_call(
        analysis_kernel,
        out_shape=jax.ShapeDtypeStruct((MEMBERS, NVAR, ROWS, COLS), F32),
        in_specs=[vm] * 5 + [hbm] * 4,
        out_specs=hbm,
        scratch_shapes=[
            pltpu.VMEM((GROUPS, OBS), jnp.int32),
            pltpu.VMEM((GROUPS, OBS), jnp.int32),
            pltpu.VMEM((GROUPS, OBS), F32),
            pltpu.VMEM((GROUPS, OBS), F32),
            pltpu.VMEM((MEMBERS, NVAR, ROWS, COLS), F32),
            pltpu.VMEM((MEMBERS, NB * BLOCK), F32),
            pltpu.VMEM((NB, BLOCK, 128), BF),
            pltpu.VMEM((NB, MEMBERS, 256), BF),
            pltpu.VMEM((NB, KC, 128), BF),
            pltpu.VMEM((NB, MEMBERS, 3 * KC), BF),
            pltpu.VMEM((NB // 2, KC + MEMBERS, 3 * KC), BF),
            pltpu.VMEM((more, KC, 128), BF),
            pltpu.VMEM((more, MEMBERS, 3 * KC), BF),
            pltpu.VMEM((more, KC, ROWS * COLS), F32),
            pltpu.VMEM((VG, MEMBERS, ROWS * COLS), F32),
            pltpu.VMEM((VG, 128, ROWS * COLS), BF),
            pltpu.VMEM((VG, KC, ROWS * COLS), F32),
            pltpu.VMEM((VG, 3 * KC, ROWS * COLS), BF),
            pltpu.SMEM((NB,), jnp.int32),
            dma((4,)), dma((NVAR // VG,)),
        ],
        compiler_params=pltpu.CompilerParams(vmem_limit_bytes=22 << 20),
        name="analysis",
    )(x, y, rank, t0, pairs, lat, lon, val, err)


def solution(mesh):
    nlat, nlon = mesh.shape["lat"], mesh.shape["lon"]

    def body(prognostic_samples, wind, obs_lat, obs_lon, obs_var, obs_value, obs_error):
        hbm = [
            pltpu.with_memory_space_constraint(a, pltpu.HBM)
            for a in (prognostic_samples, wind, obs_lat, obs_lon, obs_var, obs_value, obs_error)
        ]
        xf, y, rank, t0, pairs = forecast(*hbm[:5], nlat, nlon)
        return analysis(xf, y, rank, t0, pairs, hbm[2], hbm[3], hbm[5], hbm[6])

    in_specs = (P(None, None, "lat", "lon"), P(None, "lat", "lon"), P(), P(), P(), P(), P())
    out_specs = P(None, None, "lat", "lon")
    return jax.shard_map(body, mesh=mesh, in_specs=in_specs, out_specs=out_specs, check_vma=False)
```

```python
import jax
import jax.numpy as jnp
from jax import lax
from jax.experimental import pallas as pl
from jax.experimental.pallas import tpu as pltpu
from jax.sharding import PartitionSpec as P

MEMBERS, NVAR, ROWS, COLS = 40, 25, 8, 128
NLON = 2048
GROUPS, OBS = 2, 512
NB, BLOCK = 8, 128
PER = OBS // BLOCK
LOC = 32.0
DIFFUSE = 0.1
VS = 5
NVG = NVAR // VS
MG = MEMBERS // 8
SIDE = (ROWS + 2) // 3
PIECE = 24
KC = 32
NCH = BLOCK // KC
VG = 5
F32, BF = jnp.float32, jnp.bfloat16
MESH = pl.DeviceIdType.MESH


def hi(x):
    return x.astype(BF).astype(F32)


def split(x):
    high = x.astype(BF)
    return high, (x - high.astype(F32)).astype(BF)


def dot(a, b, dims=((1,), (0,))):
    return lax.dot_general(a, b, (dims, ((), ())), preferred_element_type=F32)


def peers(nlat, nlon):
    me_lat = lax.axis_index("lat")
    me_lon = lax.axis_index("lon")

    def place(dlat, dlon):
        lat = lax.rem(me_lat + (dlat + nlat), nlat) if dlat else me_lat
        lon = lax.rem(me_lon + (dlon + nlon), nlon) if dlon else me_lon
        return lat, lon

    def remote(src, dst, ssem, rsem, dlat, dlon):
        return pltpu.make_async_remote_copy(
            src_ref=src,
            dst_ref=dst,
            send_sem=ssem,
            recv_sem=rsem,
            device_id=place(dlat, dlon),
            device_id_type=MESH,
        )

    def signal(barrier, offsets):
        for o in offsets:
            pl.semaphore_signal(barrier, inc=1, device_id=place(*o), device_id_type=MESH)

    return me_lat, me_lon, place, remote, signal


def taper_sq(d2):
    z = jnp.sqrt(d2) * (1.0 / LOC)
    inner = (((-0.25 * z + 0.5) * z + 0.625) * z - 5.0 / 3.0) * z * z + 1.0
    outer = (
        ((((z * (1.0 / 12.0) - 0.5) * z + 0.625) * z + 5.0 / 3.0) * z - 5.0) * z
        + 4.0
        - (2.0 / 3.0) / jnp.maximum(z, 1.0)
    )
    return jnp.where(z <= 1.0, inner, jnp.where(z < 2.0, outer, 0.0))


def by_block(ref):
    parts = []
    for b in range(NB):
        first = (b % PER) * BLOCK
        parts.append(ref[b // PER : b // PER + 1, first : first + BLOCK])
    return jnp.concatenate(parts, axis=0)


def pair_at(b, j):
    return b * (2 * NB - b - 1) // 2 + j - b - 1


def cell_tapers(pick, lat_row, lon_row, lat0f, lon0f, out, slot):
    col_f = lax.broadcasted_iota(jnp.int32, (KC, COLS), 1).astype(F32) + lon0f
    latc = jnp.sum(pick * lat_row, axis=1, keepdims=True)
    lonc = jnp.sum(pick * lon_row, axis=1, keepdims=True)
    dlon = jnp.abs(lonc - col_f)
    dlon = jnp.minimum(dlon, NLON - dlon)
    dlon = dlon * dlon
    for r in range(ROWS):
        dlat = latc - (lat0f + float(r))
        out[slot, :, r * COLS : (r + 1) * COLS] = taper_sq(dlon + dlat * dlat)


def reach_tables(lat, lon, lat0f, lon0f, rank_ref, t0_ref):
    dy = jnp.maximum(jnp.maximum(lat0f - lat, lat - (lat0f + (ROWS - 1))), 0.0)
    off = lon - lon0f
    off = jnp.where(off < 0, off + NLON, off)
    dx = jnp.maximum(jnp.minimum(off - (COLS - 1), NLON - off), 0.0)
    reach = dx * dx + dy * dy < 4.0 * LOC * LOC
    before = (
        lax.broadcasted_iota(jnp.int32, (BLOCK, BLOCK), 0)
        < lax.broadcasted_iota(jnp.int32, (BLOCK, BLOCK), 1)
    ).astype(F32)
    rank = jnp.where(reach, dot(reach.astype(F32).astype(BF), before.astype(BF)), -1.0)
    rank_ref[...] = rank
    row_id = lax.broadcasted_iota(jnp.int32, (KC, BLOCK), 0).astype(F32)
    for b in range(NB):
        pick = (row_id == rank[b : b + 1, :]).astype(F32)
        cell_tapers(pick, lat[b : b + 1, :], lon[b : b + 1, :], lat0f, lon0f, t0_ref, b)


def pair_tables(lat, lon, pair_ref):
    lat_t, lon_t = lat.T, lon.T
    for b in range(NB):
        for j in range(b + 1, NB):
            dlat = lat_t[:, b : b + 1] - lat[j : j + 1, :]
            dlon = jnp.abs(lon_t[:, b : b + 1] - lon[j : j + 1, :])
            dlon = jnp.minimum(dlon, NLON - dlon)
            pair_ref[pair_at(b, j)] = taper_sq(dlat * dlat + dlon * dlon)


def forecast_kernel(
    nlat, nlon,
    x_hbm, wind_hbm, lat_hbm, lon_hbm, var_hbm,
    xf, out, rank_ref, t0_ref, pair_ref,
    xb, wind_ref, lat_ref, lon_ref, var_ref, desc, desc_s, xft, yo, part, line, block_sum, got_a, got_b,
    xt, edge, edge_w, edge_e, corner, wind_n, halo, halo_s, halo1_s, coef, shift, unit, q1_s, to_edge, at8,
    s_row, r_row, s_edge, r_edge, s_corner, r_corner, s_wind, r_wind,
    send, send_a, recv_a, recv_b, recv_c, l_x, l_small,
):
    def fetch(vg):
        vs = pl.ds(vg * VS, VS)
        return pltpu.make_async_copy(x_hbm.at[:, vs], xb.at[:, vs], l_x.at[vg])

    small = [
        pltpu.make_async_copy(a, b, l_small.at[i])
        for i, (a, b) in enumerate(
            [(wind_hbm, wind_ref), (lat_hbm, lat_ref), (lon_hbm, lon_ref), (var_hbm, var_ref)]
        )
    ]
    for vg in range(NVG):
        fetch(vg).start()
    for c in small:
        c.start()
    x_ref = xb.reshape(MEMBERS * NVAR * ROWS, COLS)
    me_lat, me_lon, place, remote, signal = peers(nlat, nlon)
    barrier = pltpu.get_barrier_semaphore()
    near = [(o, 0) for o in range(1, nlat)] + [(0, o) for o in range(1, nlon)]
    near += [(-1, -1), (-1, 1), (1, -1), (1, 1)]
    signal(barrier, near)

    def column(r, mg, v):
        return x_ref[pl.ds(mg * (8 * NVAR * ROWS) + v * ROWS + r, 8, stride=NVAR * ROWS), :]

    def rows(vg, up):
        vs = pl.ds(vg * VS, VS)
        if up:
            return remote(
                xt.at[vs, 2:4],
                xt.at[vs, ROWS + 2 : ROWS + 4],
                s_row.at[vg, 0], r_row.at[vg, 0], -1, 0,
            )
        return remote(
            xt.at[vs, ROWS : ROWS + 2], xt.at[vs, 0:2], s_row.at[vg, 1], r_row.at[vg, 1], 1, 0
        )

    def send_rows(vg):
        rows(vg, True).start()
        rows(vg, False).start()

    def sent_rows(vg):
        rows(vg, True).wait_send()
        rows(vg, False).wait_send()

    winds = [
        remote(wind_ref, wind_n.at[i], s_wind.at[i], r_wind.at[i], dlat, dlon)
        for i, (dlat, dlon) in enumerate([(1, 0), (-1, 0), (0, 1), (0, -1)])
    ]
    edges = [
        remote(edge, edge_w, s_edge.at[0], r_edge.at[0], 0, 1),
        remote(edge, edge_e, s_edge.at[1], r_edge.at[1], 0, -1),
    ]
    corners = [
        remote(edge.at[ROWS - 1], corner.at[0], s_corner.at[0], r_corner.at[0], 1, 1),
        remote(edge.at[ROWS - 1], corner.at[1], s_corner.at[1], r_corner.at[1], 1, -1),
        remote(edge.at[0], corner.at[2], s_corner.at[2], r_corner.at[2], -1, 1),
        remote(edge.at[0], corner.at[3], s_corner.at[3], r_corner.at[3], -1, -1),
    ]
    edge_src = lax.rem(lax.broadcasted_iota(jnp.int32, (2 * COLS, COLS), 0), COLS)
    edge_dst = lax.broadcasted_iota(jnp.int32, (2 * COLS, COLS), 1)
    outer = (edge_src < 2) | (edge_src >= COLS - 2)
    moved = jnp.where(outer, (edge_dst - edge_src) & (COLS - 1), -1)

    @pl.loop(0, NVG)
    def _(vg):
        for vi in range(VS):
            to_edge[vg, vi * 2 * COLS : (vi + 1) * 2 * COLS, :] = jnp.where(
                moved == 4 * (vg * VS + vi), 1.0, 0.0
            ).astype(BF)

    for vg in range(NVG):
        fetch(vg).wait()

        @pl.loop(vg * VS, (vg + 1) * VS)
        def _(v):
            for r in (0, 1, ROWS - 2, ROWS - 1):
                for mg in range(MG):
                    xt[v, r + 2, mg * 8 : (mg + 1) * 8, :] = column(r, mg, v)

        if vg == 0:
            for c in small:
                c.wait()
            pl.semaphore_wait(barrier, len(near))
            for w in winds:
                w.start()
        if vg < 2:
            send_rows(vg)

    edge[...] = jnp.zeros_like(edge)

    @pl.loop(0, NVG)
    def _(vg):
        pieces = []
        for vi in range(VS):
            v = vg * VS + vi
            for r in range(2, ROWS - 2):
                for mg in range(MG):
                    xt[v, r + 2, mg * 8 : (mg + 1) * 8, :] = column(r, mg, v)
        for vi in range(VS):
            pieces += split(xt[vg * VS + vi, 2 : ROWS + 2].reshape(ROWS * MEMBERS, COLS))
        packed = dot(jnp.concatenate(pieces, axis=1), to_edge[vg])
        edge[...] += packed.reshape(ROWS, MEMBERS, COLS)

    for e in edges + corners:
        e.start()
    sent_rows(0)
    send_rows(2)

    lat_all, lon_all = lat_ref[...], lon_ref[...]
    owned = (lat_all // ROWS == me_lat) & (lon_all // COLS == me_lon)
    row_all = lat_all & (ROWS - 1)
    group = (row_all >= 3).astype(jnp.int32) + (row_all >= 6).astype(jnp.int32)
    part_of = row_all - 3 * group
    desc[...] = (var_ref[...] * SIDE + group) * COLS + (lon_all & (COLS - 1))
    to_scalar = pltpu.make_async_copy(desc, desc_s, l_small.at[4])
    to_scalar.start()
    at_all = jnp.where(owned, part_of, -1)
    for b in range(NB):
        cut = (b % PER) * BLOCK
        at8[b : b + 1, :] = at_all[b // PER : b // PER + 1, cut : cut + BLOCK]

    src = lax.rem(lax.broadcasted_iota(jnp.int32, (2 * COLS, 2 * COLS), 0), COLS)
    dst = lax.broadcasted_iota(jnp.int32, (2 * COLS, 2 * COLS), 1)
    east_of = (dst < COLS) & (src == dst + 1)
    west_of = (dst >= COLS) & (src == dst - COLS - 1)
    shift[...] = jnp.where(east_of | west_of, 1.0, 0.0).astype(BF)
    col_of = lax.rem(lax.broadcasted_iota(jnp.int32, (COLS, 2 * COLS), 1), COLS)
    row_of = lax.broadcasted_iota(jnp.int32, (COLS, 2 * COLS), 0)
    unit[...] = jnp.where(col_of == row_of, 1.0, 0.0).astype(BF)

    for w in winds:
        w.wait_recv()
    has_lo = (me_lat > 0).astype(F32)
    has_hi = (me_lat < nlat - 1).astype(F32)

    def row_wind(r):
        if r < 0:
            return wind_n[0, 0, ROWS - 1 : ROWS, :], wind_n[0, 1, ROWS - 1 : ROWS, :]
        if r == ROWS:
            return wind_n[1, 0, 0:1, :], wind_n[1, 1, 0:1, :]
        return wind_ref[0, r : r + 1, :], wind_ref[1, r : r + 1, :]

    def four(u, v, r):
        nxt, prv = DIFFUSE - 0.5 * v, DIFFUSE + 0.5 * v
        if r == 0:
            prv = prv * has_lo
        if r == ROWS - 1:
            nxt = nxt * has_hi
        return DIFFUSE - 0.5 * u, DIFFUSE + 0.5 * u, nxt, prv

    for r in range(-1, ROWS + 1):
        u, v = row_wind(r)
        for i, c in enumerate(four(u, v, r)):
            coef[i, r + 1] = jnp.broadcast_to(c, (8, COLS))

    sent_rows(1)
    send_rows(3)

    for e in edges + corners:
        e.wait_recv()
    lane4 = lax.rem(lax.broadcasted_iota(jnp.int32, (MEMBERS, COLS), 1), 4)
    from_west = lane4 >= 2
    halo[0] = jnp.where(from_west, corner[0], corner[1])
    halo[ROWS + 1] = jnp.where(from_west, corner[2], corner[3])
    for r in range(ROWS):
        halo[r + 1] = jnp.where(from_west, edge_w[r], edge_e[r])

    def beside(t):
        return jnp.where(lane4 == 0, t, pltpu.roll(t, 2, 1))

    for r in range(ROWS + 2):
        halo_s[r] = beside(halo[r])
    for r in range(ROWS):
        u, v = [
            jnp.where(
                from_west,
                jnp.broadcast_to(wind_n[2, i, r : r + 1, COLS - 1 : COLS], (MEMBERS, COLS)),
                jnp.broadcast_to(wind_n[3, i, r : r + 1, 0:1], (MEMBERS, COLS)),
            )
            for i in range(2)
        ]
        ce, cw, cn, cs = four(u, v, r)
        own, got = edge[r], halo[r + 1]
        east = pltpu.roll(jnp.where(lane4 == 0, own, got), COLS - 1, 1)
        west = pltpu.roll(jnp.where(lane4 == 3, own, got), 1, 1)
        after = (
            (1.0 - 4.0 * DIFFUSE) * got
            + ce * east
            + cw * west
            + cn * halo[r + 2]
            + cs * halo[r]
        )
        halo1_s[r] = beside(after)

    def step(q, nxt, prv, side, back, first, count):
        shape = (count, MG, 8, COLS)
        high, low = split(q)
        both = dot(jnp.concatenate([high, low], axis=1), shift[...])
        lane = lax.broadcasted_iota(jnp.int32, (count * MEMBERS, COLS), 1)
        beyond = pltpu.roll(side.reshape(count * MEMBERS, COLS), back, 1)
        east = jnp.where(lane == COLS - 1, beyond, both[:, :COLS])
        west = jnp.where(lane == 0, beyond, both[:, COLS:])
        c = [coef[i, first : first + count].reshape(count, 1, 8, COLS) for i in range(4)]
        new = (
            (1.0 - 4.0 * DIFFUSE) * q.reshape(shape)
            + c[0] * east.reshape(shape)
            + c[1] * west.reshape(shape)
            + c[2] * nxt.reshape(shape)
            + c[3] * prv.reshape(shape)
        )
        return new.reshape(count * MEMBERS, COLS)

    def block(ref, v, first, count):
        return ref[v, first : first + count].reshape(count * MEMBERS, COLS)

    @pl.loop(0, NVG)
    def _(vg):
        rows(vg, True).wait_recv()
        rows(vg, False).wait_recv()

        @pl.when(vg == 0)
        def _():
            sent_rows(2)
            send_rows(4)

        n1, n2 = ROWS + 2, ROWS
        for vi in range(VS):
            v = vg * VS + vi
            q1_s[vi] = step(
                block(xt, v, 1, n1), block(xt, v, 2, n1), block(xt, v, 0, n1),
                halo_s[...], (COLS - 1 - 4 * v) & (COLS - 1), 0, n1,
            ).reshape(n1, MEMBERS, COLS)
        for vi in range(VS):
            v = vg * VS + vi
            new = step(
                block(q1_s, vi, 1, n2), block(q1_s, vi, 2, n2), block(q1_s, vi, 0, n2),
                halo1_s[...], (COLS - 1 - 4 * v) & (COLS - 1), 1, n2,
            )
            xf[v] = new.reshape(n2, MEMBERS, COLS)
            high, low = split(new)
            both = jnp.concatenate([high, low], axis=1)
            for i in range(SIDE):
                n = min(3, ROWS - 3 * i) * MEMBERS
                xft[pl.ds((v * SIDE + i) * COLS, COLS), 0:n] = dot(
                    unit[...], both[i * 3 * MEMBERS : i * 3 * MEMBERS + n, :], ((1,), (1,))
                )

    to_scalar.wait()
    half, odd = me_lon // 2, lax.rem(me_lon, 2)

    def piece(i, h, b):
        return pltpu.make_async_remote_copy(
            src_ref=part.at[2 * b + h],
            dst_ref=got_a.at[i, odd],
            send_sem=send_a.at[i, h],
            recv_sem=recv_a.at[i, odd],
            device_id=(me_lat, 2 * b + h),
            device_id_type=MESH,
        )

    def arrival(i, p):
        return pltpu.make_async_remote_copy(
            src_ref=part.at[0],
            dst_ref=got_a.at[i, p],
            send_sem=send_a.at[i, 0],
            recv_sem=recv_a.at[i, p],
            device_id=(me_lat, lax.rem(me_lon + 1, nlon)),
            device_id_type=MESH,
        )

    first = []
    for i in list(range(1, NB)) + [0]:
        b = lax.rem(half + i, NB)

        @pl.loop(0, BLOCK // 8)
        def _(g):
            for j in range(8):
                k = g * 8 + j
                at = desc_s[b // PER, lax.rem(b, PER) * BLOCK + k]
                yo[i, pl.ds(k, 1), :] = xft[pl.ds(at, 1), :]

        turned = yo[i].T
        at = jnp.broadcast_to(at8[pl.ds(b, 1), :], (MEMBERS, BLOCK))
        mine = jnp.zeros((MEMBERS, BLOCK), F32)
        for n in range(3):
            mine = jnp.where(at == n, turned[n * MEMBERS : (n + 1) * MEMBERS, :], mine)
        part[2 * b] = mine[0:PIECE]
        part[2 * b + 1] = jnp.concatenate(
            [mine[PIECE:], jnp.zeros((2 * PIECE - MEMBERS, BLOCK), F32)], axis=0
        )
        for h in (0, 1) if i else (1 - odd,):
            c = piece(i, h, b)
            c.start()
            first.append(c)
    lat_f, lon_f = by_block(lat_ref).astype(F32), by_block(lon_ref).astype(F32)
    lat0f, lon0f = (me_lat * ROWS).astype(F32), (me_lon * COLS).astype(F32)
    reach_tables(lat_f, lon_f, lat0f, lon0f, rank_ref, t0_ref)
    total = part[me_lon]
    for i in range(1, NB):
        for p in (0, 1):
            arrival(i, p).wait_recv()
            total = total + got_a[i, p]
    arrival(0, 1 - odd).wait_recv()
    total = total + got_a[0, 1 - odd]
    line[...] = total
    second = [
        remote(line, got_b.at[o - 1], send.at[o - 1], recv_b.at[o - 1], o, 0)
        for o in range(1, nlat)
    ]
    for c in second:
        c.start()
    for i, c in enumerate(second):
        c.wait_recv()
        total = total + got_b[i]
    block_sum[...] = total
    third = [
        remote(block_sum, out.at[me_lon], send.at[nlat + o - 2], recv_c.at[o - 1], 0, o)
        for o in range(1, nlon)
    ]
    for c in third:
        c.start()
    out[me_lon] = total
    pair_tables(lat_f, lon_f, pair_ref)
    for c in third:
        c.wait_recv()

    for c in winds + edges + corners + first + second + third:
        c.wait_send()

    sent_rows(3)
    sent_rows(4)


def forecast(x, wind, lat, lon, var, nlat, nlon):
    vm = pl.BlockSpec(memory_space=pltpu.VMEM)
    dma = pltpu.SemaphoreType.DMA
    return pl.pallas_call(
        lambda *refs: forecast_kernel(nlat, nlon, *refs),
        out_shape=(
            jax.ShapeDtypeStruct((NVAR, ROWS, MEMBERS, COLS), F32),
            jax.ShapeDtypeStruct((2 * NB, PIECE, BLOCK), F32),
            jax.ShapeDtypeStruct((NB, BLOCK), F32),
            jax.ShapeDtypeStruct((NB, KC, ROWS * COLS), F32),
            jax.ShapeDtypeStruct((NB * (NB - 1) // 2, BLOCK, BLOCK), F32),
        ),
        in_specs=[pl.BlockSpec(memory_space=pltpu.HBM)] * 5,
        out_specs=(vm,) * 5,
        scratch_shapes=[
            pltpu.VMEM((MEMBERS, NVAR, ROWS, COLS), F32),
            pltpu.VMEM((2, ROWS, COLS), F32),
            pltpu.VMEM((GROUPS, OBS), jnp.int32),
            pltpu.VMEM((GROUPS, OBS), jnp.int32),
            pltpu.VMEM((GROUPS, OBS), jnp.int32),
            pltpu.VMEM((GROUPS, OBS), jnp.int32),
            pltpu.SMEM((GROUPS, OBS), jnp.int32),
            pltpu.VMEM((NVAR * SIDE * COLS, COLS), F32),
            pltpu.VMEM((NB, BLOCK, COLS), F32),
            pltpu.VMEM((2 * NB, PIECE, BLOCK), F32),
            pltpu.VMEM((PIECE, BLOCK), F32),
            pltpu.VMEM((PIECE, BLOCK), F32),
            pltpu.VMEM((NB, 2, PIECE, BLOCK), F32),
            pltpu.VMEM((nlat - 1, PIECE, BLOCK), F32),
            pltpu.VMEM((NVAR, ROWS + 4, MEMBERS, COLS), F32),
            pltpu.VMEM((ROWS, MEMBERS, COLS), F32),
            pltpu.VMEM((ROWS, MEMBERS, COLS), F32),
            pltpu.VMEM((ROWS, MEMBERS, COLS), F32),
            pltpu.VMEM((4, MEMBERS, COLS), F32),
            pltpu.VMEM((4, 2, ROWS, COLS), F32),
            pltpu.VMEM((ROWS + 2, MEMBERS, COLS), F32),
            pltpu.VMEM((ROWS + 2, MEMBERS, COLS), F32),
            pltpu.VMEM((ROWS, MEMBERS, COLS), F32),
            pltpu.VMEM((4, ROWS + 2, 8, COLS), F32),
            pltpu.VMEM((2 * COLS, 2 * COLS), BF),
            pltpu.VMEM((COLS, 2 * COLS), BF),
            pltpu.VMEM((VS, ROWS + 2, MEMBERS, COLS), F32),
            pltpu.VMEM((NVG, VS * 2 * COLS, COLS), BF),
            pltpu.VMEM((NB, BLOCK), jnp.int32),
            dma((NVG, 2)), dma((NVG, 2)), dma((2,)), dma((2,)),
            dma((4,)), dma((4,)), dma((4,)), dma((4,)),
            dma((nlat + nlon - 2,)), dma((NB, 2)), dma((NB, 2)), dma((nlat - 1,)), dma((nlon - 1,)),
            dma((NVG,)), dma((5,)),
        ],
        compiler_params=pltpu.CompilerParams(
            collective_id=0, has_side_effects=True, vmem_limit_bytes=34 << 20
        ),
        name="forecast",
    )(x, wind, lat, lon, var)


def analysis_kernel(
    x_ref, y_ref, rank_ref, t0_ref, pair_ref, lat_hbm, lon_hbm, val_hbm, err_hbm,
    out_hbm,
    lat_ref, lon_ref, val_ref, err_ref, ob,
    ys, a_all, s_all, a_pk, b_pk, l_pk, a_more, b_more, t_more, xv, rhs, p2, q3, nch,
    l_small, l_out,
):
    small = [
        pltpu.make_async_copy(a, b, l_small.at[i])
        for i, (a, b) in enumerate(
            [(lat_hbm, lat_ref), (lon_hbm, lon_ref), (val_hbm, val_ref), (err_hbm, err_ref)]
        )
    ]
    for c in small:
        c.start()
    out_rows = ob.reshape(MEMBERS * NVAR * ROWS, COLS)

    def store(g):
        vs = pl.ds(g * VG, VG)
        return pltpu.make_async_copy(ob.at[:, vs], out_hbm.at[:, vs], l_out.at[g])

    rank = rank_ref[...]
    for b in range(NB):
        top = jnp.max(rank[b : b + 1, :])
        nch[b] = ((top + KC) * (1.0 / KC)).astype(jnp.int32)
        ys[0:PIECE, b * BLOCK : (b + 1) * BLOCK] = y_ref[2 * b]
        ys[PIECE:, b * BLOCK : (b + 1) * BLOCK] = y_ref[2 * b + 1][0 : MEMBERS - PIECE]
    for c in small:
        c.wait()
    lat, lon = by_block(lat_ref).astype(F32), by_block(lon_ref).astype(F32)
    values, variances = by_block(val_ref), by_block(err_ref)
    row_id = lax.broadcasted_iota(jnp.int32, (KC, BLOCK), 0).astype(F32)
    lane96 = lax.broadcasted_iota(jnp.int32, (KC, 3 * KC), 1)
    zero8 = jnp.zeros((8, BLOCK), F32)

    def packed(pick, b):
        zero = jnp.zeros_like(pick)
        pick3 = jnp.concatenate(
            [
                jnp.concatenate([pick, zero], axis=1),
                jnp.concatenate([zero, pick], axis=1),
                jnp.concatenate([pick, zero], axis=1),
            ],
            axis=0,
        )
        return dot(pick, a_all[b]).astype(BF), dot(s_all[b], pick3, ((1,), (1,))).astype(BF)

    stacked = None
    for b in range(NB):
        prior = ys[:, b * BLOCK : (b + 1) * BLOCK]
        average = jnp.sum(prior, axis=0, keepdims=True) * (1.0 / MEMBERS)
        anomaly = prior - average
        spread = jnp.sum(anomaly * anomaly, axis=0, keepdims=True) / (MEMBERS - 1)
        errors = variances[b : b + 1, :]
        total = spread + errors
        weights = anomaly * (1.0 / ((MEMBERS - 1) * total))
        shifts = (values[b : b + 1, :] - average) - anomaly * (
            1.0 / (1.0 + jnp.sqrt(errors / total))
        )
        wh = hi(weights)
        a = jnp.concatenate([wh, weights - wh, wh, zero8], axis=0).T.astype(BF)
        sh, sl = split(shifts)
        a_all[b] = a
        s_all[b] = jnp.concatenate([sh, sl], axis=1)
        s3 = jnp.concatenate([sh, sl, sh], axis=1)
        for j in range(b + 1, NB):
            yl = ys[:, j * BLOCK : (j + 1) * BLOCK]
            yh = hi(yl)
            y3 = jnp.concatenate([yh, yh, yl - yh, zero8], axis=0).astype(BF)
            qh, ql = split(dot(a, y3) * pair_ref[pair_at(b, j)])
            ys[:, j * BLOCK : (j + 1) * BLOCK] = yl + dot(
                s3, jnp.concatenate([qh, qh, ql], axis=0)
            )
        pick = (row_id == rank[b : b + 1, :]).astype(BF)
        a_pk[b], b_pk[b] = packed(pick, b)
        if b % 2 == 0:
            sh32 = sh.astype(F32)
            s_rows = jnp.concatenate([sh32, sh32, sl.astype(F32), zero8], axis=0).astype(BF)
            stacked = dot(s_rows, jnp.concatenate([pick] * 3, axis=0), ((1,), (1,))).astype(BF)
        else:
            c = dot(a_pk[b], stacked)
            ch = hi(c)
            c3 = jnp.where((lane96 >= KC) & (lane96 < 2 * KC), c - ch, ch)
            l_pk[b // 2] = jnp.concatenate([c3, b_pk[b - 1].astype(F32)], axis=0).astype(BF)

    lat0f = (lax.axis_index("lat") * ROWS).astype(F32)
    lon0f = (lax.axis_index("lon") * COLS).astype(F32)
    for b in range(NB):

        @pl.loop(1, nch[b])
        def _(c):
            slot = b * (NCH - 1) + c - 1
            pick = (row_id + (c * KC).astype(F32) == rank[b : b + 1, :]).astype(F32)
            a_more[slot], b_more[slot] = packed(pick.astype(BF), b)
            cell_tapers(pick, lat[b : b + 1, :], lon[b : b + 1, :], lat0f, lon0f, t_more, slot)

    zero_cols = jnp.zeros((8, ROWS * COLS), F32)

    def stack_x(i):
        x = xv[i]
        xh = hi(x)
        rhs[i] = jnp.concatenate([xh, xh, x - xh, zero_cols], axis=0).astype(BF)

    def put_q(i, q):
        qh, ql = split(q)
        q3[i] = jnp.concatenate([qh, qh, ql], axis=0)

    def add_chunk(a, s3, t):
        for i in range(VG):
            put_q(i, dot(a, rhs[i]) * t[...])
        for i in range(VG):
            xv[i] += dot(s3, q3[i])

    @pl.loop(0, NVAR // VG)
    def _(g):
        for i in range(VG):
            for r in range(ROWS):
                xv[i, :, r * COLS : (r + 1) * COLS] = x_ref[g * VG + i, r]

        @pl.loop(0, NB // 2)
        def _(pair):
            b = 2 * pair
            few = jnp.maximum(nch[b], nch[b + 1]) <= 1

            @pl.when(few)
            def _():
                a2 = a_pk[pl.ds(b, 2)].reshape(2 * KC, 128)
                for i in range(VG):
                    stack_x(i)
                for i in range(VG):
                    p = dot(a2, rhs[i])
                    p2[i] = p[KC:]
                    put_q(i, p[:KC] * t0_ref[b])
                for i in range(VG):
                    r = dot(l_pk[pair], q3[i])
                    xv[i] += r[KC:]
                    put_q(i, (p2[i] + r[:KC]) * t0_ref[b + 1])
                for i in range(VG):
                    xv[i] += dot(b_pk[b + 1], q3[i])

            @pl.when(jnp.logical_not(few))
            def _():
                @pl.loop(b, b + 2)
                def _(bb):
                    for i in range(VG):
                        stack_x(i)
                    add_chunk(a_pk[bb], b_pk[bb], t0_ref.at[bb])

                    @pl.loop(1, nch[bb])
                    def _(c):
                        slot = bb * (NCH - 1) + c - 1
                        add_chunk(a_more[slot], b_more[slot], t_more.at[slot])

        for i in range(VG):
            for r in range(ROWS):
                out_rows[
                    pl.ds((g * VG + i) * ROWS + r, MEMBERS, stride=NVAR * ROWS), :
                ] = xv[i, :, r * COLS : (r + 1) * COLS]
        store(g).start()

    for g in range(NVAR // VG):
        store(g).wait()


def analysis(x, y, rank, t0, pairs, lat, lon, val, err):
    vm = pl.BlockSpec(memory_space=pltpu.VMEM)
    hbm = pl.BlockSpec(memory_space=pltpu.HBM)
    more = NB * (NCH - 1)
    dma = pltpu.SemaphoreType.DMA
    return pl.pallas_call(
        analysis_kernel,
        out_shape=jax.ShapeDtypeStruct((MEMBERS, NVAR, ROWS, COLS), F32),
        in_specs=[vm] * 5 + [hbm] * 4,
        out_specs=hbm,
        scratch_shapes=[
            pltpu.VMEM((GROUPS, OBS), jnp.int32),
            pltpu.VMEM((GROUPS, OBS), jnp.int32),
            pltpu.VMEM((GROUPS, OBS), F32),
            pltpu.VMEM((GROUPS, OBS), F32),
            pltpu.VMEM((MEMBERS, NVAR, ROWS, COLS), F32),
            pltpu.VMEM((MEMBERS, NB * BLOCK), F32),
            pltpu.VMEM((NB, BLOCK, 128), BF),
            pltpu.VMEM((NB, MEMBERS, 256), BF),
            pltpu.VMEM((NB, KC, 128), BF),
            pltpu.VMEM((NB, MEMBERS, 3 * KC), BF),
            pltpu.VMEM((NB // 2, KC + MEMBERS, 3 * KC), BF),
            pltpu.VMEM((more, KC, 128), BF),
            pltpu.VMEM((more, MEMBERS, 3 * KC), BF),
            pltpu.VMEM((more, KC, ROWS * COLS), F32),
            pltpu.VMEM((VG, MEMBERS, ROWS * COLS), F32),
            pltpu.VMEM((VG, 128, ROWS * COLS), BF),
            pltpu.VMEM((VG, KC, ROWS * COLS), F32),
            pltpu.VMEM((VG, 3 * KC, ROWS * COLS), BF),
            pltpu.SMEM((NB,), jnp.int32),
            dma((4,)), dma((NVAR // VG,)),
        ],
        compiler_params=pltpu.CompilerParams(vmem_limit_bytes=22 << 20),
        name="analysis",
    )(x, y, rank, t0, pairs, lat, lon, val, err)


def solution(mesh):
    nlat, nlon = mesh.shape["lat"], mesh.shape["lon"]
    assert nlon == 2 * NB

    def body(prognostic_samples, wind, obs_lat, obs_lon, obs_var, obs_value, obs_error):
        hbm = [
            pltpu.with_memory_space_constraint(a, pltpu.HBM)
            for a in (prognostic_samples, wind, obs_lat, obs_lon, obs_var, obs_value, obs_error)
        ]
        xf, y, rank, t0, pairs = forecast(*hbm[:5], nlat, nlon)
        return analysis(xf, y, rank, t0, pairs, hbm[2], hbm[3], hbm[5], hbm[6])

    in_specs = (P(None, None, "lat", "lon"), P(None, "lat", "lon"), P(), P(), P(), P(), P())
    out_specs = P(None, None, "lat", "lon")
    return jax.shard_map(body, mesh=mesh, in_specs=in_specs, out_specs=out_specs, check_vma=False)
```

```python
import jax
import jax.numpy as jnp
from jax import lax
from jax.experimental import pallas as pl
from jax.experimental.pallas import tpu as pltpu
from jax.sharding import PartitionSpec as P

MEMBERS, NVAR, ROWS, COLS = 40, 25, 8, 128
NLON = 2048
GROUPS, OBS = 2, 512
NB, BLOCK = 8, 128
PER = OBS // BLOCK
LOC = 32.0
DIFFUSE = 0.1
VS = 5
NVG = NVAR // VS
MG = MEMBERS // 8
SIDE = (ROWS + 2) // 3
PIECE = 24
KC = 32
NCH = BLOCK // KC
VG = 5
F32, BF = jnp.float32, jnp.bfloat16
MESH = pl.DeviceIdType.MESH


def hi(x):
    return x.astype(BF).astype(F32)


def split(x):
    high = x.astype(BF)
    return high, (x - high.astype(F32)).astype(BF)


def dot(a, b, dims=((1,), (0,))):
    return lax.dot_general(a, b, (dims, ((), ())), preferred_element_type=F32)


def peers(nlat, nlon):
    me_lat = lax.axis_index("lat")
    me_lon = lax.axis_index("lon")

    def place(dlat, dlon):
        lat = lax.rem(me_lat + (dlat + nlat), nlat) if dlat else me_lat
        lon = lax.rem(me_lon + (dlon + nlon), nlon) if dlon else me_lon
        return lat, lon

    def remote(src, dst, ssem, rsem, dlat, dlon):
        return pltpu.make_async_remote_copy(
            src_ref=src,
            dst_ref=dst,
            send_sem=ssem,
            recv_sem=rsem,
            device_id=place(dlat, dlon),
            device_id_type=MESH,
        )

    def signal(barrier, offsets):
        for o in offsets:
            pl.semaphore_signal(barrier, inc=1, device_id=place(*o), device_id_type=MESH)

    return me_lat, me_lon, place, remote, signal


def taper_sq(d2):
    z = jnp.sqrt(d2) * (1.0 / LOC)
    inner = (((-0.25 * z + 0.5) * z + 0.625) * z - 5.0 / 3.0) * z * z + 1.0
    outer = (
        ((((z * (1.0 / 12.0) - 0.5) * z + 0.625) * z + 5.0 / 3.0) * z - 5.0) * z
        + 4.0
        - (2.0 / 3.0) / jnp.maximum(z, 1.0)
    )
    return jnp.where(z <= 1.0, inner, jnp.where(z < 2.0, outer, 0.0))


def by_block(ref):
    parts = []
    for b in range(NB):
        first = (b % PER) * BLOCK
        parts.append(ref[b // PER : b // PER + 1, first : first + BLOCK])
    return jnp.concatenate(parts, axis=0)


def pair_at(b, j):
    return b * (2 * NB - b - 1) // 2 + j - b - 1


def cell_tapers(pick, lat_row, lon_row, lat0f, lon0f, out, slot):
    col_f = lax.broadcasted_iota(jnp.int32, (KC, COLS), 1).astype(F32) + lon0f
    latc = jnp.sum(pick * lat_row, axis=1, keepdims=True)
    lonc = jnp.sum(pick * lon_row, axis=1, keepdims=True)
    dlon = jnp.abs(lonc - col_f)
    dlon = jnp.minimum(dlon, NLON - dlon)
    dlon = dlon * dlon
    for r in range(ROWS):
        dlat = latc - (lat0f + float(r))
        out[slot, :, r * COLS : (r + 1) * COLS] = taper_sq(dlon + dlat * dlat)


def reach_tables(lat, lon, lat0f, lon0f, rank_ref, t0_ref):
    dy = jnp.maximum(jnp.maximum(lat0f - lat, lat - (lat0f + (ROWS - 1))), 0.0)
    off = lon - lon0f
    off = jnp.where(off < 0, off + NLON, off)
    dx = jnp.maximum(jnp.minimum(off - (COLS - 1), NLON - off), 0.0)
    reach = dx * dx + dy * dy < 4.0 * LOC * LOC
    before = (
        lax.broadcasted_iota(jnp.int32, (BLOCK, BLOCK), 0)
        < lax.broadcasted_iota(jnp.int32, (BLOCK, BLOCK), 1)
    ).astype(F32)
    rank = jnp.where(reach, dot(reach.astype(F32).astype(BF), before.astype(BF)), -1.0)
    rank_ref[...] = rank
    row_id = lax.broadcasted_iota(jnp.int32, (KC, BLOCK), 0).astype(F32)
    for b in range(NB):
        pick = (row_id == rank[b : b + 1, :]).astype(F32)
        cell_tapers(pick, lat[b : b + 1, :], lon[b : b + 1, :], lat0f, lon0f, t0_ref, b)


def pair_tables(lat, lon, pair_ref):
    lat_t, lon_t = lat.T, lon.T
    for b in range(NB):
        for j in range(b + 1, NB):
            dlat = lat_t[:, b : b + 1] - lat[j : j + 1, :]
            dlon = jnp.abs(lon_t[:, b : b + 1] - lon[j : j + 1, :])
            dlon = jnp.minimum(dlon, NLON - dlon)
            pair_ref[pair_at(b, j)] = taper_sq(dlat * dlat + dlon * dlon)


def forecast_kernel(
    nlat, nlon,
    x_hbm, wind_hbm, lat_hbm, lon_hbm, var_hbm, val_hbm, err_hbm,
    xf, out, rank_ref, t0_ref, pair_ref, obs_ref,
    xb, wind_ref, lat_ref, lon_ref, var_ref, val_ref, err_ref, desc, desc_s, xft, yo, part, line, block_sum, got_a, got_b,
    xt, edge, edge_w, edge_e, corner, wind_n, halo, halo_s, halo1_s, coef, shift, unit, q1_s, to_edge, at8,
    s_row, r_row, s_edge, r_edge, s_corner, r_corner, s_wind, r_wind,
    send, send_a, recv_a, recv_b, recv_c, l_x, l_small,
):
    def fetch(vg):
        vs = pl.ds(vg * VS, VS)
        return pltpu.make_async_copy(x_hbm.at[:, vs], xb.at[:, vs], l_x.at[vg])

    small = [
        pltpu.make_async_copy(a, b, l_small.at[i])
        for i, (a, b) in enumerate(
            [
                (wind_hbm, wind_ref), (lat_hbm, lat_ref), (lon_hbm, lon_ref),
                (var_hbm, var_ref), (val_hbm, val_ref), (err_hbm, err_ref),
            ]
        )
    ]
    for vg in range(NVG):
        fetch(vg).start()
    for c in small:
        c.start()
    x_ref = xb.reshape(MEMBERS * NVAR * ROWS, COLS)
    me_lat, me_lon, place, remote, signal = peers(nlat, nlon)
    barrier = pltpu.get_barrier_semaphore()
    near = [(o, 0) for o in range(1, nlat)] + [(0, o) for o in range(1, nlon)]
    near += [(-1, -1), (-1, 1), (1, -1), (1, 1)]
    signal(barrier, near)

    def column(r, mg, v):
        return x_ref[pl.ds(mg * (8 * NVAR * ROWS) + v * ROWS + r, 8, stride=NVAR * ROWS), :]

    def rows(vg, up):
        vs = pl.ds(vg * VS, VS)
        if up:
            return remote(
                xt.at[vs, 2:4],
                xt.at[vs, ROWS + 2 : ROWS + 4],
                s_row.at[vg, 0], r_row.at[vg, 0], -1, 0,
            )
        return remote(
            xt.at[vs, ROWS : ROWS + 2], xt.at[vs, 0:2], s_row.at[vg, 1], r_row.at[vg, 1], 1, 0
        )

    def send_rows(vg):
        rows(vg, True).start()
        rows(vg, False).start()

    def sent_rows(vg):
        rows(vg, True).wait_send()
        rows(vg, False).wait_send()

    winds = [
        remote(wind_ref, wind_n.at[i], s_wind.at[i], r_wind.at[i], dlat, dlon)
        for i, (dlat, dlon) in enumerate([(1, 0), (-1, 0), (0, 1), (0, -1)])
    ]
    edges = [
        remote(edge, edge_w, s_edge.at[0], r_edge.at[0], 0, 1),
        remote(edge, edge_e, s_edge.at[1], r_edge.at[1], 0, -1),
    ]
    corners = [
        remote(edge.at[ROWS - 1], corner.at[0], s_corner.at[0], r_corner.at[0], 1, 1),
        remote(edge.at[ROWS - 1], corner.at[1], s_corner.at[1], r_corner.at[1], 1, -1),
        remote(edge.at[0], corner.at[2], s_corner.at[2], r_corner.at[2], -1, 1),
        remote(edge.at[0], corner.at[3], s_corner.at[3], r_corner.at[3], -1, -1),
    ]
    for vg in range(NVG):
        fetch(vg).wait()

        @pl.loop(vg * VS, (vg + 1) * VS)
        def _(v):
            for r in (0, 1, ROWS - 2, ROWS - 1):
                for mg in range(MG):
                    xt[v, r + 2, mg * 8 : (mg + 1) * 8, :] = column(r, mg, v)

        if vg == 0:
            for c in small:
                c.wait()
            pl.semaphore_wait(barrier, len(near))
            for w in winds:
                w.start()
        if vg < 2:
            send_rows(vg)

    edge_src = lax.rem(lax.broadcasted_iota(jnp.int32, (2 * COLS, COLS), 0), COLS)
    edge_dst = lax.broadcasted_iota(jnp.int32, (2 * COLS, COLS), 1)
    outer = (edge_src < 2) | (edge_src >= COLS - 2)
    moved = jnp.where(outer, (edge_dst - edge_src) & (COLS - 1), -1)

    @pl.loop(0, NVG)
    def _(vg):
        for vi in range(VS):
            to_edge[vg, vi * 2 * COLS : (vi + 1) * 2 * COLS, :] = jnp.where(
                moved == 4 * (vg * VS + vi), 1.0, 0.0
            ).astype(BF)

    edge[...] = jnp.zeros_like(edge)

    @pl.loop(0, NVG)
    def _(vg):
        pieces = []
        for vi in range(VS):
            v = vg * VS + vi
            for r in range(2, ROWS - 2):
                for mg in range(MG):
                    xt[v, r + 2, mg * 8 : (mg + 1) * 8, :] = column(r, mg, v)
        for vi in range(VS):
            pieces += split(xt[vg * VS + vi, 2 : ROWS + 2].reshape(ROWS * MEMBERS, COLS))
        packed = dot(jnp.concatenate(pieces, axis=1), to_edge[vg])
        edge[...] += packed.reshape(ROWS, MEMBERS, COLS)

    for e in edges + corners:
        e.start()
    sent_rows(0)
    send_rows(2)

    lat_all, lon_all = lat_ref[...], lon_ref[...]
    owned = (lat_all // ROWS == me_lat) & (lon_all // COLS == me_lon)
    row_all = lat_all & (ROWS - 1)
    group = (row_all >= 3).astype(jnp.int32) + (row_all >= 6).astype(jnp.int32)
    part_of = row_all - 3 * group
    desc[...] = (var_ref[...] * SIDE + group) * COLS + (lon_all & (COLS - 1))
    to_scalar = pltpu.make_async_copy(desc, desc_s, l_small.at[6])
    to_scalar.start()
    at_all = jnp.where(owned, part_of, -1)
    for b in range(NB):
        cut = (b % PER) * BLOCK
        at8[b : b + 1, :] = at_all[b // PER : b // PER + 1, cut : cut + BLOCK]

    src = lax.rem(lax.broadcasted_iota(jnp.int32, (2 * COLS, 2 * COLS), 0), COLS)
    dst = lax.broadcasted_iota(jnp.int32, (2 * COLS, 2 * COLS), 1)
    east_of = (dst < COLS) & (src == dst + 1)
    west_of = (dst >= COLS) & (src == dst - COLS - 1)
    shift[...] = jnp.where(east_of | west_of, 1.0, 0.0).astype(BF)
    col_of = lax.rem(lax.broadcasted_iota(jnp.int32, (COLS, 2 * COLS), 1), COLS)
    row_of = lax.broadcasted_iota(jnp.int32, (COLS, 2 * COLS), 0)
    unit[...] = jnp.where(col_of == row_of, 1.0, 0.0).astype(BF)

    for w in winds:
        w.wait_recv()
    has_lo = (me_lat > 0).astype(F32)
    has_hi = (me_lat < nlat - 1).astype(F32)

    def row_wind(r):
        if r < 0:
            return wind_n[0, 0, ROWS - 1 : ROWS, :], wind_n[0, 1, ROWS - 1 : ROWS, :]
        if r == ROWS:
            return wind_n[1, 0, 0:1, :], wind_n[1, 1, 0:1, :]
        return wind_ref[0, r : r + 1, :], wind_ref[1, r : r + 1, :]

    def four(u, v, r):
        nxt, prv = DIFFUSE - 0.5 * v, DIFFUSE + 0.5 * v
        if r == 0:
            prv = prv * has_lo
        if r == ROWS - 1:
            nxt = nxt * has_hi
        return DIFFUSE - 0.5 * u, DIFFUSE + 0.5 * u, nxt, prv

    for r in range(-1, ROWS + 1):
        u, v = row_wind(r)
        for i, c in enumerate(four(u, v, r)):
            coef[i, r + 1] = jnp.broadcast_to(c, (8, COLS))

    sent_rows(1)
    send_rows(3)

    for e in edges + corners:
        e.wait_recv()
    lane4 = lax.rem(lax.broadcasted_iota(jnp.int32, (MEMBERS, COLS), 1), 4)
    from_west = lane4 >= 2
    halo[0] = jnp.where(from_west, corner[0], corner[1])
    halo[ROWS + 1] = jnp.where(from_west, corner[2], corner[3])
    for r in range(ROWS):
        halo[r + 1] = jnp.where(from_west, edge_w[r], edge_e[r])

    def beside(t):
        return jnp.where(lane4 == 0, t, pltpu.roll(t, 2, 1))

    for r in range(ROWS + 2):
        halo_s[r] = beside(halo[r])
    for r in range(ROWS):
        u, v = [
            jnp.where(
                from_west,
                jnp.broadcast_to(wind_n[2, i, r : r + 1, COLS - 1 : COLS], (MEMBERS, COLS)),
                jnp.broadcast_to(wind_n[3, i, r : r + 1, 0:1], (MEMBERS, COLS)),
            )
            for i in range(2)
        ]
        ce, cw, cn, cs = four(u, v, r)
        own, got = edge[r], halo[r + 1]
        east = pltpu.roll(jnp.where(lane4 == 0, own, got), COLS - 1, 1)
        west = pltpu.roll(jnp.where(lane4 == 3, own, got), 1, 1)
        after = (
            (1.0 - 4.0 * DIFFUSE) * got
            + ce * east
            + cw * west
            + cn * halo[r + 2]
            + cs * halo[r]
        )
        halo1_s[r] = beside(after)

    def step(q, nxt, prv, side, back, first, count):
        shape = (count, MG, 8, COLS)
        high, low = split(q)
        both = dot(jnp.concatenate([high, low], axis=1), shift[...])
        lane = lax.broadcasted_iota(jnp.int32, (count * MEMBERS, COLS), 1)
        beyond = pltpu.roll(side.reshape(count * MEMBERS, COLS), back, 1)
        east = jnp.where(lane == COLS - 1, beyond, both[:, :COLS])
        west = jnp.where(lane == 0, beyond, both[:, COLS:])
        c = [coef[i, first : first + count].reshape(count, 1, 8, COLS) for i in range(4)]
        new = (
            (1.0 - 4.0 * DIFFUSE) * q.reshape(shape)
            + c[0] * east.reshape(shape)
            + c[1] * west.reshape(shape)
            + c[2] * nxt.reshape(shape)
            + c[3] * prv.reshape(shape)
        )
        return new.reshape(count * MEMBERS, COLS)

    def block(ref, v, first, count):
        return ref[v, first : first + count].reshape(count * MEMBERS, COLS)

    @pl.loop(0, NVG)
    def _(vg):
        rows(vg, True).wait_recv()
        rows(vg, False).wait_recv()

        @pl.when(vg == 0)
        def _():
            sent_rows(2)
            send_rows(4)

        n1, n2 = ROWS + 2, ROWS
        for vi in range(VS):
            v = vg * VS + vi
            q1_s[vi] = step(
                block(xt, v, 1, n1), block(xt, v, 2, n1), block(xt, v, 0, n1),
                halo_s[...], (COLS - 1 - 4 * v) & (COLS - 1), 0, n1,
            ).reshape(n1, MEMBERS, COLS)
        for vi in range(VS):
            v = vg * VS + vi
            new = step(
                block(q1_s, vi, 1, n2), block(q1_s, vi, 2, n2), block(q1_s, vi, 0, n2),
                halo1_s[...], (COLS - 1 - 4 * v) & (COLS - 1), 1, n2,
            )
            xf[v] = new.reshape(n2, MEMBERS, COLS)
            high, low = split(new)
            both = jnp.concatenate([high, low], axis=1)
            for i in range(SIDE):
                n = min(3, ROWS - 3 * i) * MEMBERS
                xft[pl.ds((v * SIDE + i) * COLS, COLS), 0:n] = dot(
                    unit[...], both[i * 3 * MEMBERS : i * 3 * MEMBERS + n, :], ((1,), (1,))
                )

    to_scalar.wait()
    half, odd = me_lon // 2, lax.rem(me_lon, 2)

    def piece(i, h, b):
        return pltpu.make_async_remote_copy(
            src_ref=part.at[2 * b + h],
            dst_ref=got_a.at[i, odd],
            send_sem=send_a.at[i, h],
            recv_sem=recv_a.at[i, odd],
            device_id=(me_lat, 2 * b + h),
            device_id_type=MESH,
        )

    def arrival(i, p):
        return pltpu.make_async_remote_copy(
            src_ref=part.at[0],
            dst_ref=got_a.at[i, p],
            send_sem=send_a.at[i, 0],
            recv_sem=recv_a.at[i, p],
            device_id=(me_lat, lax.rem(me_lon + 1, nlon)),
            device_id_type=MESH,
        )

    first = []
    for i in list(range(1, NB)) + [0]:
        b = lax.rem(half + i, NB)

        @pl.loop(0, BLOCK // 8)
        def _(g):
            for j in range(8):
                k = g * 8 + j
                at = desc_s[b // PER, lax.rem(b, PER) * BLOCK + k]
                yo[i, pl.ds(k, 1), :] = xft[pl.ds(at, 1), :]

        turned = yo[i].T
        at = jnp.broadcast_to(at8[pl.ds(b, 1), :], (MEMBERS, BLOCK))
        mine = jnp.zeros((MEMBERS, BLOCK), F32)
        for n in range(3):
            mine = jnp.where(at == n, turned[n * MEMBERS : (n + 1) * MEMBERS, :], mine)
        part[2 * b] = mine[0:PIECE]
        part[2 * b + 1] = jnp.concatenate(
            [mine[PIECE:], jnp.zeros((2 * PIECE - MEMBERS, BLOCK), F32)], axis=0
        )
        for h in (0, 1) if i else (1 - odd,):
            c = piece(i, h, b)
            c.start()
            first.append(c)
    lat_f, lon_f = by_block(lat_ref).astype(F32), by_block(lon_ref).astype(F32)
    lat0f, lon0f = (me_lat * ROWS).astype(F32), (me_lon * COLS).astype(F32)
    for i, t in enumerate([lat_f, lon_f, by_block(val_ref), by_block(err_ref)]):
        obs_ref[i] = t
    reach_tables(lat_f, lon_f, lat0f, lon0f, rank_ref, t0_ref)
    total = part[me_lon]
    for i in range(1, NB):
        for p in (0, 1):
            arrival(i, p).wait_recv()
            total = total + got_a[i, p]
    arrival(0, 1 - odd).wait_recv()
    total = total + got_a[0, 1 - odd]
    line[...] = total
    second = [
        remote(line, got_b.at[o - 1], send.at[o - 1], recv_b.at[o - 1], o, 0)
        for o in range(1, nlat)
    ]
    for c in second:
        c.start()
    for i, c in enumerate(second):
        c.wait_recv()
        total = total + got_b[i]
    block_sum[...] = total
    third = [
        remote(block_sum, out.at[me_lon], send.at[nlat + o - 2], recv_c.at[o - 1], 0, o)
        for o in range(1, nlon)
    ]
    for c in third:
        c.start()
    out[me_lon] = total
    pair_tables(lat_f, lon_f, pair_ref)
    for c in third:
        c.wait_recv()

    for c in winds + edges + corners + first + second + third:
        c.wait_send()

    sent_rows(3)
    sent_rows(4)


def forecast(x, wind, lat, lon, var, val, err, nlat, nlon):
    vm = pl.BlockSpec(memory_space=pltpu.VMEM)
    dma = pltpu.SemaphoreType.DMA
    return pl.pallas_call(
        lambda *refs: forecast_kernel(nlat, nlon, *refs),
        out_shape=(
            jax.ShapeDtypeStruct((NVAR, ROWS, MEMBERS, COLS), F32),
            jax.ShapeDtypeStruct((2 * NB, PIECE, BLOCK), F32),
            jax.ShapeDtypeStruct((NB, BLOCK), F32),
            jax.ShapeDtypeStruct((NB, KC, ROWS * COLS), F32),
            jax.ShapeDtypeStruct((NB * (NB - 1) // 2, BLOCK, BLOCK), F32),
            jax.ShapeDtypeStruct((4, NB, BLOCK), F32),
        ),
        in_specs=[pl.BlockSpec(memory_space=pltpu.HBM)] * 7,
        out_specs=(vm,) * 6,
        scratch_shapes=[
            pltpu.VMEM((MEMBERS, NVAR, ROWS, COLS), F32),
            pltpu.VMEM((2, ROWS, COLS), F32),
            pltpu.VMEM((GROUPS, OBS), jnp.int32),
            pltpu.VMEM((GROUPS, OBS), jnp.int32),
            pltpu.VMEM((GROUPS, OBS), jnp.int32),
            pltpu.VMEM((GROUPS, OBS), F32),
            pltpu.VMEM((GROUPS, OBS), F32),
            pltpu.VMEM((GROUPS, OBS), jnp.int32),
            pltpu.SMEM((GROUPS, OBS), jnp.int32),
            pltpu.VMEM((NVAR * SIDE * COLS, COLS), F32),
            pltpu.VMEM((NB, BLOCK, COLS), F32),
            pltpu.VMEM((2 * NB, PIECE, BLOCK), F32),
            pltpu.VMEM((PIECE, BLOCK), F32),
            pltpu.VMEM((PIECE, BLOCK), F32),
            pltpu.VMEM((NB, 2, PIECE, BLOCK), F32),
            pltpu.VMEM((nlat - 1, PIECE, BLOCK), F32),
            pltpu.VMEM((NVAR, ROWS + 4, MEMBERS, COLS), F32),
            pltpu.VMEM((ROWS, MEMBERS, COLS), F32),
            pltpu.VMEM((ROWS, MEMBERS, COLS), F32),
            pltpu.VMEM((ROWS, MEMBERS, COLS), F32),
            pltpu.VMEM((4, MEMBERS, COLS), F32),
            pltpu.VMEM((4, 2, ROWS, COLS), F32),
            pltpu.VMEM((ROWS + 2, MEMBERS, COLS), F32),
            pltpu.VMEM((ROWS + 2, MEMBERS, COLS), F32),
            pltpu.VMEM((ROWS, MEMBERS, COLS), F32),
            pltpu.VMEM((4, ROWS + 2, 8, COLS), F32),
            pltpu.VMEM((2 * COLS, 2 * COLS), BF),
            pltpu.VMEM((COLS, 2 * COLS), BF),
            pltpu.VMEM((VS, ROWS + 2, MEMBERS, COLS), F32),
            pltpu.VMEM((NVG, VS * 2 * COLS, COLS), BF),
            pltpu.VMEM((NB, BLOCK), jnp.int32),
            dma((NVG, 2)), dma((NVG, 2)), dma((2,)), dma((2,)),
            dma((4,)), dma((4,)), dma((4,)), dma((4,)),
            dma((nlat + nlon - 2,)), dma((NB, 2)), dma((NB, 2)), dma((nlat - 1,)), dma((nlon - 1,)),
            dma((NVG,)), dma((7,)),
        ],
        compiler_params=pltpu.CompilerParams(
            collective_id=0, has_side_effects=True, vmem_limit_bytes=34 << 20
        ),
        name="forecast",
    )(x, wind, lat, lon, var, val, err)


def analysis_kernel(
    x_ref, y_ref, rank_ref, t0_ref, pair_ref, obs_ref,
    out_hbm,
    ob,
    ys, a_all, s_all, a_pk, b_pk, l_pk, a_more, b_more, t_more, xv, rhs, p2, q3, nch,
    l_out,
):
    out_rows = ob.reshape(MEMBERS * NVAR * ROWS, COLS)

    def store(g):
        vs = pl.ds(g * VG, VG)
        return pltpu.make_async_copy(ob.at[:, vs], out_hbm.at[:, vs], l_out.at[g])

    rank = rank_ref[...]
    for b in range(NB):
        top = jnp.max(rank[b : b + 1, :])
        nch[b] = ((top + KC) * (1.0 / KC)).astype(jnp.int32)
        ys[0:PIECE, b * BLOCK : (b + 1) * BLOCK] = y_ref[2 * b]
        ys[PIECE:, b * BLOCK : (b + 1) * BLOCK] = y_ref[2 * b + 1][0 : MEMBERS - PIECE]
    lat, lon, values, variances = [obs_ref[i] for i in range(4)]
    row_id = lax.broadcasted_iota(jnp.int32, (KC, BLOCK), 0).astype(F32)
    lane96 = lax.broadcasted_iota(jnp.int32, (KC, 3 * KC), 1)
    zero8 = jnp.zeros((8, BLOCK), F32)

    def packed(pick, b):
        zero = jnp.zeros_like(pick)
        pick3 = jnp.concatenate(
            [
                jnp.concatenate([pick, zero], axis=1),
                jnp.concatenate([zero, pick], axis=1),
                jnp.concatenate([pick, zero], axis=1),
            ],
            axis=0,
        )
        return dot(pick, a_all[b]).astype(BF), dot(s_all[b], pick3, ((1,), (1,))).astype(BF)

    stacked = None
    for b in range(NB):
        prior = ys[:, b * BLOCK : (b + 1) * BLOCK]
        average = jnp.sum(prior, axis=0, keepdims=True) * (1.0 / MEMBERS)
        anomaly = prior - average
        spread = jnp.sum(anomaly * anomaly, axis=0, keepdims=True) / (MEMBERS - 1)
        errors = variances[b : b + 1, :]
        total = spread + errors
        weights = anomaly * (1.0 / ((MEMBERS - 1) * total))
        shifts = (values[b : b + 1, :] - average) - anomaly * (
            1.0 / (1.0 + jnp.sqrt(errors / total))
        )
        wh = hi(weights)
        a = jnp.concatenate([wh, weights - wh, wh, zero8], axis=0).T.astype(BF)
        sh, sl = split(shifts)
        a_all[b] = a
        s_all[b] = jnp.concatenate([sh, sl], axis=1)
        s3 = jnp.concatenate([sh, sl, sh], axis=1)
        for j in range(b + 1, NB):
            yl = ys[:, j * BLOCK : (j + 1) * BLOCK]
            yh = hi(yl)
            y3 = jnp.concatenate([yh, yh, yl - yh, zero8], axis=0).astype(BF)
            qh, ql = split(dot(a, y3) * pair_ref[pair_at(b, j)])
            ys[:, j * BLOCK : (j + 1) * BLOCK] = yl + dot(
                s3, jnp.concatenate([qh, qh, ql], axis=0)
            )
        pick = (row_id == rank[b : b + 1, :]).astype(BF)
        a_pk[b], b_pk[b] = packed(pick, b)
        if b % 2 == 0:
            sh32 = sh.astype(F32)
            s_rows = jnp.concatenate([sh32, sh32, sl.astype(F32), zero8], axis=0).astype(BF)
            stacked = dot(s_rows, jnp.concatenate([pick] * 3, axis=0), ((1,), (1,))).astype(BF)
        else:
            c = dot(a_pk[b], stacked)
            ch = hi(c)
            c3 = jnp.where((lane96 >= KC) & (lane96 < 2 * KC), c - ch, ch)
            l_pk[b // 2] = jnp.concatenate([c3, b_pk[b - 1].astype(F32)], axis=0).astype(BF)

    lat0f = (lax.axis_index("lat") * ROWS).astype(F32)
    lon0f = (lax.axis_index("lon") * COLS).astype(F32)
    for b in range(NB):

        @pl.loop(1, nch[b])
        def _(c):
            slot = b * (NCH - 1) + c - 1
            pick = (row_id + (c * KC).astype(F32) == rank[b : b + 1, :]).astype(F32)
            a_more[slot], b_more[slot] = packed(pick.astype(BF), b)
            cell_tapers(pick, lat[b : b + 1, :], lon[b : b + 1, :], lat0f, lon0f, t_more, slot)

    zero_cols = jnp.zeros((8, ROWS * COLS), F32)

    def stack_x(i):
        x = xv[i]
        xh = hi(x)
        rhs[i] = jnp.concatenate([xh, xh, x - xh, zero_cols], axis=0).astype(BF)

    def put_q(i, q):
        qh, ql = split(q)
        q3[i] = jnp.concatenate([qh, qh, ql], axis=0)

    def add_chunk(a, s3, t):
        for i in range(VG):
            put_q(i, dot(a, rhs[i]) * t[...])
        for i in range(VG):
            xv[i] += dot(s3, q3[i])

    @pl.loop(0, NVAR // VG)
    def _(g):
        for i in range(VG):
            for r in range(ROWS):
                xv[i, :, r * COLS : (r + 1) * COLS] = x_ref[g * VG + i, r]

        @pl.loop(0, NB // 2)
        def _(pair):
            b = 2 * pair
            few = jnp.maximum(nch[b], nch[b + 1]) <= 1

            @pl.when(few)
            def _():
                a2 = a_pk[pl.ds(b, 2)].reshape(2 * KC, 128)
                for i in range(VG):
                    stack_x(i)
                for i in range(VG):
                    p = dot(a2, rhs[i])
                    p2[i] = p[KC:]
                    put_q(i, p[:KC] * t0_ref[b])
                for i in range(VG):
                    r = dot(l_pk[pair], q3[i])
                    xv[i] += r[KC:]
                    put_q(i, (p2[i] + r[:KC]) * t0_ref[b + 1])
                for i in range(VG):
                    xv[i] += dot(b_pk[b + 1], q3[i])

            @pl.when(jnp.logical_not(few))
            def _():
                @pl.loop(b, b + 2)
                def _(bb):
                    for i in range(VG):
                        stack_x(i)
                    add_chunk(a_pk[bb], b_pk[bb], t0_ref.at[bb])

                    @pl.loop(1, nch[bb])
                    def _(c):
                        slot = bb * (NCH - 1) + c - 1
                        add_chunk(a_more[slot], b_more[slot], t_more.at[slot])

        for i in range(VG):
            for r in range(ROWS):
                out_rows[
                    pl.ds((g * VG + i) * ROWS + r, MEMBERS, stride=NVAR * ROWS), :
                ] = xv[i, :, r * COLS : (r + 1) * COLS]
        store(g).start()

    for g in range(NVAR // VG):
        store(g).wait()


def analysis(x, y, rank, t0, pairs, obs):
    vm = pl.BlockSpec(memory_space=pltpu.VMEM)
    hbm = pl.BlockSpec(memory_space=pltpu.HBM)
    more = NB * (NCH - 1)
    dma = pltpu.SemaphoreType.DMA
    return pl.pallas_call(
        analysis_kernel,
        out_shape=jax.ShapeDtypeStruct((MEMBERS, NVAR, ROWS, COLS), F32),
        in_specs=[vm] * 6,
        out_specs=hbm,
        scratch_shapes=[
            pltpu.VMEM((MEMBERS, NVAR, ROWS, COLS), F32),
            pltpu.VMEM((MEMBERS, NB * BLOCK), F32),
            pltpu.VMEM((NB, BLOCK, 128), BF),
            pltpu.VMEM((NB, MEMBERS, 256), BF),
            pltpu.VMEM((NB, KC, 128), BF),
            pltpu.VMEM((NB, MEMBERS, 3 * KC), BF),
            pltpu.VMEM((NB // 2, KC + MEMBERS, 3 * KC), BF),
            pltpu.VMEM((more, KC, 128), BF),
            pltpu.VMEM((more, MEMBERS, 3 * KC), BF),
            pltpu.VMEM((more, KC, ROWS * COLS), F32),
            pltpu.VMEM((VG, MEMBERS, ROWS * COLS), F32),
            pltpu.VMEM((VG, 128, ROWS * COLS), BF),
            pltpu.VMEM((VG, KC, ROWS * COLS), F32),
            pltpu.VMEM((VG, 3 * KC, ROWS * COLS), BF),
            pltpu.SMEM((NB,), jnp.int32),
            dma((NVAR // VG,)),
        ],
        compiler_params=pltpu.CompilerParams(vmem_limit_bytes=22 << 20),
        name="analysis",
    )(x, y, rank, t0, pairs, obs)


def solution(mesh):
    nlat, nlon = mesh.shape["lat"], mesh.shape["lon"]
    assert nlon == 2 * NB

    def body(prognostic_samples, wind, obs_lat, obs_lon, obs_var, obs_value, obs_error):
        hbm = [
            pltpu.with_memory_space_constraint(a, pltpu.HBM)
            for a in (prognostic_samples, wind, obs_lat, obs_lon, obs_var, obs_value, obs_error)
        ]
        return analysis(*forecast(*hbm, nlat, nlon))

    in_specs = (P(None, None, "lat", "lon"), P(None, "lat", "lon"), P(), P(), P(), P(), P())
    out_specs = P(None, None, "lat", "lon")
    return jax.shard_map(body, mesh=mesh, in_specs=in_specs, out_specs=out_specs, check_vma=False)
```

```python
import jax
import jax.numpy as jnp
from jax import lax
from jax.experimental import pallas as pl
from jax.experimental.pallas import tpu as pltpu
from jax.sharding import PartitionSpec as P

MEMBERS, NVAR, ROWS, COLS = 40, 25, 8, 128
NLON = 2048
GROUPS, OBS = 2, 512
NB, BLOCK = 8, 128
PER = OBS // BLOCK
LOC = 32.0
DIFFUSE = 0.1
VS = 5
NVG = NVAR // VS
MG = MEMBERS // 8
SIDE = (ROWS + 2) // 3
PIECE = 24
KC = 32
NCH = BLOCK // KC
VG = 5
F32, BF = jnp.float32, jnp.bfloat16
MESH = pl.DeviceIdType.MESH


def hi(x):
    return x.astype(BF).astype(F32)


def split(x):
    high = x.astype(BF)
    return high, (x - high.astype(F32)).astype(BF)


def dot(a, b, dims=((1,), (0,))):
    return lax.dot_general(a, b, (dims, ((), ())), preferred_element_type=F32)


def peers(nlat, nlon):
    me_lat = lax.axis_index("lat")
    me_lon = lax.axis_index("lon")

    def place(dlat, dlon):
        lat = lax.rem(me_lat + (dlat + nlat), nlat) if dlat else me_lat
        lon = lax.rem(me_lon + (dlon + nlon), nlon) if dlon else me_lon
        return lat, lon

    def remote(src, dst, ssem, rsem, dlat, dlon):
        return pltpu.make_async_remote_copy(
            src_ref=src,
            dst_ref=dst,
            send_sem=ssem,
            recv_sem=rsem,
            device_id=place(dlat, dlon),
            device_id_type=MESH,
        )

    def signal(barrier, offsets):
        for o in offsets:
            pl.semaphore_signal(barrier, inc=1, device_id=place(*o), device_id_type=MESH)

    return me_lat, me_lon, place, remote, signal


def taper_sq(d2):
    z = jnp.sqrt(d2) * (1.0 / LOC)
    inner = (((-0.25 * z + 0.5) * z + 0.625) * z - 5.0 / 3.0) * z * z + 1.0
    outer = (
        ((((z * (1.0 / 12.0) - 0.5) * z + 0.625) * z + 5.0 / 3.0) * z - 5.0) * z
        + 4.0
        - (2.0 / 3.0) / jnp.maximum(z, 1.0)
    )
    return jnp.where(z <= 1.0, inner, jnp.where(z < 2.0, outer, 0.0))


def by_block(ref):
    parts = []
    for b in range(NB):
        first = (b % PER) * BLOCK
        parts.append(ref[b // PER : b // PER + 1, first : first + BLOCK])
    return jnp.concatenate(parts, axis=0)


def pair_at(b, j):
    return b * (2 * NB - b - 1) // 2 + j - b - 1


def cell_tapers(pick, lat_row, lon_row, lat0f, lon0f, out, slot):
    col_f = lax.broadcasted_iota(jnp.int32, (KC, COLS), 1).astype(F32) + lon0f
    latc = jnp.sum(pick * lat_row, axis=1, keepdims=True)
    lonc = jnp.sum(pick * lon_row, axis=1, keepdims=True)
    dlon = jnp.abs(lonc - col_f)
    dlon = jnp.minimum(dlon, NLON - dlon)
    dlon = dlon * dlon
    for r in range(ROWS):
        dlat = latc - (lat0f + float(r))
        out[slot, :, r * COLS : (r + 1) * COLS] = taper_sq(dlon + dlat * dlat)


def reach_tables(lat, lon, lat0f, lon0f, rank_ref, t0_ref):
    dy = jnp.maximum(jnp.maximum(lat0f - lat, lat - (lat0f + (ROWS - 1))), 0.0)
    off = lon - lon0f
    off = jnp.where(off < 0, off + NLON, off)
    dx = jnp.maximum(jnp.minimum(off - (COLS - 1), NLON - off), 0.0)
    reach = dx * dx + dy * dy < 4.0 * LOC * LOC
    before = (
        lax.broadcasted_iota(jnp.int32, (BLOCK, BLOCK), 0)
        < lax.broadcasted_iota(jnp.int32, (BLOCK, BLOCK), 1)
    ).astype(F32)
    rank = jnp.where(reach, dot(reach.astype(F32).astype(BF), before.astype(BF)), -1.0)
    rank_ref[...] = rank
    row_id = lax.broadcasted_iota(jnp.int32, (KC, BLOCK), 0).astype(F32)
    for b in range(NB):
        pick = (row_id == rank[b : b + 1, :]).astype(F32)
        cell_tapers(pick, lat[b : b + 1, :], lon[b : b + 1, :], lat0f, lon0f, t0_ref, b)


def pair_tables(lat, lon, pair_ref):
    lat_t, lon_t = lat.T, lon.T
    for b in range(NB):
        for j in range(b + 1, NB):
            dlat = lat_t[:, b : b + 1] - lat[j : j + 1, :]
            dlon = jnp.abs(lon_t[:, b : b + 1] - lon[j : j + 1, :])
            dlon = jnp.minimum(dlon, NLON - dlon)
            pair_ref[pair_at(b, j)] = taper_sq(dlat * dlat + dlon * dlon)


def forecast_kernel(
    nlat, nlon,
    x_hbm, wind_hbm, lat_hbm, lon_hbm, var_hbm, val_hbm, err_hbm,
    xf, out, rank_ref, t0_ref, pair_ref, obs_ref,
    xb, wind_ref, lat_ref, lon_ref, var_ref, val_ref, err_ref, desc, desc_s, xft, yo, part, line, block_sum, got_a, got_b,
    xt, edge, edge_w, edge_e, corner, wind_n, halo, halo_s, halo1_s, coef, shift, unit, q1_s, to_edge, at8,
    s_row, r_row, s_edge, r_edge, s_corner, r_corner, s_wind, r_wind,
    send, send_a, recv_a, recv_b, recv_c, l_x, l_small,
):
    def fetch(vg):
        vs = pl.ds(vg * VS, VS)
        return pltpu.make_async_copy(x_hbm.at[:, vs], xb.at[:, vs], l_x.at[vg])

    small = [
        pltpu.make_async_copy(a, b, l_small.at[i])
        for i, (a, b) in enumerate(
            [
                (wind_hbm, wind_ref), (lat_hbm, lat_ref), (lon_hbm, lon_ref),
                (var_hbm, var_ref), (val_hbm, val_ref), (err_hbm, err_ref),
            ]
        )
    ]
    for vg in range(NVG):
        fetch(vg).start()
    for c in small:
        c.start()
    x_ref = xb.reshape(MEMBERS * NVAR * ROWS, COLS)
    me_lat, me_lon, place, remote, signal = peers(nlat, nlon)
    barrier = pltpu.get_barrier_semaphore()
    near = [(o, 0) for o in range(1, nlat)] + [(0, o) for o in range(1, nlon)]
    near += [(-1, -1), (-1, 1), (1, -1), (1, 1)]
    signal(barrier, near)

    def column(r, mg, v):
        return x_ref[pl.ds(mg * (8 * NVAR * ROWS) + v * ROWS + r, 8, stride=NVAR * ROWS), :]

    def rows(vg, up):
        vs = pl.ds(vg * VS, VS)
        if up:
            return remote(
                xt.at[vs, 2:4],
                xt.at[vs, ROWS + 2 : ROWS + 4],
                s_row.at[vg, 0], r_row.at[vg, 0], -1, 0,
            )
        return remote(
            xt.at[vs, ROWS : ROWS + 2], xt.at[vs, 0:2], s_row.at[vg, 1], r_row.at[vg, 1], 1, 0
        )

    def send_rows(vg):
        rows(vg, True).start()
        rows(vg, False).start()

    def sent_rows(vg):
        rows(vg, True).wait_send()
        rows(vg, False).wait_send()

    winds = [
        remote(wind_ref, wind_n.at[i], s_wind.at[i], r_wind.at[i], dlat, dlon)
        for i, (dlat, dlon) in enumerate([(1, 0), (-1, 0), (0, 1), (0, -1)])
    ]
    edges = [
        remote(edge, edge_w, s_edge.at[0], r_edge.at[0], 0, 1),
        remote(edge, edge_e, s_edge.at[1], r_edge.at[1], 0, -1),
    ]
    corners = [
        remote(edge.at[ROWS - 1], corner.at[0], s_corner.at[0], r_corner.at[0], 1, 1),
        remote(edge.at[ROWS - 1], corner.at[1], s_corner.at[1], r_corner.at[1], 1, -1),
        remote(edge.at[0], corner.at[2], s_corner.at[2], r_corner.at[2], -1, 1),
        remote(edge.at[0], corner.at[3], s_corner.at[3], r_corner.at[3], -1, -1),
    ]
    for vg in range(NVG):
        fetch(vg).wait()

        @pl.loop(vg * VS, (vg + 1) * VS)
        def _(v):
            for r in (0, 1, ROWS - 2, ROWS - 1):
                for mg in range(MG):
                    xt[v, r + 2, mg * 8 : (mg + 1) * 8, :] = column(r, mg, v)

        if vg == 0:
            for c in small:
                c.wait()
            pl.semaphore_wait(barrier, len(near))
            for w in winds:
                w.start()
        if vg < 2:
            send_rows(vg)

    edge_src = lax.rem(lax.broadcasted_iota(jnp.int32, (2 * COLS, COLS), 0), COLS)
    edge_dst = lax.broadcasted_iota(jnp.int32, (2 * COLS, COLS), 1)
    outer = (edge_src < 2) | (edge_src >= COLS - 2)
    moved = jnp.where(outer, (edge_dst - edge_src) & (COLS - 1), -1)

    @pl.loop(0, NVG)
    def _(vg):
        for vi in range(VS):
            to_edge[vg, vi * 2 * COLS : (vi + 1) * 2 * COLS, :] = jnp.where(
                moved == 4 * (vg * VS + vi), 1.0, 0.0
            ).astype(BF)

    edge[...] = jnp.zeros_like(edge)

    @pl.loop(0, NVG)
    def _(vg):
        pieces = []
        for vi in range(VS):
            v = vg * VS + vi
            for r in range(2, ROWS - 2):
                for mg in range(MG):
                    xt[v, r + 2, mg * 8 : (mg + 1) * 8, :] = column(r, mg, v)
        for vi in range(VS):
            pieces += split(xt[vg * VS + vi, 2 : ROWS + 2].reshape(ROWS * MEMBERS, COLS))
        packed = dot(jnp.concatenate(pieces, axis=1), to_edge[vg])
        edge[...] += packed.reshape(ROWS, MEMBERS, COLS)

    for e in edges + corners:
        e.start()
    sent_rows(0)
    send_rows(2)

    lat_all, lon_all = lat_ref[...], lon_ref[...]
    owned = (lat_all // ROWS == me_lat) & (lon_all // COLS == me_lon)
    row_all = lat_all & (ROWS - 1)
    group = (row_all >= 3).astype(jnp.int32) + (row_all >= 6).astype(jnp.int32)
    part_of = row_all - 3 * group
    desc[...] = (var_ref[...] * SIDE + group) * COLS + (lon_all & (COLS - 1))
    to_scalar = pltpu.make_async_copy(desc, desc_s, l_small.at[6])
    to_scalar.start()
    at_all = jnp.where(owned, part_of, -1)
    for b in range(NB):
        cut = (b % PER) * BLOCK
        at8[b : b + 1, :] = at_all[b // PER : b // PER + 1, cut : cut + BLOCK]

    src = lax.rem(lax.broadcasted_iota(jnp.int32, (2 * COLS, 2 * COLS), 0), COLS)
    dst = lax.broadcasted_iota(jnp.int32, (2 * COLS, 2 * COLS), 1)
    east_of = (dst < COLS) & (src == dst + 1)
    west_of = (dst >= COLS) & (src == dst - COLS - 1)
    shift[...] = jnp.where(east_of | west_of, 1.0, 0.0).astype(BF)
    col_of = lax.rem(lax.broadcasted_iota(jnp.int32, (COLS, 2 * COLS), 1), COLS)
    row_of = lax.broadcasted_iota(jnp.int32, (COLS, 2 * COLS), 0)
    unit[...] = jnp.where(col_of == row_of, 1.0, 0.0).astype(BF)

    for w in winds:
        w.wait_recv()
    has_lo = (me_lat > 0).astype(F32)
    has_hi = (me_lat < nlat - 1).astype(F32)

    def row_wind(r):
        if r < 0:
            return wind_n[0, 0, ROWS - 1 : ROWS, :], wind_n[0, 1, ROWS - 1 : ROWS, :]
        if r == ROWS:
            return wind_n[1, 0, 0:1, :], wind_n[1, 1, 0:1, :]
        return wind_ref[0, r : r + 1, :], wind_ref[1, r : r + 1, :]

    def four(u, v, r):
        nxt, prv = DIFFUSE - 0.5 * v, DIFFUSE + 0.5 * v
        if r == 0:
            prv = prv * has_lo
        if r == ROWS - 1:
            nxt = nxt * has_hi
        return DIFFUSE - 0.5 * u, DIFFUSE + 0.5 * u, nxt, prv

    for r in range(-1, ROWS + 1):
        u, v = row_wind(r)
        for i, c in enumerate(four(u, v, r)):
            coef[i, r + 1] = jnp.broadcast_to(c, (8, COLS))

    sent_rows(1)
    send_rows(3)

    for e in edges + corners:
        e.wait_recv()
    lane4 = lax.rem(lax.broadcasted_iota(jnp.int32, (MEMBERS, COLS), 1), 4)
    from_west = lane4 >= 2
    halo[0] = jnp.where(from_west, corner[0], corner[1])
    halo[ROWS + 1] = jnp.where(from_west, corner[2], corner[3])
    for r in range(ROWS):
        halo[r + 1] = jnp.where(from_west, edge_w[r], edge_e[r])

    def beside(t):
        return jnp.where(lane4 == 0, t, pltpu.roll(t, 2, 1))

    for r in range(ROWS + 2):
        halo_s[r] = beside(halo[r])
    for r in range(ROWS):
        u, v = [
            jnp.where(
                from_west,
                jnp.broadcast_to(wind_n[2, i, r : r + 1, COLS - 1 : COLS], (MEMBERS, COLS)),
                jnp.broadcast_to(wind_n[3, i, r : r + 1, 0:1], (MEMBERS, COLS)),
            )
            for i in range(2)
        ]
        ce, cw, cn, cs = four(u, v, r)
        own, got = edge[r], halo[r + 1]
        east = pltpu.roll(jnp.where(lane4 == 0, own, got), COLS - 1, 1)
        west = pltpu.roll(jnp.where(lane4 == 3, own, got), 1, 1)
        after = (
            (1.0 - 4.0 * DIFFUSE) * got
            + ce * east
            + cw * west
            + cn * halo[r + 2]
            + cs * halo[r]
        )
        halo1_s[r] = beside(after)

    def step(q, nxt, prv, side, back, first, count):
        shape = (count, MG, 8, COLS)
        high, low = split(q)
        both = dot(jnp.concatenate([high, low], axis=1), shift[...])
        lane = lax.broadcasted_iota(jnp.int32, (count * MEMBERS, COLS), 1)
        beyond = pltpu.roll(side.reshape(count * MEMBERS, COLS), back, 1)
        east = jnp.where(lane == COLS - 1, beyond, both[:, :COLS])
        west = jnp.where(lane == 0, beyond, both[:, COLS:])
        c = [coef[i, first : first + count].reshape(count, 1, 8, COLS) for i in range(4)]
        new = (
            (1.0 - 4.0 * DIFFUSE) * q.reshape(shape)
            + c[0] * east.reshape(shape)
            + c[1] * west.reshape(shape)
            + c[2] * nxt.reshape(shape)
            + c[3] * prv.reshape(shape)
        )
        return new.reshape(count * MEMBERS, COLS)

    def block(ref, v, first, count):
        return ref[v, first : first + count].reshape(count * MEMBERS, COLS)

    @pl.loop(0, NVG)
    def _(vg):
        rows(vg, True).wait_recv()
        rows(vg, False).wait_recv()

        @pl.when(vg == 0)
        def _():
            sent_rows(2)
            send_rows(4)

        n1, n2 = ROWS + 2, ROWS
        for vi in range(VS):
            v = vg * VS + vi
            q1_s[vi] = step(
                block(xt, v, 1, n1), block(xt, v, 2, n1), block(xt, v, 0, n1),
                halo_s[...], (COLS - 1 - 4 * v) & (COLS - 1), 0, n1,
            ).reshape(n1, MEMBERS, COLS)
        for vi in range(VS):
            v = vg * VS + vi
            xf[v] = step(
                block(q1_s, vi, 1, n2), block(q1_s, vi, 2, n2), block(q1_s, vi, 0, n2),
                halo1_s[...], (COLS - 1 - 4 * v) & (COLS - 1), 1, n2,
            ).reshape(n2, MEMBERS, COLS)
        for vi in range(VS):
            v = vg * VS + vi
            both = jnp.concatenate(split(block(xf, v, 0, n2)), axis=1)
            for i in range(SIDE):
                n = min(3, ROWS - 3 * i) * MEMBERS
                xft[pl.ds((v * SIDE + i) * COLS, COLS), 0:n] = dot(
                    unit[...], both[i * 3 * MEMBERS : i * 3 * MEMBERS + n, :], ((1,), (1,))
                )

    to_scalar.wait()
    half, odd = me_lon // 2, lax.rem(me_lon, 2)

    def piece(i, h, b):
        return pltpu.make_async_remote_copy(
            src_ref=part.at[2 * b + h],
            dst_ref=got_a.at[i, odd],
            send_sem=send_a.at[i, h],
            recv_sem=recv_a.at[i, odd],
            device_id=(me_lat, 2 * b + h),
            device_id_type=MESH,
        )

    def arrival(i, p):
        return pltpu.make_async_remote_copy(
            src_ref=part.at[0],
            dst_ref=got_a.at[i, p],
            send_sem=send_a.at[i, 0],
            recv_sem=recv_a.at[i, p],
            device_id=(me_lat, lax.rem(me_lon + 1, nlon)),
            device_id_type=MESH,
        )

    first = []
    for i in list(range(1, NB)) + [0]:
        b = lax.rem(half + i, NB)

        @pl.loop(0, BLOCK // 8)
        def _(g):
            for j in range(8):
                k = g * 8 + j
                at = desc_s[b // PER, lax.rem(b, PER) * BLOCK + k]
                yo[i, pl.ds(k, 1), :] = xft[pl.ds(at, 1), :]

        turned = yo[i].T
        at = jnp.broadcast_to(at8[pl.ds(b, 1), :], (MEMBERS, BLOCK))
        mine = jnp.zeros((MEMBERS, BLOCK), F32)
        for n in range(3):
            mine = jnp.where(at == n, turned[n * MEMBERS : (n + 1) * MEMBERS, :], mine)
        part[2 * b] = mine[0:PIECE]
        part[2 * b + 1] = jnp.concatenate(
            [mine[PIECE:], jnp.zeros((2 * PIECE - MEMBERS, BLOCK), F32)], axis=0
        )
        for h in (0, 1) if i else (1 - odd,):
            c = piece(i, h, b)
            c.start()
            first.append(c)
    lat_f, lon_f = by_block(lat_ref).astype(F32), by_block(lon_ref).astype(F32)
    lat0f, lon0f = (me_lat * ROWS).astype(F32), (me_lon * COLS).astype(F32)
    for i, t in enumerate([lat_f, lon_f, by_block(val_ref), by_block(err_ref)]):
        obs_ref[i] = t
    reach_tables(lat_f, lon_f, lat0f, lon0f, rank_ref, t0_ref)
    total = part[me_lon]
    for i in range(1, NB):
        for p in (0, 1):
            arrival(i, p).wait_recv()
            total = total + got_a[i, p]
    arrival(0, 1 - odd).wait_recv()
    total = total + got_a[0, 1 - odd]
    line[...] = total
    second = [
        remote(line, got_b.at[o - 1], send.at[o - 1], recv_b.at[o - 1], o, 0)
        for o in range(1, nlat)
    ]
    for c in second:
        c.start()
    for i, c in enumerate(second):
        c.wait_recv()
        total = total + got_b[i]
    block_sum[...] = total
    third = [
        remote(block_sum, out.at[me_lon], send.at[nlat + o - 2], recv_c.at[o - 1], 0, o)
        for o in range(1, nlon)
    ]
    for c in third:
        c.start()
    out[me_lon] = total
    pair_tables(lat_f, lon_f, pair_ref)
    for c in third:
        c.wait_recv()

    for c in winds + edges + corners + first + second + third:
        c.wait_send()

    sent_rows(3)
    sent_rows(4)


def forecast(x, wind, lat, lon, var, val, err, nlat, nlon):
    vm = pl.BlockSpec(memory_space=pltpu.VMEM)
    dma = pltpu.SemaphoreType.DMA
    return pl.pallas_call(
        lambda *refs: forecast_kernel(nlat, nlon, *refs),
        out_shape=(
            jax.ShapeDtypeStruct((NVAR, ROWS, MEMBERS, COLS), F32),
            jax.ShapeDtypeStruct((2 * NB, PIECE, BLOCK), F32),
            jax.ShapeDtypeStruct((NB, BLOCK), F32),
            jax.ShapeDtypeStruct((NB, KC, ROWS * COLS), F32),
            jax.ShapeDtypeStruct((NB * (NB - 1) // 2, BLOCK, BLOCK), F32),
            jax.ShapeDtypeStruct((4, NB, BLOCK), F32),
        ),
        in_specs=[pl.BlockSpec(memory_space=pltpu.HBM)] * 7,
        out_specs=(vm,) * 6,
        scratch_shapes=[
            pltpu.VMEM((MEMBERS, NVAR, ROWS, COLS), F32),
            pltpu.VMEM((2, ROWS, COLS), F32),
            pltpu.VMEM((GROUPS, OBS), jnp.int32),
            pltpu.VMEM((GROUPS, OBS), jnp.int32),
            pltpu.VMEM((GROUPS, OBS), jnp.int32),
            pltpu.VMEM((GROUPS, OBS), F32),
            pltpu.VMEM((GROUPS, OBS), F32),
            pltpu.VMEM((GROUPS, OBS), jnp.int32),
            pltpu.SMEM((GROUPS, OBS), jnp.int32),
            pltpu.VMEM((NVAR * SIDE * COLS, COLS), F32),
            pltpu.VMEM((NB, BLOCK, COLS), F32),
            pltpu.VMEM((2 * NB, PIECE, BLOCK), F32),
            pltpu.VMEM((PIECE, BLOCK), F32),
            pltpu.VMEM((PIECE, BLOCK), F32),
            pltpu.VMEM((NB, 2, PIECE, BLOCK), F32),
            pltpu.VMEM((nlat - 1, PIECE, BLOCK), F32),
            pltpu.VMEM((NVAR, ROWS + 4, MEMBERS, COLS), F32),
            pltpu.VMEM((ROWS, MEMBERS, COLS), F32),
            pltpu.VMEM((ROWS, MEMBERS, COLS), F32),
            pltpu.VMEM((ROWS, MEMBERS, COLS), F32),
            pltpu.VMEM((4, MEMBERS, COLS), F32),
            pltpu.VMEM((4, 2, ROWS, COLS), F32),
            pltpu.VMEM((ROWS + 2, MEMBERS, COLS), F32),
            pltpu.VMEM((ROWS + 2, MEMBERS, COLS), F32),
            pltpu.VMEM((ROWS, MEMBERS, COLS), F32),
            pltpu.VMEM((4, ROWS + 2, 8, COLS), F32),
            pltpu.VMEM((2 * COLS, 2 * COLS), BF),
            pltpu.VMEM((COLS, 2 * COLS), BF),
            pltpu.VMEM((VS, ROWS + 2, MEMBERS, COLS), F32),
            pltpu.VMEM((NVG, VS * 2 * COLS, COLS), BF),
            pltpu.VMEM((NB, BLOCK), jnp.int32),
            dma((NVG, 2)), dma((NVG, 2)), dma((2,)), dma((2,)),
            dma((4,)), dma((4,)), dma((4,)), dma((4,)),
            dma((nlat + nlon - 2,)), dma((NB, 2)), dma((NB, 2)), dma((nlat - 1,)), dma((nlon - 1,)),
            dma((NVG,)), dma((7,)),
        ],
        compiler_params=pltpu.CompilerParams(
            collective_id=0, has_side_effects=True, vmem_limit_bytes=34 << 20
        ),
        name="forecast",
    )(x, wind, lat, lon, var, val, err)


def analysis_kernel(
    x_ref, y_ref, rank_ref, t0_ref, pair_ref, obs_ref,
    out_hbm,
    ob,
    ys, a_all, s_all, a_pk, b_pk, l_pk, a_more, b_more, t_more, xv, rhs, p2, q3, nch,
    l_out,
):
    out_rows = ob.reshape(MEMBERS * NVAR * ROWS, COLS)

    def store(g):
        vs = pl.ds(g * VG, VG)
        return pltpu.make_async_copy(ob.at[:, vs], out_hbm.at[:, vs], l_out.at[g])

    rank = rank_ref[...]
    for b in range(NB):
        top = jnp.max(rank[b : b + 1, :])
        nch[b] = ((top + KC) * (1.0 / KC)).astype(jnp.int32)
        ys[0:PIECE, b * BLOCK : (b + 1) * BLOCK] = y_ref[2 * b]
        ys[PIECE:, b * BLOCK : (b + 1) * BLOCK] = y_ref[2 * b + 1][0 : MEMBERS - PIECE]
    lat, lon, values, variances = [obs_ref[i] for i in range(4)]
    row_id = lax.broadcasted_iota(jnp.int32, (KC, BLOCK), 0).astype(F32)
    lane96 = lax.broadcasted_iota(jnp.int32, (KC, 3 * KC), 1)
    zero8 = jnp.zeros((8, BLOCK), F32)

    def packed(pick, b):
        zero = jnp.zeros_like(pick)
        pick3 = jnp.concatenate(
            [
                jnp.concatenate([pick, zero], axis=1),
                jnp.concatenate([zero, pick], axis=1),
                jnp.concatenate([pick, zero], axis=1),
            ],
            axis=0,
        )
        return dot(pick, a_all[b]).astype(BF), dot(s_all[b], pick3, ((1,), (1,))).astype(BF)

    stacked = None
    for b in range(NB):
        prior = ys[:, b * BLOCK : (b + 1) * BLOCK]
        average = jnp.sum(prior, axis=0, keepdims=True) * (1.0 / MEMBERS)
        anomaly = prior - average
        spread = jnp.sum(anomaly * anomaly, axis=0, keepdims=True) / (MEMBERS - 1)
        errors = variances[b : b + 1, :]
        total = spread + errors
        weights = anomaly * (1.0 / ((MEMBERS - 1) * total))
        shifts = (values[b : b + 1, :] - average) - anomaly * (
            1.0 / (1.0 + jnp.sqrt(errors / total))
        )
        wh = hi(weights)
        a = jnp.concatenate([wh, weights - wh, wh, zero8], axis=0).T.astype(BF)
        sh, sl = split(shifts)
        a_all[b] = a
        s_all[b] = jnp.concatenate([sh, sl], axis=1)
        s3 = jnp.concatenate([sh, sl, sh], axis=1)
        for j in range(b + 1, NB):
            yl = ys[:, j * BLOCK : (j + 1) * BLOCK]
            yh = hi(yl)
            y3 = jnp.concatenate([yh, yh, yl - yh, zero8], axis=0).astype(BF)
            qh, ql = split(dot(a, y3) * pair_ref[pair_at(b, j)])
            ys[:, j * BLOCK : (j + 1) * BLOCK] = yl + dot(
                s3, jnp.concatenate([qh, qh, ql], axis=0)
            )
        pick = (row_id == rank[b : b + 1, :]).astype(BF)
        a_pk[b], b_pk[b] = packed(pick, b)
        if b % 2 == 0:
            sh32 = sh.astype(F32)
            s_rows = jnp.concatenate([sh32, sh32, sl.astype(F32), zero8], axis=0).astype(BF)
            stacked = dot(s_rows, jnp.concatenate([pick] * 3, axis=0), ((1,), (1,))).astype(BF)
        else:
            c = dot(a_pk[b], stacked)
            ch = hi(c)
            c3 = jnp.where((lane96 >= KC) & (lane96 < 2 * KC), c - ch, ch)
            l_pk[b // 2] = jnp.concatenate([c3, b_pk[b - 1].astype(F32)], axis=0).astype(BF)

    lat0f = (lax.axis_index("lat") * ROWS).astype(F32)
    lon0f = (lax.axis_index("lon") * COLS).astype(F32)
    for b in range(NB):

        @pl.loop(1, nch[b])
        def _(c):
            slot = b * (NCH - 1) + c - 1
            pick = (row_id + (c * KC).astype(F32) == rank[b : b + 1, :]).astype(F32)
            a_more[slot], b_more[slot] = packed(pick.astype(BF), b)
            cell_tapers(pick, lat[b : b + 1, :], lon[b : b + 1, :], lat0f, lon0f, t_more, slot)

    zero_cols = jnp.zeros((8, ROWS * COLS), F32)

    def stack_x(i):
        x = xv[i]
        xh = hi(x)
        rhs[i] = jnp.concatenate([xh, xh, x - xh, zero_cols], axis=0).astype(BF)

    def put_q(i, q):
        qh, ql = split(q)
        q3[i] = jnp.concatenate([qh, qh, ql], axis=0)

    def add_chunk(a, s3, t):
        for i in range(VG):
            put_q(i, dot(a, rhs[i]) * t[...])
        for i in range(VG):
            xv[i] += dot(s3, q3[i])

    @pl.loop(0, NVAR // VG)
    def _(g):
        for i in range(VG):
            for r in range(ROWS):
                xv[i, :, r * COLS : (r + 1) * COLS] = x_ref[g * VG + i, r]

        @pl.loop(0, NB // 2)
        def _(pair):
            b = 2 * pair
            few = jnp.maximum(nch[b], nch[b + 1]) <= 1

            @pl.when(few)
            def _():
                a2 = a_pk[pl.ds(b, 2)].reshape(2 * KC, 128)
                for i in range(VG):
                    stack_x(i)
                for i in range(VG):
                    p = dot(a2, rhs[i])
                    p2[i] = p[KC:]
                    put_q(i, p[:KC] * t0_ref[b])
                for i in range(VG):
                    r = dot(l_pk[pair], q3[i])
                    xv[i] += r[KC:]
                    put_q(i, (p2[i] + r[:KC]) * t0_ref[b + 1])
                for i in range(VG):
                    xv[i] += dot(b_pk[b + 1], q3[i])

            @pl.when(jnp.logical_not(few))
            def _():
                @pl.loop(b, b + 2)
                def _(bb):
                    for i in range(VG):
                        stack_x(i)
                    add_chunk(a_pk[bb], b_pk[bb], t0_ref.at[bb])

                    @pl.loop(1, nch[bb])
                    def _(c):
                        slot = bb * (NCH - 1) + c - 1
                        add_chunk(a_more[slot], b_more[slot], t_more.at[slot])

        for i in range(VG):
            for r in range(ROWS):
                out_rows[
                    pl.ds((g * VG + i) * ROWS + r, MEMBERS, stride=NVAR * ROWS), :
                ] = xv[i, :, r * COLS : (r + 1) * COLS]
        store(g).start()

    for g in range(NVAR // VG):
        store(g).wait()


def analysis(x, y, rank, t0, pairs, obs):
    vm = pl.BlockSpec(memory_space=pltpu.VMEM)
    hbm = pl.BlockSpec(memory_space=pltpu.HBM)
    more = NB * (NCH - 1)
    dma = pltpu.SemaphoreType.DMA
    return pl.pallas_call(
        analysis_kernel,
        out_shape=jax.ShapeDtypeStruct((MEMBERS, NVAR, ROWS, COLS), F32),
        in_specs=[vm] * 6,
        out_specs=hbm,
        scratch_shapes=[
            pltpu.VMEM((MEMBERS, NVAR, ROWS, COLS), F32),
            pltpu.VMEM((MEMBERS, NB * BLOCK), F32),
            pltpu.VMEM((NB, BLOCK, 128), BF),
            pltpu.VMEM((NB, MEMBERS, 256), BF),
            pltpu.VMEM((NB, KC, 128), BF),
            pltpu.VMEM((NB, MEMBERS, 3 * KC), BF),
            pltpu.VMEM((NB // 2, KC + MEMBERS, 3 * KC), BF),
            pltpu.VMEM((more, KC, 128), BF),
            pltpu.VMEM((more, MEMBERS, 3 * KC), BF),
            pltpu.VMEM((more, KC, ROWS * COLS), F32),
            pltpu.VMEM((VG, MEMBERS, ROWS * COLS), F32),
            pltpu.VMEM((VG, 128, ROWS * COLS), BF),
            pltpu.VMEM((VG, KC, ROWS * COLS), F32),
            pltpu.VMEM((VG, 3 * KC, ROWS * COLS), BF),
            pltpu.SMEM((NB,), jnp.int32),
            dma((NVAR // VG,)),
        ],
        compiler_params=pltpu.CompilerParams(vmem_limit_bytes=22 << 20),
        name="analysis",
    )(x, y, rank, t0, pairs, obs)


def solution(mesh):
    nlat, nlon = mesh.shape["lat"], mesh.shape["lon"]
    assert nlon == 2 * NB

    def body(prognostic_samples, wind, obs_lat, obs_lon, obs_var, obs_value, obs_error):
        hbm = [
            pltpu.with_memory_space_constraint(a, pltpu.HBM)
            for a in (prognostic_samples, wind, obs_lat, obs_lon, obs_var, obs_value, obs_error)
        ]
        return analysis(*forecast(*hbm, nlat, nlon))

    in_specs = (P(None, None, "lat", "lon"), P(None, "lat", "lon"), P(), P(), P(), P(), P())
    out_specs = P(None, None, "lat", "lon")
    return jax.shard_map(body, mesh=mesh, in_specs=in_specs, out_specs=out_specs, check_vma=False)
```

```python
import jax
import jax.numpy as jnp
from jax import lax
from jax.experimental import pallas as pl
from jax.experimental.pallas import tpu as pltpu
from jax.sharding import PartitionSpec as P

MEMBERS, NVAR, ROWS, COLS = 40, 25, 8, 128
NLON = 2048
GROUPS, OBS = 2, 512
NB, BLOCK = 8, 128
PER = OBS // BLOCK
LOC = 32.0
DIFFUSE = 0.1
VS = 5
NVG = NVAR // VS
MG = MEMBERS // 8
SIDE = (ROWS + 2) // 3
PIECE = 24
KC = 32
NCH = BLOCK // KC
VG = 5
F32, BF = jnp.float32, jnp.bfloat16
MESH = pl.DeviceIdType.MESH


def hi(x):
    return x.astype(BF).astype(F32)


def split(x):
    high = x.astype(BF)
    return high, (x - high.astype(F32)).astype(BF)


def dot(a, b, dims=((1,), (0,))):
    return lax.dot_general(a, b, (dims, ((), ())), preferred_element_type=F32)


def peers(nlat, nlon):
    me_lat = lax.axis_index("lat")
    me_lon = lax.axis_index("lon")

    def place(dlat, dlon):
        lat = lax.rem(me_lat + (dlat + nlat), nlat) if dlat else me_lat
        lon = lax.rem(me_lon + (dlon + nlon), nlon) if dlon else me_lon
        return lat, lon

    def remote(src, dst, ssem, rsem, dlat, dlon):
        return pltpu.make_async_remote_copy(
            src_ref=src,
            dst_ref=dst,
            send_sem=ssem,
            recv_sem=rsem,
            device_id=place(dlat, dlon),
            device_id_type=MESH,
        )

    def signal(barrier, offsets):
        for o in offsets:
            pl.semaphore_signal(barrier, inc=1, device_id=place(*o), device_id_type=MESH)

    return me_lat, me_lon, place, remote, signal


def taper_sq(d2):
    z = jnp.sqrt(d2) * (1.0 / LOC)
    inner = (((-0.25 * z + 0.5) * z + 0.625) * z - 5.0 / 3.0) * z * z + 1.0
    outer = (
        ((((z * (1.0 / 12.0) - 0.5) * z + 0.625) * z + 5.0 / 3.0) * z - 5.0) * z
        + 4.0
        - (2.0 / 3.0) / jnp.maximum(z, 1.0)
    )
    return jnp.where(z <= 1.0, inner, jnp.where(z < 2.0, outer, 0.0))


def by_block(ref):
    parts = []
    for b in range(NB):
        first = (b % PER) * BLOCK
        parts.append(ref[b // PER : b // PER + 1, first : first + BLOCK])
    return jnp.concatenate(parts, axis=0)


def pair_at(b, j):
    return b * (2 * NB - b - 1) // 2 + j - b - 1


def cell_tapers(pick, lat_row, lon_row, lat0f, lon0f, out, slot):
    col_f = lax.broadcasted_iota(jnp.int32, (KC, COLS), 1).astype(F32) + lon0f
    latc = jnp.sum(pick * lat_row, axis=1, keepdims=True)
    lonc = jnp.sum(pick * lon_row, axis=1, keepdims=True)
    dlon = jnp.abs(lonc - col_f)
    dlon = jnp.minimum(dlon, NLON - dlon)
    dlon = dlon * dlon
    for r in range(ROWS):
        dlat = latc - (lat0f + float(r))
        out[slot, :, r * COLS : (r + 1) * COLS] = taper_sq(dlon + dlat * dlat)


def reach_tables(lat, lon, lat0f, lon0f, rank_ref, t0_ref):
    dy = jnp.maximum(jnp.maximum(lat0f - lat, lat - (lat0f + (ROWS - 1))), 0.0)
    off = lon - lon0f
    off = jnp.where(off < 0, off + NLON, off)
    dx = jnp.maximum(jnp.minimum(off - (COLS - 1), NLON - off), 0.0)
    reach = dx * dx + dy * dy < 4.0 * LOC * LOC
    before = (
        lax.broadcasted_iota(jnp.int32, (BLOCK, BLOCK), 0)
        < lax.broadcasted_iota(jnp.int32, (BLOCK, BLOCK), 1)
    ).astype(F32)
    rank = jnp.where(reach, dot(reach.astype(F32).astype(BF), before.astype(BF)), -1.0)
    rank_ref[...] = rank
    row_id = lax.broadcasted_iota(jnp.int32, (KC, BLOCK), 0).astype(F32)
    for b in range(NB):
        pick = (row_id == rank[b : b + 1, :]).astype(F32)
        cell_tapers(pick, lat[b : b + 1, :], lon[b : b + 1, :], lat0f, lon0f, t0_ref, b)


def pair_tables(lat, lon, pair_ref):
    lat_t, lon_t = lat.T, lon.T
    for b in range(NB):
        for j in range(b + 1, NB):
            dlat = lat_t[:, b : b + 1] - lat[j : j + 1, :]
            dlon = jnp.abs(lon_t[:, b : b + 1] - lon[j : j + 1, :])
            dlon = jnp.minimum(dlon, NLON - dlon)
            pair_ref[pair_at(b, j)] = taper_sq(dlat * dlat + dlon * dlon)


def forecast_kernel(
    nlat, nlon,
    x_hbm, wind_hbm, lat_hbm, lon_hbm, var_hbm, val_hbm, err_hbm,
    xf, out, rank_ref, t0_ref, pair_ref, obs_ref,
    xb, wind_ref, lat_ref, lon_ref, var_ref, val_ref, err_ref, desc, desc_s, xft, yo, part, line, block_sum, got_a, got_b,
    xt, edge, edge_w, edge_e, corner, wind_n, halo, halo_s, halo1_s, coef, shift, unit, q1_s, both_s, to_edge, at8,
    s_row, r_row, s_edge, r_edge, s_corner, r_corner, s_wind, r_wind,
    send, send_a, recv_a, recv_b, recv_c, l_x, l_small,
):
    def fetch(vg):
        vs = pl.ds(vg * VS, VS)
        return pltpu.make_async_copy(x_hbm.at[:, vs], xb.at[:, vs], l_x.at[vg])

    small = [
        pltpu.make_async_copy(a, b, l_small.at[i])
        for i, (a, b) in enumerate(
            [
                (wind_hbm, wind_ref), (lat_hbm, lat_ref), (lon_hbm, lon_ref),
                (var_hbm, var_ref), (val_hbm, val_ref), (err_hbm, err_ref),
            ]
        )
    ]
    for vg in range(NVG):
        fetch(vg).start()
    for c in small:
        c.start()
    x_ref = xb.reshape(MEMBERS * NVAR * ROWS, COLS)
    me_lat, me_lon, place, remote, signal = peers(nlat, nlon)
    barrier = pltpu.get_barrier_semaphore()
    near = [(o, 0) for o in range(1, nlat)] + [(0, o) for o in range(1, nlon)]
    near += [(-1, -1), (-1, 1), (1, -1), (1, 1)]
    signal(barrier, near)

    def column(r, mg, v):
        return x_ref[pl.ds(mg * (8 * NVAR * ROWS) + v * ROWS + r, 8, stride=NVAR * ROWS), :]

    def rows(vg, up):
        vs = pl.ds(vg * VS, VS)
        if up:
            return remote(
                xt.at[vs, 2:4],
                xt.at[vs, ROWS + 2 : ROWS + 4],
                s_row.at[vg, 0], r_row.at[vg, 0], -1, 0,
            )
        return remote(
            xt.at[vs, ROWS : ROWS + 2], xt.at[vs, 0:2], s_row.at[vg, 1], r_row.at[vg, 1], 1, 0
        )

    def send_rows(vg):
        rows(vg, True).start()
        rows(vg, False).start()

    def sent_rows(vg):
        rows(vg, True).wait_send()
        rows(vg, False).wait_send()

    winds = [
        remote(wind_ref, wind_n.at[i], s_wind.at[i], r_wind.at[i], dlat, dlon)
        for i, (dlat, dlon) in enumerate([(1, 0), (-1, 0), (0, 1), (0, -1)])
    ]
    edges = [
        remote(edge, edge_w, s_edge.at[0], r_edge.at[0], 0, 1),
        remote(edge, edge_e, s_edge.at[1], r_edge.at[1], 0, -1),
    ]
    corners = [
        remote(edge.at[ROWS - 1], corner.at[0], s_corner.at[0], r_corner.at[0], 1, 1),
        remote(edge.at[ROWS - 1], corner.at[1], s_corner.at[1], r_corner.at[1], 1, -1),
        remote(edge.at[0], corner.at[2], s_corner.at[2], r_corner.at[2], -1, 1),
        remote(edge.at[0], corner.at[3], s_corner.at[3], r_corner.at[3], -1, -1),
    ]
    for vg in range(NVG):
        fetch(vg).wait()

        @pl.loop(vg * VS, (vg + 1) * VS)
        def _(v):
            for r in (0, 1, ROWS - 2, ROWS - 1):
                for mg in range(MG):
                    xt[v, r + 2, mg * 8 : (mg + 1) * 8, :] = column(r, mg, v)

        if vg == 0:
            for c in small:
                c.wait()
            pl.semaphore_wait(barrier, len(near))
            for w in winds:
                w.start()
        if vg < 2:
            send_rows(vg)

    edge_src = lax.rem(lax.broadcasted_iota(jnp.int32, (2 * COLS, COLS), 0), COLS)
    edge_dst = lax.broadcasted_iota(jnp.int32, (2 * COLS, COLS), 1)
    outer = (edge_src < 2) | (edge_src >= COLS - 2)
    moved = jnp.where(outer, (edge_dst - edge_src) & (COLS - 1), -1)

    @pl.loop(0, NVG)
    def _(vg):
        for vi in range(VS):
            to_edge[vg, vi * 2 * COLS : (vi + 1) * 2 * COLS, :] = jnp.where(
                moved == 4 * (vg * VS + vi), 1.0, 0.0
            ).astype(BF)

    edge[...] = jnp.zeros_like(edge)

    @pl.loop(0, NVG)
    def _(vg):
        pieces = []
        for vi in range(VS):
            v = vg * VS + vi
            for r in range(2, ROWS - 2):
                for mg in range(MG):
                    xt[v, r + 2, mg * 8 : (mg + 1) * 8, :] = column(r, mg, v)
        for vi in range(VS):
            pieces += split(xt[vg * VS + vi, 2 : ROWS + 2].reshape(ROWS * MEMBERS, COLS))
        packed = dot(jnp.concatenate(pieces, axis=1), to_edge[vg])
        edge[...] += packed.reshape(ROWS, MEMBERS, COLS)

    for e in edges + corners:
        e.start()
    sent_rows(0)
    send_rows(2)

    lat_all, lon_all = lat_ref[...], lon_ref[...]
    owned = (lat_all // ROWS == me_lat) & (lon_all // COLS == me_lon)
    row_all = lat_all & (ROWS - 1)
    group = (row_all >= 3).astype(jnp.int32) + (row_all >= 6).astype(jnp.int32)
    part_of = row_all - 3 * group
    desc[...] = (var_ref[...] * SIDE + group) * COLS + (lon_all & (COLS - 1))
    to_scalar = pltpu.make_async_copy(desc, desc_s, l_small.at[6])
    to_scalar.start()
    at_all = jnp.where(owned, part_of, -1)
    for b in range(NB):
        cut = (b % PER) * BLOCK
        at8[b : b + 1, :] = at_all[b // PER : b // PER + 1, cut : cut + BLOCK]

    src = lax.rem(lax.broadcasted_iota(jnp.int32, (2 * COLS, 2 * COLS), 0), COLS)
    dst = lax.broadcasted_iota(jnp.int32, (2 * COLS, 2 * COLS), 1)
    east_of = (dst < COLS) & (src == dst + 1)
    west_of = (dst >= COLS) & (src == dst - COLS - 1)
    shift[...] = jnp.where(east_of | west_of, 1.0, 0.0).astype(BF)
    col_of = lax.rem(lax.broadcasted_iota(jnp.int32, (COLS, 2 * COLS), 1), COLS)
    row_of = lax.broadcasted_iota(jnp.int32, (COLS, 2 * COLS), 0)
    unit[...] = jnp.where(col_of == row_of, 1.0, 0.0).astype(BF)

    for w in winds:
        w.wait_recv()
    has_lo = (me_lat > 0).astype(F32)
    has_hi = (me_lat < nlat - 1).astype(F32)

    def row_wind(r):
        if r < 0:
            return wind_n[0, 0, ROWS - 1 : ROWS, :], wind_n[0, 1, ROWS - 1 : ROWS, :]
        if r == ROWS:
            return wind_n[1, 0, 0:1, :], wind_n[1, 1, 0:1, :]
        return wind_ref[0, r : r + 1, :], wind_ref[1, r : r + 1, :]

    def four(u, v, r):
        nxt, prv = DIFFUSE - 0.5 * v, DIFFUSE + 0.5 * v
        if r == 0:
            prv = prv * has_lo
        if r == ROWS - 1:
            nxt = nxt * has_hi
        return DIFFUSE - 0.5 * u, DIFFUSE + 0.5 * u, nxt, prv

    for r in range(-1, ROWS + 1):
        u, v = row_wind(r)
        for i, c in enumerate(four(u, v, r)):
            coef[i, r + 1] = jnp.broadcast_to(c, (8, COLS))

    sent_rows(1)
    send_rows(3)

    for e in edges + corners:
        e.wait_recv()
    lane4 = lax.rem(lax.broadcasted_iota(jnp.int32, (MEMBERS, COLS), 1), 4)
    from_west = lane4 >= 2
    halo[0] = jnp.where(from_west, corner[0], corner[1])
    halo[ROWS + 1] = jnp.where(from_west, corner[2], corner[3])
    for r in range(ROWS):
        halo[r + 1] = jnp.where(from_west, edge_w[r], edge_e[r])

    def beside(t):
        return jnp.where(lane4 == 0, t, pltpu.roll(t, 2, 1))

    for r in range(ROWS + 2):
        halo_s[r] = beside(halo[r])
    for r in range(ROWS):
        u, v = [
            jnp.where(
                from_west,
                jnp.broadcast_to(wind_n[2, i, r : r + 1, COLS - 1 : COLS], (MEMBERS, COLS)),
                jnp.broadcast_to(wind_n[3, i, r : r + 1, 0:1], (MEMBERS, COLS)),
            )
            for i in range(2)
        ]
        ce, cw, cn, cs = four(u, v, r)
        own, got = edge[r], halo[r + 1]
        east = pltpu.roll(jnp.where(lane4 == 0, own, got), COLS - 1, 1)
        west = pltpu.roll(jnp.where(lane4 == 3, own, got), 1, 1)
        after = (
            (1.0 - 4.0 * DIFFUSE) * got
            + ce * east
            + cw * west
            + cn * halo[r + 2]
            + cs * halo[r]
        )
        halo1_s[r] = beside(after)

    def shifted(vi, q, count):
        both_s[vi, 0 : count * MEMBERS] = dot(jnp.concatenate(split(q), axis=1), shift[...])

    def step(vi, q, nxt, prv, side, back, first, count):
        shape = (count, MG, 8, COLS)
        both = both_s[vi, 0 : count * MEMBERS]
        lane = lax.broadcasted_iota(jnp.int32, (count * MEMBERS, COLS), 1)
        beyond = pltpu.roll(side.reshape(count * MEMBERS, COLS), back, 1)
        east = jnp.where(lane == COLS - 1, beyond, both[:, :COLS])
        west = jnp.where(lane == 0, beyond, both[:, COLS:])
        c = [coef[i, first : first + count].reshape(count, 1, 8, COLS) for i in range(4)]
        new = (
            (1.0 - 4.0 * DIFFUSE) * q.reshape(shape)
            + c[0] * east.reshape(shape)
            + c[1] * west.reshape(shape)
            + c[2] * nxt.reshape(shape)
            + c[3] * prv.reshape(shape)
        )
        return new.reshape(count * MEMBERS, COLS)

    def block(ref, v, first, count):
        return ref[v, first : first + count].reshape(count * MEMBERS, COLS)

    @pl.loop(0, NVG)
    def _(vg):
        rows(vg, True).wait_recv()
        rows(vg, False).wait_recv()

        @pl.when(vg == 0)
        def _():
            sent_rows(2)
            send_rows(4)

        n1, n2 = ROWS + 2, ROWS
        for vi in range(VS):
            shifted(vi, block(xt, vg * VS + vi, 1, n1), n1)
        for vi in range(VS):
            v = vg * VS + vi
            q1_s[vi] = step(
                vi, block(xt, v, 1, n1), block(xt, v, 2, n1), block(xt, v, 0, n1),
                halo_s[...], (COLS - 1 - 4 * v) & (COLS - 1), 0, n1,
            ).reshape(n1, MEMBERS, COLS)
        for vi in range(VS):
            shifted(vi, block(q1_s, vi, 1, n2), n2)
        for vi in range(VS):
            v = vg * VS + vi
            xf[v] = step(
                vi, block(q1_s, vi, 1, n2), block(q1_s, vi, 2, n2), block(q1_s, vi, 0, n2),
                halo1_s[...], (COLS - 1 - 4 * v) & (COLS - 1), 1, n2,
            ).reshape(n2, MEMBERS, COLS)
        for vi in range(VS):
            v = vg * VS + vi
            both = jnp.concatenate(split(block(xf, v, 0, n2)), axis=1)
            for i in range(SIDE):
                n = min(3, ROWS - 3 * i) * MEMBERS
                xft[pl.ds((v * SIDE + i) * COLS, COLS), 0:n] = dot(
                    unit[...], both[i * 3 * MEMBERS : i * 3 * MEMBERS + n, :], ((1,), (1,))
                )

    to_scalar.wait()
    half, odd = me_lon // 2, lax.rem(me_lon, 2)

    def piece(i, h, b):
        return pltpu.make_async_remote_copy(
            src_ref=part.at[2 * b + h],
            dst_ref=got_a.at[i, odd],
            send_sem=send_a.at[i, h],
            recv_sem=recv_a.at[i, odd],
            device_id=(me_lat, 2 * b + h),
            device_id_type=MESH,
        )

    def arrival(i, p):
        return pltpu.make_async_remote_copy(
            src_ref=part.at[0],
            dst_ref=got_a.at[i, p],
            send_sem=send_a.at[i, 0],
            recv_sem=recv_a.at[i, p],
            device_id=(me_lat, lax.rem(me_lon + 1, nlon)),
            device_id_type=MESH,
        )

    first = []
    for i in list(range(1, NB)) + [0]:
        b = lax.rem(half + i, NB)

        @pl.loop(0, BLOCK // 8)
        def _(g):
            for j in range(8):
                k = g * 8 + j
                at = desc_s[b // PER, lax.rem(b, PER) * BLOCK + k]
                yo[i, pl.ds(k, 1), :] = xft[pl.ds(at, 1), :]

        turned = yo[i].T
        at = jnp.broadcast_to(at8[pl.ds(b, 1), :], (MEMBERS, BLOCK))
        mine = jnp.zeros((MEMBERS, BLOCK), F32)
        for n in range(3):
            mine = jnp.where(at == n, turned[n * MEMBERS : (n + 1) * MEMBERS, :], mine)
        part[2 * b] = mine[0:PIECE]
        part[2 * b + 1] = jnp.concatenate(
            [mine[PIECE:], jnp.zeros((2 * PIECE - MEMBERS, BLOCK), F32)], axis=0
        )
        for h in (0, 1) if i else (1 - odd,):
            c = piece(i, h, b)
            c.start()
            first.append(c)
    lat_f, lon_f = by_block(lat_ref).astype(F32), by_block(lon_ref).astype(F32)
    lat0f, lon0f = (me_lat * ROWS).astype(F32), (me_lon * COLS).astype(F32)
    for i, t in enumerate([lat_f, lon_f, by_block(val_ref), by_block(err_ref)]):
        obs_ref[i] = t
    reach_tables(lat_f, lon_f, lat0f, lon0f, rank_ref, t0_ref)
    total = part[me_lon]
    for i in range(1, NB):
        for p in (0, 1):
            arrival(i, p).wait_recv()
            total = total + got_a[i, p]
    arrival(0, 1 - odd).wait_recv()
    total = total + got_a[0, 1 - odd]
    line[...] = total
    second = [
        remote(line, got_b.at[o - 1], send.at[o - 1], recv_b.at[o - 1], o, 0)
        for o in range(1, nlat)
    ]
    for c in second:
        c.start()
    for i, c in enumerate(second):
        c.wait_recv()
        total = total + got_b[i]
    block_sum[...] = total
    third = [
        remote(block_sum, out.at[me_lon], send.at[nlat + o - 2], recv_c.at[o - 1], 0, o)
        for o in range(1, nlon)
    ]
    for c in third:
        c.start()
    out[me_lon] = total
    pair_tables(lat_f, lon_f, pair_ref)
    for c in third:
        c.wait_recv()

    for c in winds + edges + corners + first + second + third:
        c.wait_send()

    sent_rows(3)
    sent_rows(4)


def forecast(x, wind, lat, lon, var, val, err, nlat, nlon):
    vm = pl.BlockSpec(memory_space=pltpu.VMEM)
    dma = pltpu.SemaphoreType.DMA
    return pl.pallas_call(
        lambda *refs: forecast_kernel(nlat, nlon, *refs),
        out_shape=(
            jax.ShapeDtypeStruct((NVAR, ROWS, MEMBERS, COLS), F32),
            jax.ShapeDtypeStruct((2 * NB, PIECE, BLOCK), F32),
            jax.ShapeDtypeStruct((NB, BLOCK), F32),
            jax.ShapeDtypeStruct((NB, KC, ROWS * COLS), F32),
            jax.ShapeDtypeStruct((NB * (NB - 1) // 2, BLOCK, BLOCK), F32),
            jax.ShapeDtypeStruct((4, NB, BLOCK), F32),
        ),
        in_specs=[pl.BlockSpec(memory_space=pltpu.HBM)] * 7,
        out_specs=(vm,) * 6,
        scratch_shapes=[
            pltpu.VMEM((MEMBERS, NVAR, ROWS, COLS), F32),
            pltpu.VMEM((2, ROWS, COLS), F32),
            pltpu.VMEM((GROUPS, OBS), jnp.int32),
            pltpu.VMEM((GROUPS, OBS), jnp.int32),
            pltpu.VMEM((GROUPS, OBS), jnp.int32),
            pltpu.VMEM((GROUPS, OBS), F32),
            pltpu.VMEM((GROUPS, OBS), F32),
            pltpu.VMEM((GROUPS, OBS), jnp.int32),
            pltpu.SMEM((GROUPS, OBS), jnp.int32),
            pltpu.VMEM((NVAR * SIDE * COLS, COLS), F32),
            pltpu.VMEM((NB, BLOCK, COLS), F32),
            pltpu.VMEM((2 * NB, PIECE, BLOCK), F32),
            pltpu.VMEM((PIECE, BLOCK), F32),
            pltpu.VMEM((PIECE, BLOCK), F32),
            pltpu.VMEM((NB, 2, PIECE, BLOCK), F32),
            pltpu.VMEM((nlat - 1, PIECE, BLOCK), F32),
            pltpu.VMEM((NVAR, ROWS + 4, MEMBERS, COLS), F32),
            pltpu.VMEM((ROWS, MEMBERS, COLS), F32),
            pltpu.VMEM((ROWS, MEMBERS, COLS), F32),
            pltpu.VMEM((ROWS, MEMBERS, COLS), F32),
            pltpu.VMEM((4, MEMBERS, COLS), F32),
            pltpu.VMEM((4, 2, ROWS, COLS), F32),
            pltpu.VMEM((ROWS + 2, MEMBERS, COLS), F32),
            pltpu.VMEM((ROWS + 2, MEMBERS, COLS), F32),
            pltpu.VMEM((ROWS, MEMBERS, COLS), F32),
            pltpu.VMEM((4, ROWS + 2, 8, COLS), F32),
            pltpu.VMEM((2 * COLS, 2 * COLS), BF),
            pltpu.VMEM((COLS, 2 * COLS), BF),
            pltpu.VMEM((VS, ROWS + 2, MEMBERS, COLS), F32),
            pltpu.VMEM((VS, (ROWS + 2) * MEMBERS, 2 * COLS), F32),
            pltpu.VMEM((NVG, VS * 2 * COLS, COLS), BF),
            pltpu.VMEM((NB, BLOCK), jnp.int32),
            dma((NVG, 2)), dma((NVG, 2)), dma((2,)), dma((2,)),
            dma((4,)), dma((4,)), dma((4,)), dma((4,)),
            dma((nlat + nlon - 2,)), dma((NB, 2)), dma((NB, 2)), dma((nlat - 1,)), dma((nlon - 1,)),
            dma((NVG,)), dma((7,)),
        ],
        compiler_params=pltpu.CompilerParams(
            collective_id=0, has_side_effects=True, vmem_limit_bytes=34 << 20
        ),
        name="forecast",
    )(x, wind, lat, lon, var, val, err)


def analysis_kernel(
    x_ref, y_ref, rank_ref, t0_ref, pair_ref, obs_ref,
    out_hbm,
    ob,
    ys, a_all, s_all, a_pk, b_pk, l_pk, a_more, b_more, t_more, xv, rhs, p2, q3, nch,
    l_out,
):
    out_rows = ob.reshape(MEMBERS * NVAR * ROWS, COLS)

    def store(g):
        vs = pl.ds(g * VG, VG)
        return pltpu.make_async_copy(ob.at[:, vs], out_hbm.at[:, vs], l_out.at[g])

    rank = rank_ref[...]
    for b in range(NB):
        top = jnp.max(rank[b : b + 1, :])
        nch[b] = ((top + KC) * (1.0 / KC)).astype(jnp.int32)
        ys[0:PIECE, b * BLOCK : (b + 1) * BLOCK] = y_ref[2 * b]
        ys[PIECE:, b * BLOCK : (b + 1) * BLOCK] = y_ref[2 * b + 1][0 : MEMBERS - PIECE]
    lat, lon, values, variances = [obs_ref[i] for i in range(4)]
    row_id = lax.broadcasted_iota(jnp.int32, (KC, BLOCK), 0).astype(F32)
    lane96 = lax.broadcasted_iota(jnp.int32, (KC, 3 * KC), 1)
    zero8 = jnp.zeros((8, BLOCK), F32)

    def packed(pick, b):
        zero = jnp.zeros_like(pick)
        pick3 = jnp.concatenate(
            [
                jnp.concatenate([pick, zero], axis=1),
                jnp.concatenate([zero, pick], axis=1),
                jnp.concatenate([pick, zero], axis=1),
            ],
            axis=0,
        )
        return dot(pick, a_all[b]).astype(BF), dot(s_all[b], pick3, ((1,), (1,))).astype(BF)

    stacked = None
    for b in range(NB):
        prior = ys[:, b * BLOCK : (b + 1) * BLOCK]
        average = jnp.sum(prior, axis=0, keepdims=True) * (1.0 / MEMBERS)
        anomaly = prior - average
        spread = jnp.sum(anomaly * anomaly, axis=0, keepdims=True) / (MEMBERS - 1)
        errors = variances[b : b + 1, :]
        total = spread + errors
        weights = anomaly * (1.0 / ((MEMBERS - 1) * total))
        shifts = (values[b : b + 1, :] - average) - anomaly * (
            1.0 / (1.0 + jnp.sqrt(errors / total))
        )
        wh = hi(weights)
        a = jnp.concatenate([wh, weights - wh, wh, zero8], axis=0).T.astype(BF)
        sh, sl = split(shifts)
        a_all[b] = a
        s_all[b] = jnp.concatenate([sh, sl], axis=1)
        s3 = jnp.concatenate([sh, sl, sh], axis=1)
        for j in range(b + 1, NB):
            yl = ys[:, j * BLOCK : (j + 1) * BLOCK]
            yh = hi(yl)
            y3 = jnp.concatenate([yh, yh, yl - yh, zero8], axis=0).astype(BF)
            qh, ql = split(dot(a, y3) * pair_ref[pair_at(b, j)])
            ys[:, j * BLOCK : (j + 1) * BLOCK] = yl + dot(
                s3, jnp.concatenate([qh, qh, ql], axis=0)
            )
        pick = (row_id == rank[b : b + 1, :]).astype(BF)
        a_pk[b], b_pk[b] = packed(pick, b)
        if b % 2 == 0:
            sh32 = sh.astype(F32)
            s_rows = jnp.concatenate([sh32, sh32, sl.astype(F32), zero8], axis=0).astype(BF)
            stacked = dot(s_rows, jnp.concatenate([pick] * 3, axis=0), ((1,), (1,))).astype(BF)
        else:
            c = dot(a_pk[b], stacked)
            ch = hi(c)
            c3 = jnp.where((lane96 >= KC) & (lane96 < 2 * KC), c - ch, ch)
            l_pk[b // 2] = jnp.concatenate([c3, b_pk[b - 1].astype(F32)], axis=0).astype(BF)

    lat0f = (lax.axis_index("lat") * ROWS).astype(F32)
    lon0f = (lax.axis_index("lon") * COLS).astype(F32)
    for b in range(NB):

        @pl.loop(1, nch[b])
        def _(c):
            slot = b * (NCH - 1) + c - 1
            pick = (row_id + (c * KC).astype(F32) == rank[b : b + 1, :]).astype(F32)
            a_more[slot], b_more[slot] = packed(pick.astype(BF), b)
            cell_tapers(pick, lat[b : b + 1, :], lon[b : b + 1, :], lat0f, lon0f, t_more, slot)

    zero_cols = jnp.zeros((8, ROWS * COLS), F32)

    def stack_x(i):
        x = xv[i]
        xh = hi(x)
        rhs[i] = jnp.concatenate([xh, xh, x - xh, zero_cols], axis=0).astype(BF)

    def put_q(i, q):
        qh, ql = split(q)
        q3[i] = jnp.concatenate([qh, qh, ql], axis=0)

    def add_chunk(a, s3, t):
        for i in range(VG):
            put_q(i, dot(a, rhs[i]) * t[...])
        for i in range(VG):
            xv[i] += dot(s3, q3[i])

    @pl.loop(0, NVAR // VG)
    def _(g):
        for i in range(VG):
            for r in range(ROWS):
                xv[i, :, r * COLS : (r + 1) * COLS] = x_ref[g * VG + i, r]

        @pl.loop(0, NB // 2)
        def _(pair):
            b = 2 * pair
            few = jnp.maximum(nch[b], nch[b + 1]) <= 1

            @pl.when(few)
            def _():
                a2 = a_pk[pl.ds(b, 2)].reshape(2 * KC, 128)
                for i in range(VG):
                    stack_x(i)
                for i in range(VG):
                    p = dot(a2, rhs[i])
                    p2[i] = p[KC:]
                    put_q(i, p[:KC] * t0_ref[b])
                for i in range(VG):
                    r = dot(l_pk[pair], q3[i])
                    xv[i] += r[KC:]
                    put_q(i, (p2[i] + r[:KC]) * t0_ref[b + 1])
                for i in range(VG):
                    xv[i] += dot(b_pk[b + 1], q3[i])

            @pl.when(jnp.logical_not(few))
            def _():
                @pl.loop(b, b + 2)
                def _(bb):
                    for i in range(VG):
                        stack_x(i)
                    add_chunk(a_pk[bb], b_pk[bb], t0_ref.at[bb])

                    @pl.loop(1, nch[bb])
                    def _(c):
                        slot = bb * (NCH - 1) + c - 1
                        add_chunk(a_more[slot], b_more[slot], t_more.at[slot])

        for i in range(VG):
            for r in range(ROWS):
                out_rows[
                    pl.ds((g * VG + i) * ROWS + r, MEMBERS, stride=NVAR * ROWS), :
                ] = xv[i, :, r * COLS : (r + 1) * COLS]
        store(g).start()

    for g in range(NVAR // VG):
        store(g).wait()


def analysis(x, y, rank, t0, pairs, obs):
    vm = pl.BlockSpec(memory_space=pltpu.VMEM)
    hbm = pl.BlockSpec(memory_space=pltpu.HBM)
    more = NB * (NCH - 1)
    dma = pltpu.SemaphoreType.DMA
    return pl.pallas_call(
        analysis_kernel,
        out_shape=jax.ShapeDtypeStruct((MEMBERS, NVAR, ROWS, COLS), F32),
        in_specs=[vm] * 6,
        out_specs=hbm,
        scratch_shapes=[
            pltpu.VMEM((MEMBERS, NVAR, ROWS, COLS), F32),
            pltpu.VMEM((MEMBERS, NB * BLOCK), F32),
            pltpu.VMEM((NB, BLOCK, 128), BF),
            pltpu.VMEM((NB, MEMBERS, 256), BF),
            pltpu.VMEM((NB, KC, 128), BF),
            pltpu.VMEM((NB, MEMBERS, 3 * KC), BF),
            pltpu.VMEM((NB // 2, KC + MEMBERS, 3 * KC), BF),
            pltpu.VMEM((more, KC, 128), BF),
            pltpu.VMEM((more, MEMBERS, 3 * KC), BF),
            pltpu.VMEM((more, KC, ROWS * COLS), F32),
            pltpu.VMEM((VG, MEMBERS, ROWS * COLS), F32),
            pltpu.VMEM((VG, 128, ROWS * COLS), BF),
            pltpu.VMEM((VG, KC, ROWS * COLS), F32),
            pltpu.VMEM((VG, 3 * KC, ROWS * COLS), BF),
            pltpu.SMEM((NB,), jnp.int32),
            dma((NVAR // VG,)),
        ],
        compiler_params=pltpu.CompilerParams(vmem_limit_bytes=22 << 20),
        name="analysis",
    )(x, y, rank, t0, pairs, obs)


def solution(mesh):
    nlat, nlon = mesh.shape["lat"], mesh.shape["lon"]
    assert nlon == 2 * NB

    def body(prognostic_samples, wind, obs_lat, obs_lon, obs_var, obs_value, obs_error):
        hbm = [
            pltpu.with_memory_space_constraint(a, pltpu.HBM)
            for a in (prognostic_samples, wind, obs_lat, obs_lon, obs_var, obs_value, obs_error)
        ]
        return analysis(*forecast(*hbm, nlat, nlon))

    in_specs = (P(None, None, "lat", "lon"), P(None, "lat", "lon"), P(), P(), P(), P(), P())
    out_specs = P(None, None, "lat", "lon")
    return jax.shard_map(body, mesh=mesh, in_specs=in_specs, out_specs=out_specs, check_vma=False)
```
